128 devices in a mesh: expert: 16 (over x, y_hi, core), dp: 8 (over y_lo, z).
Axes of the slice: x: 4, y: 4 (y_hi: 2, y_lo: 2; y = y_hi * 2 + y_lo), z: 4, core: 2. Of those that a mesh axis runs over, the one named last changes fastest.
Arguments:
- attn_rows: bfloat16 [16384, 7168], P('dp', 'expert'), may hold values from -6 to 6
- out_grad: bfloat16 [16384, 7168], P('dp', 'expert'), may hold values from -6 to 6
- routes: int32 [16384, 8], P(('dp', 'expert')), may hold values from 0 to 255, as said below
- gates: bfloat16 [16384, 8], P(('dp', 'expert')), may hold values from 0.049804688 to 0.5
- w_gate: bfloat16 [16, 7168, 2048], P('expert', None, 'dp'), may hold values from -0.0625 to 0.0625
- w_up: bfloat16 [16, 7168, 2048], P('expert', None, 'dp'), may hold values from -0.0625 to 0.0625
- w_down: bfloat16 [16, 2048, 7168], P('expert', 'dp'), may hold values from -0.125 to 0.125
Outputs:
- grad_input: bfloat16 [16384, 7168], P('dp', 'expert')
- grad_w_gate: bfloat16 [16, 7168, 2048], P('expert', None, 'dp')
- grad_w_up: bfloat16 [16, 7168, 2048], P('expert', None, 'dp')
The draws below stay inside these ranges and needn't reach their ends.
Inputs may be any that keep to these rules, and one draw needn't show every extreme that they name: `routes`: each row names 8 different experts. In the 128 rows of one device (aligned blocks of 128 rows) no window expert (below 16) is named by more than 6 rows; in every device's rows some window expert is named by exactly 6 rows, and one window expert is named by exactly 6 rows of every device.
All inputs are finite; a program needn't handle non-finite values.
Results may differ from the reference program's by a relative error of at most 0.0058.
Values may be sent and summed in bfloat16 or wider, within the bound.
A program may use at most 256 MiB of HBM per device.

```python
import math
import jax
import jax.numpy as jnp
from jax import lax

D = 7168
FF = 2048
TOP = 8
ROUTED = 256
TOK_DEV = 128
EXPERTS = 16
TOKENS = 16384
CAP = 6
EXPERT_ROWS = 768
N_DP = 8


def draw_routes(key, part):
    blocks = TOKENS // TOK_DEV
    keys = jax.random.split(jax.random.fold_in(key, 17), 6)
    expert_ids = jnp.arange(EXPERTS, dtype=jnp.int32)
    level = (2 ** jax.random.randint(keys[0], (EXPERTS,), 0, 4)).astype(jnp.int32)
    top_load = level * CAP // 4 + 1
    counts = jax.random.randint(keys[1], (blocks, EXPERTS), 0, 1 << 20).astype(jnp.int32) % top_load[None, :]
    counts = jnp.minimum(counts, CAP).astype(jnp.int32)
    steady = jax.random.randint(keys[2], (), 0, EXPERTS).astype(jnp.int32)
    moving = jax.random.randint(keys[3], (blocks,), 0, EXPERTS).astype(jnp.int32)
    forced = (expert_ids[None, :] == steady) | (expert_ids[None, :] == moving[:, None])
    counts = jnp.where(forced, CAP, counts).astype(jnp.int32)
    slot_ids = jnp.arange(CAP, dtype=jnp.int32)
    active = (slot_ids[None, None, :] < counts[:, :, None]).reshape(blocks, EXPERTS * CAP).astype(jnp.int32)
    rank = (jnp.cumsum(active, axis=1) - active).astype(jnp.int32)
    orders = jax.vmap(lambda sub: jax.random.permutation(sub, TOK_DEV))(jax.random.split(keys[4], blocks)).astype(jnp.int32)
    row_pos = rank % TOK_DEV
    slot_pos = rank // TOK_DEV
    row_of = jnp.take_along_axis(orders, row_pos, axis=1).astype(jnp.int32)
    row_of = jnp.where(active > 0, row_of, TOK_DEV).astype(jnp.int32)
    named = jnp.broadcast_to(jnp.repeat(expert_ids, CAP)[None, :], (blocks, EXPERTS * CAP))
    block_ids = jnp.broadcast_to(jnp.arange(blocks, dtype=jnp.int32)[:, None], (blocks, EXPERTS * CAP))
    table = jnp.full((blocks, TOK_DEV, TOP), -1, jnp.int32)
    table = table.at[block_ids, row_of, slot_pos].set(named, mode='drop')
    table = table.reshape(TOKENS, TOP)
    outside = ROUTED - EXPERTS
    scores = jax.random.randint(keys[5], (TOKENS, outside), 0, 1 << 20).astype(jnp.int32) * outside + jnp.arange(outside, dtype=jnp.int32)[None, :]
    unused, chosen = lax.top_k(scores, TOP)
    return jnp.where(table >= 0, table, EXPERTS + chosen.astype(jnp.int32)).astype(jnp.int32)


def steps_of(key, extent, shards, smallest, top_value):
    level = 1.0
    for dim, blocks in shards:
        steps = jax.random.uniform(jax.random.fold_in(jax.random.fold_in(key, 6), dim), (blocks,), jnp.float32, smallest / len(shards), top_value / len(shards))
        level = level * jnp.repeat(jnp.exp(steps), extent[dim] // blocks).reshape((-1,) + (1,) * (len(extent) - 1 - dim))
    return level


def gaussian(stream_key, extent, spread, reach, shards=(), kind=jnp.bfloat16):
    entries = spread * jax.random.normal(stream_key, extent, jnp.float32)
    if shards:
        entries = entries * steps_of(stream_key, extent, shards, -0.22, 0.18)
    return jnp.clip(entries, -reach, reach).astype(kind)


def setup_inputs(seed: int = 0) -> dict:
    key_list = jax.random.split(jax.random.key(seed), 8)
    return {
        "attn_rows": gaussian(key_list[0], (TOKENS, D), 1.0, 6.0, ((0, 8), (1, 16))),
        "out_grad": gaussian(key_list[1], (TOKENS, D), 1.0, 6.0, ((0, 8), (1, 16))),
        "routes": draw_routes(jax.random.fold_in(key_list[7], 71), 0),
        "gates": jnp.clip(jnp.exp(math.log(0.5) - 2.306499 * jax.random.uniform(key_list[3], (TOKENS, TOP), jnp.float32) ** steps_of(key_list[3], (TOKENS, TOP), ((0, 128),), -0.2, 0.2)), 0.049804688, 0.5).astype(jnp.bfloat16),
        "w_gate": gaussian(key_list[4], (EXPERTS, D, FF), D ** -0.5, 0.0625, ((0, 16), (2, 8))),
        "w_up": gaussian(key_list[5], (EXPERTS, D, FF), D ** -0.5, 0.0625, ((0, 16), (2, 8))),
        "w_down": gaussian(key_list[6], (EXPERTS, FF, D), FF ** -0.5, 0.125, ((0, 16), (1, 8))),
    }


def reference(attn_rows, out_grad, routes, gates, w_gate, w_up, w_down):
    expert_ids = jnp.arange(EXPERTS, dtype=jnp.int32)
    gate_full = gates.astype(jnp.float32)
    slices = FF // N_DP

    def one_expert(carry, items):
        expert_id, gate_mat, up_mat, down_mat = items
        routed = jnp.any(routes == expert_id, axis=1)
        picked = jnp.argsort(jnp.where(routed, 0, 1).astype(jnp.int32), stable=True)[:EXPERT_ROWS].astype(jnp.int32)
        coef_all = jnp.sum(jnp.where(routes == expert_id, gate_full, jnp.zeros_like(gate_full)), axis=1)
        coef = coef_all[picked]
        token_rows = attn_rows[picked]
        grad_rows = out_grad[picked]
        gate_pre = jnp.dot(token_rows, gate_mat, preferred_element_type=jnp.float32)
        up_proj = jnp.dot(token_rows, up_mat, preferred_element_type=jnp.float32)
        sigma_gate = jax.nn.sigmoid(gate_pre)
        activated = gate_pre * sigma_gate
        back_proj = jnp.dot(grad_rows, down_mat.T, preferred_element_type=jnp.float32)
        grad_hidden = coef[:, None] * back_proj
        grad_gate = (grad_hidden * up_proj * sigma_gate * (1.0 + gate_pre * (1.0 - sigma_gate))).astype(jnp.bfloat16)
        grad_up = (grad_hidden * activated).astype(jnp.bfloat16)
        g_gate = jnp.dot(token_rows.T, grad_gate, preferred_element_type=jnp.float32).astype(jnp.bfloat16)
        g_up = jnp.dot(token_rows.T, grad_up, preferred_element_type=jnp.float32).astype(jnp.bfloat16)
        left_gate = grad_gate.astype(jnp.float32).reshape(EXPERT_ROWS, N_DP, slices)
        left_up = grad_up.astype(jnp.float32).reshape(EXPERT_ROWS, N_DP, slices)
        right_gate = gate_mat.astype(jnp.float32).reshape(D, N_DP, slices)
        right_up = up_mat.astype(jnp.float32).reshape(D, N_DP, slices)
        pieces = jnp.einsum("tsf,dsf->tsd", left_gate, right_gate) + jnp.einsum("tsf,dsf->tsd", left_up, right_up)
        pieces = lax.optimization_barrier(pieces.astype(jnp.bfloat16)).astype(jnp.float32)
        contribution = jnp.sum(pieces, axis=1)
        carry = carry.at[picked].add(contribution)
        return carry, (g_gate, g_up)

    total, grads = lax.scan(one_expert, jnp.zeros((TOKENS, D), jnp.float32), (expert_ids, w_gate, w_up, w_down))
    return (total.astype(jnp.bfloat16), grads[0], grads[1])
```

```python
import jax
import jax.numpy as jnp
from jax import lax
from jax.sharding import PartitionSpec as P

BF = jnp.bfloat16
F32 = jnp.float32


def slot_tables(routes, gates, experts, capacity):
    matches = (routes[..., None] == jnp.arange(experts, dtype=routes.dtype)).astype(F32)
    per_token = jnp.sum(matches, axis=2)
    coef = jnp.sum(matches * gates[..., None].astype(F32), axis=2)
    tokens = routes.shape[1]
    earlier = (jnp.arange(tokens)[:, None] < jnp.arange(tokens)[None, :]).astype(BF)
    before = jnp.einsum("bse,st->bte", per_token.astype(BF), earlier, preferred_element_type=F32)
    slot = jnp.arange(capacity, dtype=F32)
    hit = (before[..., None] == slot) & (per_token[..., None] > 0)
    hit = jnp.transpose(hit, (0, 2, 3, 1))
    scaled = jnp.where(hit, jnp.transpose(coef, (0, 2, 1))[:, :, None, :], 0.0)
    return hit.astype(BF), scaled.astype(BF)


def per_device(attn_rows, out_grad, routes, gates, w_gate, w_up, w_down):
    experts = lax.axis_size("expert")
    groups = lax.axis_size("dp")
    own = routes.shape[0]
    capacity = 3 * own // 64
    width = attn_rows.shape[1]
    packed = jnp.concatenate([routes.astype(BF), gates], axis=1)
    packed = lax.all_gather(packed, "expert", axis=0, tiled=False)
    top = routes.shape[1]
    place, scaled = slot_tables(packed[..., :top], packed[..., top:], experts, capacity)

    def dispatch(table, rows):
        rows = rows.reshape(experts, own, width)
        sent = jnp.einsum("bect,btd->ebcd", table, rows, preferred_element_type=F32).astype(BF)
        sent = sent.reshape(experts, experts * capacity, width)
        got = lax.all_to_all(sent, "expert", split_axis=0, concat_axis=0, tiled=True)
        got = jnp.transpose(got, (1, 0, 2)).reshape(experts * capacity, experts * width)
        return lax.all_gather(got, "dp", axis=0, tiled=True)

    x = dispatch(place, attn_rows)
    dy = dispatch(scaled, out_grad)

    gate_mat, up_mat, down_mat = w_gate[0], w_up[0], w_down[0]
    rows_dims = (((1,), (1,)), ((), ()))
    first_dims = (((0,), (0,)), ((), ()))
    g = jnp.dot(x, gate_mat, preferred_element_type=F32)
    u = jnp.dot(x, up_mat, preferred_element_type=F32)
    gh = lax.dot_general(dy, down_mat, rows_dims, preferred_element_type=F32)
    s = jax.nn.sigmoid(g)
    dg = (gh * u * s * (1.0 + g * (1.0 - s))).astype(BF)
    du = (gh * (g * s)).astype(BF)
    part = lax.dot_general(dg, gate_mat, rows_dims, preferred_element_type=F32)
    part = (part + lax.dot_general(du, up_mat, rows_dims, preferred_element_type=F32)).astype(BF)
    back = lax.psum_scatter(part, "dp", scatter_dimension=0, tiled=True)
    g_gate = lax.dot_general(x, dg, first_dims, preferred_element_type=F32).astype(BF)
    g_up = lax.dot_general(x, du, first_dims, preferred_element_type=F32).astype(BF)
    back = back.reshape(experts * capacity, experts, width)
    back = jnp.transpose(back, (1, 0, 2))
    back = lax.all_to_all(back, "expert", split_axis=0, concat_axis=0, tiled=True)
    back = back.reshape(experts, experts, capacity, width)
    grad_input = jnp.einsum("bect,ebcd->btd", place, back, preferred_element_type=F32).astype(BF)
    return grad_input.reshape(experts * own, width), g_gate[None], g_up[None]


def solution(mesh):
    return jax.shard_map(
        per_device,
        mesh=mesh,
        in_specs=(
            P("dp", "expert"),
            P("dp", "expert"),
            P(("dp", "expert"), None),
            P(("dp", "expert"), None),
            P("expert", None, "dp"),
            P("expert", None, "dp"),
            P("expert", "dp", None),
        ),
        out_specs=(P("dp", "expert"), P("expert", None, "dp"), P("expert", None, "dp")),
        check_vma=False,
    )
```

```python
import functools

import jax
import jax.numpy as jnp
from jax import lax
from jax.experimental import pallas as pl
from jax.experimental.pallas import tpu as pltpu
from jax.sharding import PartitionSpec as P

BF = jnp.bfloat16
F32 = jnp.float32
MESH = pl.DeviceIdType.MESH
NT = (((1,), (1,)), ((), ()))
EXP, DP, NZ, CHIPS = 16, 8, 4, 8
TOK, TOP, CAP = 128, 8, 6
LOCAL = EXP * TOK
WIDE, D, HID = 896, 7168, 256
PIECE = 48
SHARD = 96
STEP = 1024


def gather_kernel(
    xt_ref, dt_ref, pk_ref, wg_ref, wu_ref, wd_ref,
    x_out, dg_ref, du_ref,
    raw, tabs, code, coef, onehot, pay, xall, dall, wg, wu, wd, acc,
    ssem, rsem, lsem,
):
    ex = lax.axis_index("expert")
    dp = lax.axis_index("dp")
    core = ex % 2
    chip = ex // 2
    row, z = dp // NZ, dp % NZ

    def at(dy, dz):
        return (row + dy) % 2 * NZ + (z + dz) % NZ

    up, down, side = at(0, 1), at(0, NZ - 1), at(1, 0)
    bufs = (xall, dall)

    barrier = pltpu.get_barrier_semaphore()
    for r in range(1, EXP):
        pl.semaphore_signal(barrier, inc=1, device_id=((ex + r) % EXP, dp), device_id_type=MESH)
    for peer in (up, down, side):
        pl.semaphore_signal(barrier, inc=1, device_id=(ex, peer), device_id_type=MESH)

    local = []

    def copy_in(src, dst):
        c = pltpu.make_async_copy(src, dst, lsem.at[len(local)])
        c.start()
        local.append(c)
        return c

    mine = pl.ds(pl.multiple_of(core * (WIDE // 2), WIDE // 2), WIDE // 2)
    lanes = pl.ds(pl.multiple_of(ex * TOK, TOK), TOK)
    in_tab = copy_in(pk_ref, tabs.at[:, lanes])
    in_raw = [copy_in(ref, raw.at[t, mine, :]) for t, ref in enumerate((xt_ref, dt_ref))]
    in_w = [copy_in(wg_ref, wg), copy_in(wu_ref, wu), copy_in(wd_ref, wd)]

    pl.semaphore_wait(barrier, EXP - 1 + 3)

    sent = []
    slots = [0]

    def slot():
        slots[0] += 1
        return slots[0] - 1

    def send(k, src, dst, device):
        c = pltpu.make_async_remote_copy(
            src_ref=src, dst_ref=dst, send_sem=ssem.at[k], recv_sem=rsem.at[k],
            device_id=device, device_id_type=MESH,
        )
        c.start()
        sent.append(c)

    def arrive(k, dst):
        pltpu.make_async_remote_copy(
            src_ref=dst, dst_ref=dst, send_sem=ssem.at[k], recv_sem=rsem.at[k],
            device_id=(ex, side), device_id_type=MESH,
        ).wait_recv()

    other = pl.ds(pl.multiple_of((1 - core) * (WIDE // 2), WIDE // 2), WIDE // 2)
    tab_slot = [slot() for _ in range(EXP)]
    for r in range(1, EXP):
        send(tab_slot[r], pk_ref, tabs.at[:, lanes], ((ex + r) % EXP, dp))
    raw_slot = [slot(), slot()]
    sibling = (chip * 2 + 1 - core, dp)
    for t, ref in enumerate((xt_ref, dt_ref)):
        send(raw_slot[t], ref, raw.at[t, mine, :], sibling)

    in_tab.wait()
    for r in range(1, EXP):
        src = (ex + EXP - r) % EXP
        arrive(tab_slot[r], tabs.at[:, pl.ds(pl.multiple_of(src * TOK, TOK), TOK)])

    table = tabs[...].astype(F32)
    route, gate = table[:TOP], table[TOP:]
    ids = (lax.broadcasted_iota(jnp.int32, (CHIPS, LOCAL), 0) * 2 + core).astype(F32)
    hit = jnp.zeros((CHIPS, LOCAL), F32)
    weight = jnp.zeros((CHIPS, LOCAL), F32)
    for k in range(TOP):
        same = route[k : k + 1] == ids
        hit = hit + jnp.where(same, 1.0, 0.0)
        weight = weight + jnp.where(same, gate[k : k + 1], 0.0)
    coef[...] = weight
    stacked = jnp.concatenate([hit[:, b * TOK : (b + 1) * TOK] for b in range(EXP)], axis=0)
    tri = (
        lax.broadcasted_iota(jnp.int32, (TOK, TOK), 0) < lax.broadcasted_iota(jnp.int32, (TOK, TOK), 1)
    ).astype(F32).astype(BF)
    before = jnp.dot(stacked.astype(BF), tri, preferred_element_type=F32)
    for b in range(EXP):
        part = slice(b * CHIPS, (b + 1) * CHIPS)
        code[:, b * TOK : (b + 1) * TOK] = jnp.where(
            stacked[part] > 0.0, before[part] + float(CAP * (b % CHIPS)), -1.0
        )

    slot_row = lax.broadcasted_iota(jnp.int32, (PIECE, LOCAL // 2), 0).astype(F32)
    own_rows = [pl.ds(pl.multiple_of(dp * SHARD + h * PIECE, PIECE), PIECE) for h in range(2)]
    chip_cols = pl.ds(pl.multiple_of(chip * WIDE, WIDE), WIDE)
    a2a_slot = [[[slot() for _ in range(CHIPS)] for _ in range(2)] for _ in range(2)]
    a2a_self = [[None, None], [None, None]]

    def dispatch(t, h):
        half = slice(h * (LOCAL // 2), (h + 1) * (LOCAL // 2))
        for i in range(CHIPS):
            equal = code[i : i + 1, half] == slot_row
            value = 1.0 if t == 0 else coef[i : i + 1, half]
            onehot[i * PIECE : (i + 1) * PIECE] = jnp.where(equal, value, 0.0).astype(BF)
        for n in range(0, WIDE, 128):
            got = lax.dot_general(onehot[...], raw[t, n : n + 128, half], NT, preferred_element_type=F32)
            pay[t, h, :, :, n : n + 128] = got.astype(BF).reshape(CHIPS, PIECE, 128)
        where = bufs[t].at[own_rows[h], chip_cols]
        for r in range(1, CHIPS):
            to = (chip + r) % CHIPS
            send(a2a_slot[t][h][r], pay.at[t, h, to], where, (to * 2 + core, dp))
        a2a_self[t][h] = copy_in(pay.at[t, h, chip], where)

    def complete(t, h):
        a2a_self[t][h].wait()
        for r in range(1, CHIPS):
            src = (chip + CHIPS - r) % CHIPS
            arrive(a2a_slot[t][h][r], bufs[t].at[own_rows[h], pl.ds(pl.multiple_of(src * WIDE, WIDE), WIDE)])

    def piece(t, h, s):
        return bufs[t].at[pl.ds(pl.multiple_of(s * SHARD + h * PIECE, PIECE), PIECE), :]

    def slots_for():
        return {(t, h): slot() for t in range(2) for h in range(2)}

    to_up, to_down, to_side = slots_for(), slots_for(), slots_for()

    def spread(t, h):
        for k, peer in ((to_side, side), (to_up, up), (to_down, down)):
            send(k[t, h], piece(t, h, dp), piece(t, h, dp), (ex, peer))

    in_raw[0].wait()
    arrive(raw_slot[0], raw.at[0, other, :])
    dispatch(0, 0)
    dispatch(0, 1)
    complete(0, 0)
    spread(0, 0)
    in_raw[1].wait()
    arrive(raw_slot[1], raw.at[1, other, :])
    dispatch(1, 0)
    complete(0, 1)
    spread(0, 1)
    dispatch(1, 1)
    complete(1, 0)
    spread(1, 0)
    complete(1, 1)
    spread(1, 1)
    for c in in_w:
        c.wait()

    def rows_of(s):
        return pl.ds(pl.multiple_of(s * SHARD, SHARD), SHARD)

    def hidden(s):
        rows = rows_of(s)
        acc[...] = jnp.zeros_like(acc)

        def contract(k, _):
            cols = pl.ds(pl.multiple_of(k * STEP, STEP), STEP)
            xs = xall[rows, cols]
            acc[0] += jnp.dot(xs, wg[cols, :], preferred_element_type=F32)
            acc[1] += jnp.dot(xs, wu[cols, :], preferred_element_type=F32)
            acc[2] += lax.dot_general(dall[rows, cols], wd[:, cols], NT, preferred_element_type=F32)
            return 0

        lax.fori_loop(0, D // STEP, contract, 0)
        g, u, q = acc[0], acc[1], acc[2]
        sig = jax.nn.sigmoid(g)
        dg_ref[rows, :] = (q * u * sig * (1.0 + g * (1.0 - sig))).astype(BF)
        du_ref[rows, :] = (q * (g * sig)).astype(BF)

    def pair(of):
        def body(i, _):
            hidden(of(i))
            return 0

        lax.fori_loop(0, 2, body, 0)

    def keep(s):
        copy_in(xall.at[rows_of(s), :], x_out.at[rows_of(s), :])

    via_up, via_down = slots_for(), slots_for()
    for t, h in ((0, 0), (0, 1), (1, 0)):
        arrive(to_side[t, h], piece(t, h, side))
        send(via_up[t, h], piece(t, h, side), piece(t, h, side), (ex, up))
        send(via_down[t, h], piece(t, h, side), piece(t, h, side), (ex, down))
    halves = (slice(0, D // 2), slice(D // 2, D))

    def half_piece(s, j):
        return dall.at[pl.ds(pl.multiple_of(s * SHARD + PIECE, PIECE), PIECE), halves[j]]

    far_up, far_down = slot(), slot()
    arrive(to_up[1, 1], piece(1, 1, down))
    send(far_up, half_piece(down, 0), half_piece(down, 0), (ex, up))
    over = [slot(), slot(), slot(), slot()]
    send(over[0], piece(1, 1, down), piece(1, 1, down), (ex, side))
    arrive(to_down[1, 1], piece(1, 1, up))
    send(far_down, half_piece(up, 1), half_piece(up, 1), (ex, down))
    send(over[1], piece(1, 1, up), piece(1, 1, up), (ex, side))
    fwd = {name: slot() for name in ("x0", "x1", "px0", "px1", "d0", "pd0")}
    for t, h in ((0, 0), (0, 1), (1, 0)):
        arrive(to_up[t, h], piece(t, h, down))
        arrive(to_down[t, h], piece(t, h, up))
    send(fwd["x0"], piece(0, 0, down), piece(0, 0, down), (ex, up))
    send(fwd["x1"], piece(0, 1, up), piece(0, 1, up), (ex, down))
    arrive(to_side[1, 1], piece(1, 1, side))
    pair(lambda i: at(i, 0))
    keep(dp)
    keep(side)
    pside_down, pside_up = at(1, NZ - 1), at(1, 1)
    far, pfar = at(0, 2), at(1, 2)
    arrive(via_up[0, 0], piece(0, 0, pside_down))
    send(fwd["px0"], piece(0, 0, pside_down), piece(0, 0, pside_down), (ex, up))
    arrive(via_down[0, 1], piece(0, 1, pside_up))
    send(fwd["px1"], piece(0, 1, pside_up), piece(0, 1, pside_up), (ex, down))
    send(fwd["d0"], piece(1, 0, down), piece(1, 0, down), (ex, up))
    arrive(via_down[1, 0], piece(1, 0, pside_up))
    send(fwd["pd0"], piece(1, 0, pside_up), piece(1, 0, pside_up), (ex, down))
    pair(lambda i: at(0, NZ - 1 - 2 * i))
    keep(down)
    keep(up)
    arrive(far_up, half_piece(far, 0))
    send(over[2], half_piece(far, 0), half_piece(far, 0), (ex, side))
    arrive(far_down, half_piece(far, 1))
    send(over[3], half_piece(far, 1), half_piece(far, 1), (ex, side))
    arrive(via_up[0, 1], piece(0, 1, pside_down))
    arrive(via_up[1, 0], piece(1, 0, pside_down))
    arrive(via_down[0, 0], piece(0, 0, pside_up))
    arrive(over[0], piece(1, 1, pside_down))
    arrive(over[1], piece(1, 1, pside_up))
    pair(lambda i: at(1, NZ - 1 - 2 * i))
    keep(pside_down)
    keep(pside_up)
    arrive(fwd["x0"], piece(0, 0, far))
    arrive(fwd["x1"], piece(0, 1, far))
    arrive(fwd["d0"], piece(1, 0, far))
    arrive(fwd["px0"], piece(0, 0, pfar))
    arrive(fwd["px1"], piece(0, 1, pfar))
    arrive(fwd["pd0"], piece(1, 0, pfar))
    arrive(over[2], half_piece(pfar, 0))
    arrive(over[3], half_piece(pfar, 1))
    pair(lambda i: at(i, 2))
    keep(far)
    keep(pfar)
    for c in sent:
        c.wait_send()
    for c in local[-DP:]:
        c.wait()


def gather_rows(xt, dt, packed, wg, wu, wd):
    hbm = pl.BlockSpec(memory_space=pl.ANY)
    vmem = pl.BlockSpec(memory_space=pltpu.VMEM)
    rows = DP * SHARD
    return pl.pallas_call(
        gather_kernel,
        out_shape=(
            jax.ShapeDtypeStruct((rows, D), BF),
            jax.ShapeDtypeStruct((rows, HID), BF),
            jax.ShapeDtypeStruct((rows, HID), BF),
        ),
        in_specs=[hbm] * 6,
        out_specs=(hbm, vmem, vmem),
        scratch_shapes=[
            pltpu.VMEM((2, WIDE, LOCAL), BF),
            pltpu.VMEM((2 * TOP, LOCAL), BF),
            pltpu.VMEM((CHIPS, LOCAL), F32),
            pltpu.VMEM((CHIPS, LOCAL), F32),
            pltpu.VMEM((CHIPS * PIECE, LOCAL // 2), BF),
            pltpu.VMEM((2, 2, CHIPS, PIECE, WIDE), BF),
            pltpu.VMEM((rows, D), BF),
            pltpu.VMEM((rows, D), BF),
            pltpu.VMEM((D, HID), BF),
            pltpu.VMEM((D, HID), BF),
            pltpu.VMEM((HID, D), BF),
            pltpu.VMEM((3, SHARD, HID), F32),
            pltpu.SemaphoreType.DMA((96,)),
            pltpu.SemaphoreType.DMA((96,)),
            pltpu.SemaphoreType.DMA((24,)),
        ],
        compiler_params=pltpu.CompilerParams(
            collective_id=0, has_side_effects=True, vmem_limit_bytes=60 * 1024 * 1024
        ),
        name="gather_rows",
    )(xt, dt, packed, wg, wu, wd)


def placement(routes, experts, capacity):
    hit = jnp.sum((routes[..., None] == jnp.arange(experts, dtype=routes.dtype)).astype(F32), axis=2)
    tokens = routes.shape[1]
    earlier = (jnp.arange(tokens)[:, None] < jnp.arange(tokens)[None, :]).astype(BF)
    before = jnp.einsum("bse,st->bte", hit.astype(BF), earlier, preferred_element_type=F32)
    at_slot = (before[..., None] == jnp.arange(capacity, dtype=F32)) & (hit[..., None] > 0)
    return jnp.transpose(at_slot, (0, 2, 3, 1)).astype(BF)


def per_device(attn_rows, out_grad, routes, gates, w_gate, w_up, w_down):
    experts = lax.axis_size("expert")
    own = routes.shape[0]
    capacity = 3 * own // 64
    width = attn_rows.shape[1]
    packed = jnp.concatenate([routes.T.astype(BF), gates.T], axis=0)
    gate_mat, up_mat, down_mat = w_gate[0], w_up[0], w_down[0]
    x, dg, du = gather_rows(attn_rows.T, out_grad.T, packed, gate_mat, up_mat, down_mat)

    rows_dims = (((1,), (1,)), ((), ()))
    first_dims = (((0,), (0,)), ((), ()))
    part = lax.dot_general(dg, gate_mat, rows_dims, preferred_element_type=F32)
    part = (part + lax.dot_general(du, up_mat, rows_dims, preferred_element_type=F32)).astype(BF)
    back = lax.psum_scatter(part, "dp", scatter_dimension=0, tiled=True)
    g_gate = lax.dot_general(x, dg, first_dims, preferred_element_type=F32).astype(BF)
    g_up = lax.dot_general(x, du, first_dims, preferred_element_type=F32).astype(BF)
    back = back.reshape(experts * capacity, experts, width)
    back = jnp.transpose(back, (1, 0, 2))
    back = lax.all_to_all(back, "expert", split_axis=0, concat_axis=0, tiled=True)
    back = back.reshape(experts, experts, capacity, width)
    place = placement(lax.all_gather(routes.astype(BF), "expert"), experts, capacity)
    grad_input = jnp.einsum("bect,ebcd->btd", place, back, preferred_element_type=F32).astype(BF)
    return grad_input.reshape(experts * own, width), g_gate[None], g_up[None]


def solution(mesh):
    return jax.shard_map(
        per_device,
        mesh=mesh,
        in_specs=(
            P("dp", "expert"),
            P("dp", "expert"),
            P(("dp", "expert"), None),
            P(("dp", "expert"), None),
            P("expert", None, "dp"),
            P("expert", None, "dp"),
            P("expert", "dp", None),
        ),
        out_specs=(P("dp", "expert"), P("expert", None, "dp"), P("expert", None, "dp")),
        check_vma=False,
    )
```

```python
import jax
import jax.numpy as jnp
from jax import lax
from jax.experimental import pallas as pl
from jax.experimental.pallas import tpu as pltpu
from jax.sharding import PartitionSpec as P

BF = jnp.bfloat16
F32 = jnp.float32
MESH = pl.DeviceIdType.MESH
NT = (((1,), (1,)), ((), ()))
EXP, DP, NZ, CHIPS = 16, 8, 4, 8
TOK, TOP, CAP = 128, 8, 6
LOCAL = EXP * TOK
WIDE, D, HID = 896, 7168, 256
PIECE = 48
SHARD = 96
STEP = 1024


def gather_kernel(
    xt_ref, dt_ref, pk_ref, wg_ref, wu_ref, wd_ref,
    x_out, dg_ref, du_ref, tab_out,
    raw, tabs, code, coef, onehot, pay, xall, dall, wg, wu, wd, acc,
    ssem, rsem, lsem,
):
    ex = lax.axis_index("expert")
    dp = lax.axis_index("dp")
    core = ex % 2
    chip = ex // 2
    row, z = dp // NZ, dp % NZ

    def at(dy, dz):
        return (row + dy) % 2 * NZ + (z + dz) % NZ

    up, down, side = at(0, 1), at(0, NZ - 1), at(1, 0)
    bufs = (xall, dall)

    barrier = pltpu.get_barrier_semaphore()
    for r in range(1, EXP):
        pl.semaphore_signal(barrier, inc=1, device_id=((ex + r) % EXP, dp), device_id_type=MESH)
    for peer in (up, down, side):
        pl.semaphore_signal(barrier, inc=1, device_id=(ex, peer), device_id_type=MESH)

    local = []

    def copy_in(src, dst):
        c = pltpu.make_async_copy(src, dst, lsem.at[len(local)])
        c.start()
        local.append(c)
        return c

    mine = pl.ds(pl.multiple_of(core * (WIDE // 2), WIDE // 2), WIDE // 2)
    lanes = pl.ds(pl.multiple_of(ex * TOK, TOK), TOK)
    in_tab = copy_in(pk_ref, tabs.at[:, lanes])
    in_raw = [copy_in(ref, raw.at[t, mine, :]) for t, ref in enumerate((xt_ref, dt_ref))]
    in_w = [copy_in(wg_ref, wg), copy_in(wu_ref, wu), copy_in(wd_ref, wd)]

    pl.semaphore_wait(barrier, EXP - 1 + 3)

    sent = []
    slots = [0]

    def slot():
        slots[0] += 1
        return slots[0] - 1

    def send(k, src, dst, device):
        c = pltpu.make_async_remote_copy(
            src_ref=src, dst_ref=dst, send_sem=ssem.at[k], recv_sem=rsem.at[k],
            device_id=device, device_id_type=MESH,
        )
        c.start()
        sent.append(c)

    def arrive(k, dst):
        pltpu.make_async_remote_copy(
            src_ref=dst, dst_ref=dst, send_sem=ssem.at[k], recv_sem=rsem.at[k],
            device_id=(ex, side), device_id_type=MESH,
        ).wait_recv()

    other = pl.ds(pl.multiple_of((1 - core) * (WIDE // 2), WIDE // 2), WIDE // 2)
    tab_slot = [slot() for _ in range(EXP)]
    for r in range(1, EXP):
        send(tab_slot[r], pk_ref, tabs.at[:, lanes], ((ex + r) % EXP, dp))
    raw_slot = [slot(), slot()]
    sibling = (chip * 2 + 1 - core, dp)
    for t, ref in enumerate((xt_ref, dt_ref)):
        send(raw_slot[t], ref, raw.at[t, mine, :], sibling)

    in_tab.wait()
    for r in range(1, EXP):
        src = (ex + EXP - r) % EXP
        arrive(tab_slot[r], tabs.at[:, pl.ds(pl.multiple_of(src * TOK, TOK), TOK)])

    copy_in(tabs, tab_out)
    tab_copy = local[-1]
    table = tabs[...].astype(F32)
    route, gate = table[:TOP], table[TOP:]
    ids = (lax.broadcasted_iota(jnp.int32, (CHIPS, LOCAL), 0) * 2 + core).astype(F32)
    hit = jnp.zeros((CHIPS, LOCAL), F32)
    weight = jnp.zeros((CHIPS, LOCAL), F32)
    for k in range(TOP):
        same = route[k : k + 1] == ids
        hit = hit + jnp.where(same, 1.0, 0.0)
        weight = weight + jnp.where(same, gate[k : k + 1], 0.0)
    coef[...] = weight
    stacked = jnp.concatenate([hit[:, b * TOK : (b + 1) * TOK] for b in range(EXP)], axis=0)
    tri = (
        lax.broadcasted_iota(jnp.int32, (TOK, TOK), 0) < lax.broadcasted_iota(jnp.int32, (TOK, TOK), 1)
    ).astype(F32).astype(BF)
    before = jnp.dot(stacked.astype(BF), tri, preferred_element_type=F32)
    for b in range(EXP):
        part = slice(b * CHIPS, (b + 1) * CHIPS)
        code[:, b * TOK : (b + 1) * TOK] = jnp.where(
            stacked[part] > 0.0, before[part] + float(CAP * (b % CHIPS)), -1.0
        )

    slot_row = lax.broadcasted_iota(jnp.int32, (PIECE, LOCAL // 2), 0).astype(F32)
    own_rows = [pl.ds(pl.multiple_of(dp * SHARD + h * PIECE, PIECE), PIECE) for h in range(2)]
    chip_cols = pl.ds(pl.multiple_of(chip * WIDE, WIDE), WIDE)
    a2a_slot = [[[slot() for _ in range(CHIPS)] for _ in range(2)] for _ in range(2)]
    a2a_self = [[None, None], [None, None]]

    def dispatch(t, h):
        half = slice(h * (LOCAL // 2), (h + 1) * (LOCAL // 2))
        for i in range(CHIPS):
            equal = code[i : i + 1, half] == slot_row
            value = 1.0 if t == 0 else coef[i : i + 1, half]
            onehot[i * PIECE : (i + 1) * PIECE] = jnp.where(equal, value, 0.0).astype(BF)
        for n in range(0, WIDE, 128):
            got = lax.dot_general(onehot[...], raw[t, n : n + 128, half], NT, preferred_element_type=F32)
            pay[t, h, :, :, n : n + 128] = got.astype(BF).reshape(CHIPS, PIECE, 128)
        where = bufs[t].at[own_rows[h], chip_cols]
        for r in range(1, CHIPS):
            to = (chip + r) % CHIPS
            send(a2a_slot[t][h][r], pay.at[t, h, to], where, (to * 2 + core, dp))
        a2a_self[t][h] = copy_in(pay.at[t, h, chip], where)

    def complete(t, h):
        a2a_self[t][h].wait()
        for r in range(1, CHIPS):
            src = (chip + CHIPS - r) % CHIPS
            arrive(a2a_slot[t][h][r], bufs[t].at[own_rows[h], pl.ds(pl.multiple_of(src * WIDE, WIDE), WIDE)])

    def piece(t, h, s):
        return bufs[t].at[pl.ds(pl.multiple_of(s * SHARD + h * PIECE, PIECE), PIECE), :]

    def slots_for():
        return {(t, h): slot() for t in range(2) for h in range(2)}

    to_up, to_down, to_side = slots_for(), slots_for(), slots_for()

    def spread(t, h):
        for k, peer in ((to_side, side), (to_up, up), (to_down, down)):
            send(k[t, h], piece(t, h, dp), piece(t, h, dp), (ex, peer))

    in_raw[0].wait()
    arrive(raw_slot[0], raw.at[0, other, :])
    dispatch(0, 0)
    dispatch(0, 1)
    complete(0, 0)
    spread(0, 0)
    in_raw[1].wait()
    arrive(raw_slot[1], raw.at[1, other, :])
    dispatch(1, 0)
    complete(0, 1)
    spread(0, 1)
    dispatch(1, 1)
    complete(1, 0)
    spread(1, 0)
    complete(1, 1)
    spread(1, 1)
    for c in in_w:
        c.wait()

    def rows_of(s):
        return pl.ds(pl.multiple_of(s * SHARD, SHARD), SHARD)

    def hidden(s):
        rows = rows_of(s)
        acc[...] = jnp.zeros_like(acc)

        def contract(k, _):
            cols = pl.ds(pl.multiple_of(k * STEP, STEP), STEP)
            xs = xall[rows, cols]
            acc[0] += jnp.dot(xs, wg[cols, :], preferred_element_type=F32)
            acc[1] += jnp.dot(xs, wu[cols, :], preferred_element_type=F32)
            acc[2] += lax.dot_general(dall[rows, cols], wd[:, cols], NT, preferred_element_type=F32)
            return 0

        lax.fori_loop(0, D // STEP, contract, 0)
        g, u, q = acc[0], acc[1], acc[2]
        sig = jax.nn.sigmoid(g)
        dg_ref[rows, :] = (q * u * sig * (1.0 + g * (1.0 - sig))).astype(BF)
        du_ref[rows, :] = (q * (g * sig)).astype(BF)

    def pair(of):
        def body(i, _):
            hidden(of(i))
            return 0

        lax.fori_loop(0, 2, body, 0)

    def keep(s):
        copy_in(xall.at[rows_of(s), :], x_out.at[rows_of(s), :])

    via_up, via_down = slots_for(), slots_for()
    for t, h in ((0, 0), (0, 1), (1, 0)):
        arrive(to_side[t, h], piece(t, h, side))
        send(via_up[t, h], piece(t, h, side), piece(t, h, side), (ex, up))
        send(via_down[t, h], piece(t, h, side), piece(t, h, side), (ex, down))
    halves = (slice(0, D // 2), slice(D // 2, D))

    def half_piece(s, j):
        return dall.at[pl.ds(pl.multiple_of(s * SHARD + PIECE, PIECE), PIECE), halves[j]]

    far_up, far_down = slot(), slot()
    arrive(to_up[1, 1], piece(1, 1, down))
    send(far_up, half_piece(down, 0), half_piece(down, 0), (ex, up))
    over = [slot(), slot(), slot(), slot()]
    send(over[0], piece(1, 1, down), piece(1, 1, down), (ex, side))
    arrive(to_down[1, 1], piece(1, 1, up))
    send(far_down, half_piece(up, 1), half_piece(up, 1), (ex, down))
    send(over[1], piece(1, 1, up), piece(1, 1, up), (ex, side))
    fwd = {name: slot() for name in ("x0", "x1", "px0", "px1", "d0", "pd0")}
    for t, h in ((0, 0), (0, 1), (1, 0)):
        arrive(to_up[t, h], piece(t, h, down))
        arrive(to_down[t, h], piece(t, h, up))
    send(fwd["x0"], piece(0, 0, down), piece(0, 0, down), (ex, up))
    send(fwd["x1"], piece(0, 1, up), piece(0, 1, up), (ex, down))
    arrive(to_side[1, 1], piece(1, 1, side))
    pair(lambda i: at(i, 0))
    keep(dp)
    keep(side)
    pside_down, pside_up = at(1, NZ - 1), at(1, 1)
    far, pfar = at(0, 2), at(1, 2)
    arrive(via_up[0, 0], piece(0, 0, pside_down))
    send(fwd["px0"], piece(0, 0, pside_down), piece(0, 0, pside_down), (ex, up))
    arrive(via_down[0, 1], piece(0, 1, pside_up))
    send(fwd["px1"], piece(0, 1, pside_up), piece(0, 1, pside_up), (ex, down))
    send(fwd["d0"], piece(1, 0, down), piece(1, 0, down), (ex, up))
    arrive(via_down[1, 0], piece(1, 0, pside_up))
    send(fwd["pd0"], piece(1, 0, pside_up), piece(1, 0, pside_up), (ex, down))
    pair(lambda i: at(0, NZ - 1 - 2 * i))
    keep(down)
    keep(up)
    arrive(far_up, half_piece(far, 0))
    send(over[2], half_piece(far, 0), half_piece(far, 0), (ex, side))
    arrive(far_down, half_piece(far, 1))
    send(over[3], half_piece(far, 1), half_piece(far, 1), (ex, side))
    arrive(via_up[0, 1], piece(0, 1, pside_down))
    arrive(via_up[1, 0], piece(1, 0, pside_down))
    arrive(via_down[0, 0], piece(0, 0, pside_up))
    arrive(over[0], piece(1, 1, pside_down))
    arrive(over[1], piece(1, 1, pside_up))
    pair(lambda i: at(1, NZ - 1 - 2 * i))
    keep(pside_down)
    keep(pside_up)
    arrive(fwd["x0"], piece(0, 0, far))
    arrive(fwd["x1"], piece(0, 1, far))
    arrive(fwd["d0"], piece(1, 0, far))
    arrive(fwd["px0"], piece(0, 0, pfar))
    arrive(fwd["px1"], piece(0, 1, pfar))
    arrive(fwd["pd0"], piece(1, 0, pfar))
    arrive(over[2], half_piece(pfar, 0))
    arrive(over[3], half_piece(pfar, 1))
    pair(lambda i: at(i, 2))
    keep(far)
    keep(pfar)
    for c in sent:
        c.wait_send()
    for c in local[-DP:]:
        c.wait()
    tab_copy.wait()


def gather_rows(xt, dt, packed, wg, wu, wd):
    hbm = pl.BlockSpec(memory_space=pl.ANY)
    vmem = pl.BlockSpec(memory_space=pltpu.VMEM)
    rows = DP * SHARD
    return pl.pallas_call(
        gather_kernel,
        out_shape=(
            jax.ShapeDtypeStruct((rows, D), BF),
            jax.ShapeDtypeStruct((rows, HID), BF),
            jax.ShapeDtypeStruct((rows, HID), BF),
            jax.ShapeDtypeStruct((2 * TOP, LOCAL), BF),
        ),
        in_specs=[hbm] * 6,
        out_specs=(hbm, vmem, vmem, hbm),
        scratch_shapes=[
            pltpu.VMEM((2, WIDE, LOCAL), BF),
            pltpu.VMEM((2 * TOP, LOCAL), BF),
            pltpu.VMEM((CHIPS, LOCAL), F32),
            pltpu.VMEM((CHIPS, LOCAL), F32),
            pltpu.VMEM((CHIPS * PIECE, LOCAL // 2), BF),
            pltpu.VMEM((2, 2, CHIPS, PIECE, WIDE), BF),
            pltpu.VMEM((rows, D), BF),
            pltpu.VMEM((rows, D), BF),
            pltpu.VMEM((D, HID), BF),
            pltpu.VMEM((D, HID), BF),
            pltpu.VMEM((HID, D), BF),
            pltpu.VMEM((3, SHARD, HID), F32),
            pltpu.SemaphoreType.DMA((96,)),
            pltpu.SemaphoreType.DMA((96,)),
            pltpu.SemaphoreType.DMA((24,)),
        ],
        compiler_params=pltpu.CompilerParams(
            collective_id=0, has_side_effects=True, vmem_limit_bytes=60 * 1024 * 1024
        ),
        name="gather_rows",
    )(xt, dt, packed, wg, wu, wd)

NA = 2
CA = NA * WIDE
CB = D - CA
LA, RA = slice(0, CA // 2), slice(CA // 2, CA)
ALL_A, ALL_B = slice(0, CA), slice(CA, D)
LB, RB = slice(CA, CA + CB // 2), slice(CA + CB // 2, D)
PART = 512
TILE = 512


def return_kernel(
    dg_ref, du_ref, wg_ref, wu_ref, x_ref, tab_ref,
    out_t, gg_out, gu_out,
    p, wg, wu, xs, gbuf, tabs, code, onehot, got_a, relay_a, fin_a, relay_b, fin_b, got_b, back, outbuf,
    ssem, rsem, lsem,
):
    ex = lax.axis_index("expert")
    dp = lax.axis_index("dp")
    core = ex % 2
    row, z = dp // NZ, dp % NZ

    def at(y, dz):
        return y * NZ + (z + dz) % NZ

    up, down, side = at(row, 1), at(row, NZ - 1), at(1 - row, 0)

    barrier = pltpu.get_barrier_semaphore()
    for r in range(1, EXP):
        pl.semaphore_signal(barrier, inc=1, device_id=((ex + r) % EXP, dp), device_id_type=MESH)
    for peer in (up, down, side):
        pl.semaphore_signal(barrier, inc=1, device_id=(ex, peer), device_id_type=MESH)

    local = []

    def copy(src, dst):
        c = pltpu.make_async_copy(src, dst, lsem.at[len(local)])
        c.start()
        local.append(c)
        return c

    in_w = [copy(wg_ref, wg), copy(wu_ref, wu)]
    in_tab = copy(tab_ref, tabs)
    in_x = copy(x_ref, xs)
    for c in in_w:
        c.wait()

    sent = []
    slots = [0]

    def slot():
        slots[0] += 1
        return slots[0] - 1

    def send(k, src, dst, device):
        c = pltpu.make_async_remote_copy(
            src_ref=src, dst_ref=dst, send_sem=ssem.at[k], recv_sem=rsem.at[k],
            device_id=device, device_id_type=MESH,
        )
        c.start()
        sent.append(c)

    def arrive(k, dst):
        pltpu.make_async_remote_copy(
            src_ref=dst, dst_ref=dst, send_sem=ssem.at[k], recv_sem=rsem.at[k],
            device_id=(ex, side), device_id_type=MESH,
        ).wait_recv()

    def rows_of(s):
        return pl.ds(pl.multiple_of(s * SHARD, SHARD), SHARD)

    def part_of(s, h):
        return pl.ds(pl.multiple_of(s * SHARD + h * PIECE, PIECE), PIECE)

    def partial(dz):
        first, second = rows_of(at(0, dz)), rows_of(at(1, dz))
        g2 = jnp.concatenate([dg_ref[first, :], dg_ref[second, :]], axis=0)
        u2 = jnp.concatenate([du_ref[first, :], du_ref[second, :]], axis=0)

        def body(k, _):
            cols = pl.ds(pl.multiple_of(k * WIDE, WIDE), WIDE)
            v = lax.dot_general(g2, wg[cols, :], NT, preferred_element_type=F32)
            v = (v + lax.dot_general(u2, wu[cols, :], NT, preferred_element_type=F32)).astype(BF)
            p[first, cols] = v[:SHARD]
            p[second, cols] = v[SHARD:]
            return 0

        lax.fori_loop(0, D // WIDE, body, 0)

    def add(s, h, cols, *others):
        def body(i, _):
            here = pl.ds(pl.multiple_of(s * SHARD + h * PIECE + i * 16, 16), 16)
            total = p[here, cols].astype(F32)
            for other in others:
                total = total + other(pl.ds(pl.multiple_of(h * PIECE + i * 16, 16), 16)).astype(F32)
            p[here, cols] = total.astype(BF)
            return 0

        lax.fori_loop(0, PIECE // 16, body, 0)

    half = [slice(h * PIECE, (h + 1) * PIECE) for h in range(2)]
    s_ya = {(h, dz): slot() for h in range(2) for dz in range(NZ)}
    s_relay_b = {(h, y, d): slot() for h in range(2) for y in range(2) for d in range(2)}
    s_fin_l = {(h, y, d): slot() for h in range(2) for y in range(2) for d in range(2)}
    s_fin_r = {(h, y, d): slot() for h in range(2) for y in range(2) for d in range(2)}
    s_relay_a = {(h, d): slot() for h in range(2) for d in range(2)}
    s_fin_a = {(h, d): slot() for h in range(2) for d in range(2)}
    s_yb = [slot(), slot()]
    s_back = [[slot() for _ in range(EXP)] for _ in range(2)]
    rel_l, rel_r = slice(0, CB // 2), slice(CB // 2, CB)

    def over_y(dz, h):
        send(s_ya[h, dz], p.at[part_of(at(1 - row, dz), h), ALL_A], got_a.at[dz, half[h], :], (ex, side))

    def far_b(h):
        for y in range(2):
            src = part_of(at(y, 2), h)
            send(s_relay_b[h, y, 0], p.at[src, LB], relay_b.at[0, y, half[h], :], (ex, up))
            send(s_relay_b[h, y, 1], p.at[src, RB], relay_b.at[1, y, half[h], :], (ex, down))

    def direct_up(h):
        for y in range(2):
            send(s_fin_r[h, y, 0], p.at[part_of(at(y, 1), h), RB], fin_b.at[0, y, half[h], rel_r], (ex, up))

    def direct_down(h):
        for y in range(2):
            send(s_fin_l[h, y, 1], p.at[part_of(at(y, NZ - 1), h), LB], fin_b.at[1, y, half[h], rel_l], (ex, down))

    def combined_b(h):
        for y in range(2):
            arrive(s_relay_b[h, y, 0], relay_b.at[0, y, half[h], :])
            add(at(y, 1), h, LB, lambda r, y=y: relay_b[0, y, r, :])
            send(s_fin_l[h, y, 0], p.at[part_of(at(y, 1), h), LB], fin_b.at[0, y, half[h], rel_l], (ex, up))
            arrive(s_relay_b[h, y, 1], relay_b.at[1, y, half[h], :])
            add(at(y, NZ - 1), h, RB, lambda r, y=y: relay_b[1, y, r, :])
            send(s_fin_r[h, y, 1], p.at[part_of(at(y, NZ - 1), h), RB], fin_b.at[1, y, half[h], rel_r], (ex, down))

    def far_a(h):
        arrive(s_ya[h, 2], got_a.at[2, half[h], :])
        add(at(row, 2), h, ALL_A, lambda r: got_a[2, r, :])
        src = part_of(at(row, 2), h)
        send(s_relay_a[h, 0], p.at[src, LA], relay_a.at[0, half[h], :], (ex, up))
        send(s_relay_a[h, 1], p.at[src, RA], relay_a.at[1, half[h], :], (ex, down))

    def near_a(h):
        for d, dz, peer, mixed in ((0, 1, up, LA), (1, NZ - 1, down, RA)):
            arrive(s_ya[h, dz], got_a.at[dz, half[h], :])
            add(at(row, dz), h, ALL_A, lambda r, dz=dz: got_a[dz, r, :])
            arrive(s_relay_a[h, d], relay_a.at[d, half[h], :])
            add(at(row, dz), h, mixed, lambda r, d=d: relay_a[d, r, :])
            send(s_fin_a[h, d], p.at[part_of(at(row, dz), h), ALL_A], fin_a.at[d, half[h], :], (ex, peer))

    def fold_b(h):
        for y in range(2):
            for d in range(2):
                arrive(s_fin_l[h, y, d], fin_b.at[d, y, half[h], rel_l])
                arrive(s_fin_r[h, y, d], fin_b.at[d, y, half[h], rel_r])
        add(side, h, ALL_B, lambda r: fin_b[0, 1 - row, r, :], lambda r: fin_b[1, 1 - row, r, :])
        send(s_yb[h], p.at[part_of(side, h), ALL_B], got_b.at[half[h], :], (ex, side))

    def finish(h):
        arrive(s_ya[h, 0], got_a.at[0, half[h], :])
        for d in range(2):
            arrive(s_fin_a[h, d], fin_a.at[d, half[h], :])
        add(dp, h, ALL_A, lambda r: got_a[0, r, :], lambda r: fin_a[0, r, :], lambda r: fin_a[1, r, :])
        arrive(s_yb[h], got_b.at[half[h], :])
        add(
            dp, h, ALL_B,
            lambda r: fin_b[0, row, r, :], lambda r: fin_b[1, row, r, :], lambda r: got_b[r, :],
        )
        where = pl.ds(pl.multiple_of(ex * PIECE, PIECE), PIECE)

        def cols(e):
            return pl.ds(pl.multiple_of(e // 2 * WIDE + e % 2 * 384, 128), PART)

        for r in range(1, EXP):
            to = (ex + r) % EXP
            send(s_back[h][r], p.at[part_of(dp, h), cols(to)], back.at[h, where, :], (to, dp))
        return copy(p.at[part_of(dp, h), cols(ex)], back.at[h, where, :])

    def combine(h, own):
        own.wait()
        for r in range(1, EXP):
            src = (ex + EXP - r) % EXP
            arrive(s_back[h][r], back.at[h, pl.ds(pl.multiple_of(src * PIECE, PIECE), PIECE), :])
        for n in range(0, LOCAL // 2, 256):
            got = lax.dot_general(
                back[h], onehot[h, :, n : n + 256], (((0,), (0,)), ((), ())), preferred_element_type=F32
            )
            outbuf[:, h * (LOCAL // 2) + n : h * (LOCAL // 2) + n + 256] = got.astype(BF)
        lanes = slice(h * (LOCAL // 2), (h + 1) * (LOCAL // 2))
        keep = pl.ds(pl.multiple_of(core * 64, 64), WIDE // 2)
        return copy(outbuf.at[keep, lanes], out_t.at[:, lanes])

    def place_tables():
        in_tab.wait()
        table = tabs[...].astype(F32)[:TOP]
        ids = lax.broadcasted_iota(jnp.int32, (EXP, LOCAL), 0).astype(F32)
        hit = jnp.zeros((EXP, LOCAL), F32)
        for k in range(TOP):
            hit = hit + jnp.where(table[k : k + 1] == ids, 1.0, 0.0)
        stacked = jnp.concatenate([hit[:, b * TOK : (b + 1) * TOK] for b in range(EXP)], axis=0)
        tri = (
            lax.broadcasted_iota(jnp.int32, (TOK, TOK), 0) < lax.broadcasted_iota(jnp.int32, (TOK, TOK), 1)
        ).astype(F32).astype(BF)
        before = jnp.dot(stacked.astype(BF), tri, preferred_element_type=F32)
        for b in range(EXP):
            part = slice(b * EXP, (b + 1) * EXP)
            code[:, b * TOK : (b + 1) * TOK] = jnp.where(
                stacked[part] > 0.0, before[part] + float(CAP * (b % CHIPS)), -1.0
            )
        slot_row = lax.broadcasted_iota(jnp.int32, (PIECE, LOCAL // 2), 0).astype(F32)
        for h in range(2):
            for e in range(EXP):
                equal = code[e : e + 1, h * (LOCAL // 2) : (h + 1) * (LOCAL // 2)] == slot_row
                onehot[h, e * PIECE : (e + 1) * PIECE] = jnp.where(equal, 1.0, 0.0).astype(BF)

    def weight_grads(start, stop):
        def body(i, _):
            cols = pl.ds(pl.multiple_of(i * TILE, TILE), TILE)
            block = xs[:, cols]
            dims = (((0,), (0,)), ((), ()))
            gbuf[0, cols, :] = lax.dot_general(block, dg_ref[...], dims, preferred_element_type=F32).astype(BF)
            gbuf[1, cols, :] = lax.dot_general(block, du_ref[...], dims, preferred_element_type=F32).astype(BF)
            return 0

        lax.fori_loop(start, stop, body, 0)
        span = pl.ds(start * TILE, (stop - start) * TILE)
        return [copy(gbuf.at[j, span, :], out.at[span, :]) for j, out in enumerate((gg_out, gu_out))]

    partial(2)
    pl.semaphore_wait(barrier, EXP - 1 + 3)
    over_y(2, 0)
    far_b(0)
    partial(1)
    over_y(1, 0)
    direct_up(0)
    partial(NZ - 1)
    over_y(NZ - 1, 0)
    direct_down(0)
    partial(0)
    over_y(0, 0)
    far_a(0)
    combined_b(0)
    far_b(1)
    for dz in (2, 1, NZ - 1, 0):
        over_y(dz, 1)
    near_a(0)
    direct_up(1)
    direct_down(1)
    in_x.wait()
    stores = weight_grads(0, 4)
    fold_b(0)
    far_a(1)
    combined_b(1)
    place_tables()
    near_a(1)
    own0 = finish(0)
    stores += weight_grads(4, D // TILE)
    fold_b(1)
    out0 = combine(0, own0)
    own1 = finish(1)
    out1 = combine(1, own1)
    for c in sent:
        c.wait_send()
    for c in stores + [out0, out1]:
        c.wait()


def return_rows(dg, du, wg, wu, x, table):
    hbm = pl.BlockSpec(memory_space=pl.ANY)
    vmem = pl.BlockSpec(memory_space=pltpu.VMEM)
    rows = DP * SHARD
    return pl.pallas_call(
        return_kernel,
        out_shape=(
            jax.ShapeDtypeStruct((WIDE // 2, LOCAL), BF),
            jax.ShapeDtypeStruct((D, HID), BF),
            jax.ShapeDtypeStruct((D, HID), BF),
        ),
        in_specs=[vmem, vmem, hbm, hbm, hbm, hbm],
        out_specs=(hbm, hbm, hbm),
        scratch_shapes=[
            pltpu.VMEM((rows, D), BF),
            pltpu.VMEM((D, HID), BF),
            pltpu.VMEM((D, HID), BF),
            pltpu.VMEM((rows, D), BF),
            pltpu.VMEM((2, D, HID), BF),
            pltpu.VMEM((2 * TOP, LOCAL), BF),
            pltpu.VMEM((EXP, LOCAL), F32),
            pltpu.VMEM((2, EXP * PIECE, LOCAL // 2), BF),
            pltpu.VMEM((NZ, SHARD, CA), BF),
            pltpu.VMEM((2, SHARD, CA // 2), BF),
            pltpu.VMEM((2, SHARD, CA), BF),
            pltpu.VMEM((2, 2, SHARD, CB // 2), BF),
            pltpu.VMEM((2, 2, SHARD, CB), BF),
            pltpu.VMEM((SHARD, CB), BF),
            pltpu.VMEM((2, EXP * PIECE, PART), BF),
            pltpu.VMEM((PART, LOCAL), BF),
            pltpu.SemaphoreType.DMA((100,)),
            pltpu.SemaphoreType.DMA((100,)),
            pltpu.SemaphoreType.DMA((16,)),
        ],
        compiler_params=pltpu.CompilerParams(
            collective_id=1, has_side_effects=True, vmem_limit_bytes=63 * 1024 * 1024
        ),
        name="return_rows",
    )(dg, du, wg, wu, x, table)


def per_device(attn_rows, out_grad, routes, gates, w_gate, w_up, w_down):
    packed = jnp.concatenate([routes.T.astype(BF), gates.T], axis=0)
    gate_mat, up_mat, down_mat = w_gate[0], w_up[0], w_down[0]
    x, dg, du, table = gather_rows(attn_rows.T, out_grad.T, packed, gate_mat, up_mat, down_mat)
    grad_t, g_gate, g_up = return_rows(dg, du, gate_mat, up_mat, x, table)
    return grad_t.T, g_gate[None], g_up[None]


def solution(mesh):
    return jax.shard_map(
        per_device,
        mesh=mesh,
        in_specs=(
            P("dp", "expert"),
            P("dp", "expert"),
            P(("dp", "expert"), None),
            P(("dp", "expert"), None),
            P("expert", None, "dp"),
            P("expert", None, "dp"),
            P("expert", "dp", None),
        ),
        out_specs=(P("dp", "expert"), P("expert", None, "dp"), P("expert", None, "dp")),
        check_vma=False,
    )
```

```python
import jax
import jax.numpy as jnp
from jax import lax
from jax.experimental import pallas as pl
from jax.experimental.pallas import tpu as pltpu
from jax.sharding import PartitionSpec as P

BF = jnp.bfloat16
F32 = jnp.float32
MESH = pl.DeviceIdType.MESH
NT = (((1,), (1,)), ((), ()))
EXP, DP, NZ, CHIPS = 16, 8, 4, 8
TOK, TOP, CAP = 128, 8, 6
LOCAL = EXP * TOK
WIDE, D, HID = 896, 7168, 256
PIECE = 48
SHARD = 96
STEP = 1024


def gather_kernel(
    xt_ref, dt_ref, pk_ref, wg_ref, wu_ref, wd_ref,
    x_out, dg_ref, du_ref, tab_out,
    raw, tabs, code, coef, onehot, pay, xall, dall, wg, wu, wd, acc,
    ssem, rsem, lsem,
):
    ex = lax.axis_index("expert")
    dp = lax.axis_index("dp")
    core = ex % 2
    chip = ex // 2
    row, z = dp // NZ, dp % NZ

    def at(dy, dz):
        return (row + dy) % 2 * NZ + (z + dz) % NZ

    up, down, side = at(0, 1), at(0, NZ - 1), at(1, 0)
    bufs = (xall, dall)

    barrier = pltpu.get_barrier_semaphore()
    for r in range(1, EXP):
        pl.semaphore_signal(barrier, inc=1, device_id=((ex + r) % EXP, dp), device_id_type=MESH)
    for peer in (up, down, side):
        pl.semaphore_signal(barrier, inc=1, device_id=(ex, peer), device_id_type=MESH)

    local = []

    def copy_in(src, dst):
        c = pltpu.make_async_copy(src, dst, lsem.at[len(local)])
        c.start()
        local.append(c)
        return c

    mine = pl.ds(pl.multiple_of(core * (WIDE // 2), WIDE // 2), WIDE // 2)
    lanes = pl.ds(pl.multiple_of(ex * TOK, TOK), TOK)
    in_tab = copy_in(pk_ref, tabs.at[:, lanes])
    in_raw = [copy_in(ref, raw.at[t, mine, :]) for t, ref in enumerate((xt_ref, dt_ref))]
    in_w = [copy_in(wg_ref, wg), copy_in(wu_ref, wu), copy_in(wd_ref, wd)]

    pl.semaphore_wait(barrier, EXP - 1 + 3)

    sent = []
    slots = [0]

    def slot():
        slots[0] += 1
        return slots[0] - 1

    def send(k, src, dst, device):
        c = pltpu.make_async_remote_copy(
            src_ref=src, dst_ref=dst, send_sem=ssem.at[k], recv_sem=rsem.at[k],
            device_id=device, device_id_type=MESH,
        )
        c.start()
        sent.append(c)

    def arrive(k, dst):
        pltpu.make_async_remote_copy(
            src_ref=dst, dst_ref=dst, send_sem=ssem.at[k], recv_sem=rsem.at[k],
            device_id=(ex, side), device_id_type=MESH,
        ).wait_recv()

    other = pl.ds(pl.multiple_of((1 - core) * (WIDE // 2), WIDE // 2), WIDE // 2)
    tab_slot = [slot() for _ in range(EXP)]
    for r in range(1, EXP):
        send(tab_slot[r], pk_ref, tabs.at[:, lanes], ((ex + r) % EXP, dp))
    raw_slot = [slot(), slot()]
    sibling = (chip * 2 + 1 - core, dp)
    for t, ref in enumerate((xt_ref, dt_ref)):
        send(raw_slot[t], ref, raw.at[t, mine, :], sibling)

    in_tab.wait()
    for r in range(1, EXP):
        src = (ex + EXP - r) % EXP
        arrive(tab_slot[r], tabs.at[:, pl.ds(pl.multiple_of(src * TOK, TOK), TOK)])

    copy_in(tabs, tab_out)
    tab_copy = local[-1]
    table = tabs[...].astype(F32)
    route, gate = table[:TOP], table[TOP:]
    ids = (lax.broadcasted_iota(jnp.int32, (CHIPS, LOCAL), 0) * 2 + core).astype(F32)
    hit = jnp.zeros((CHIPS, LOCAL), F32)
    weight = jnp.zeros((CHIPS, LOCAL), F32)
    for k in range(TOP):
        same = route[k : k + 1] == ids
        hit = hit + jnp.where(same, 1.0, 0.0)
        weight = weight + jnp.where(same, gate[k : k + 1], 0.0)
    coef[...] = weight
    stacked = jnp.concatenate([hit[:, b * TOK : (b + 1) * TOK] for b in range(EXP)], axis=0)
    tri = (
        lax.broadcasted_iota(jnp.int32, (TOK, TOK), 0) < lax.broadcasted_iota(jnp.int32, (TOK, TOK), 1)
    ).astype(F32).astype(BF)
    before = jnp.dot(stacked.astype(BF), tri, preferred_element_type=F32)
    for b in range(EXP):
        part = slice(b * CHIPS, (b + 1) * CHIPS)
        code[:, b * TOK : (b + 1) * TOK] = jnp.where(
            stacked[part] > 0.0, before[part] + float(CAP * (b % CHIPS)), -1.0
        )

    slot_row = lax.broadcasted_iota(jnp.int32, (PIECE, LOCAL // 2), 0).astype(F32)
    own_rows = [pl.ds(pl.multiple_of(dp * SHARD + h * PIECE, PIECE), PIECE) for h in range(2)]
    chip_cols = pl.ds(pl.multiple_of(chip * WIDE, WIDE), WIDE)
    a2a_slot = [[[slot() for _ in range(CHIPS)] for _ in range(2)] for _ in range(2)]
    a2a_self = [[None, None], [None, None]]

    def dispatch(t, h):
        half = slice(h * (LOCAL // 2), (h + 1) * (LOCAL // 2))
        for i in range(CHIPS):
            equal = code[i : i + 1, half] == slot_row
            value = 1.0 if t == 0 else coef[i : i + 1, half]
            onehot[i * PIECE : (i + 1) * PIECE] = jnp.where(equal, value, 0.0).astype(BF)
        for n in range(0, WIDE, 128):
            got = lax.dot_general(onehot[...], raw[t, n : n + 128, half], NT, preferred_element_type=F32)
            pay[t, h, :, :, n : n + 128] = got.astype(BF).reshape(CHIPS, PIECE, 128)
        where = bufs[t].at[own_rows[h], chip_cols]
        for r in range(1, CHIPS):
            to = (chip + r) % CHIPS
            send(a2a_slot[t][h][r], pay.at[t, h, to], where, (to * 2 + core, dp))
        a2a_self[t][h] = copy_in(pay.at[t, h, chip], where)

    def complete(t, h):
        a2a_self[t][h].wait()
        for r in range(1, CHIPS):
            src = (chip + CHIPS - r) % CHIPS
            arrive(a2a_slot[t][h][r], bufs[t].at[own_rows[h], pl.ds(pl.multiple_of(src * WIDE, WIDE), WIDE)])

    def rows_of(s):
        return pl.ds(pl.multiple_of(s * SHARD, SHARD), SHARD)

    def contract(s, with_x, with_d):
        rows = rows_of(s)
        if with_x:
            acc[0:2] = jnp.zeros((2, SHARD, HID), F32)
        if with_d:
            acc[2] = jnp.zeros((SHARD, HID), F32)

        def body(k, _):
            cols = pl.ds(pl.multiple_of(k * STEP, STEP), STEP)
            if with_x:
                xs = xall[rows, cols]
                acc[0] += jnp.dot(xs, wg[cols, :], preferred_element_type=F32)
                acc[1] += jnp.dot(xs, wu[cols, :], preferred_element_type=F32)
            if with_d:
                acc[2] += lax.dot_general(dall[rows, cols], wd[:, cols], NT, preferred_element_type=F32)
            return 0

        lax.fori_loop(0, D // STEP, body, 0)

    def activate(s):
        rows = rows_of(s)
        g, u, q = acc[0], acc[1], acc[2]
        sig = jax.nn.sigmoid(g)
        dg_ref[rows, :] = (q * u * sig * (1.0 + g * (1.0 - sig))).astype(BF)
        du_ref[rows, :] = (q * (g * sig)).astype(BF)
        copy_in(xall.at[rows, :], x_out.at[rows, :])

    def hidden(s):
        contract(s, True, True)
        activate(s)

    half = D // 2
    left, right, whole = slice(0, half), slice(half, D), slice(0, D)
    low, high = slice(0, half // 2), slice(half // 2, half)

    def piece(t, h, s, cols=whole):
        return bufs[t].at[pl.ds(pl.multiple_of(s * SHARD + h * PIECE, PIECE), PIECE), cols]

    def pass_on(k, to, t, h, s, cols=whole):
        send(k, piece(t, h, s, cols), piece(t, h, s, cols), (ex, to))

    def slots_for(*names):
        return {name: slot() for name in names}

    pieces = ((0, 0), (0, 1), (1, 0), (1, 1))
    to_up, to_down, to_side = slots_for(*pieces), slots_for(*pieces), slots_for(*pieces)

    def spread_z(t, h):
        pass_on(to_up[t, h], up, t, h, dp)
        pass_on(to_down[t, h], down, t, h, dp)

    def spread_y(t, h):
        pass_on(to_side[t, h], side, t, h, dp)

    in_raw[0].wait()
    arrive(raw_slot[0], raw.at[0, other, :])
    dispatch(0, 0)
    dispatch(0, 1)
    complete(0, 0)
    spread_z(0, 0)
    in_raw[1].wait()
    arrive(raw_slot[1], raw.at[1, other, :])
    dispatch(1, 0)
    complete(0, 1)
    spread_z(0, 1)
    dispatch(1, 1)
    spread_y(0, 0)
    spread_y(0, 1)
    complete(1, 0)
    spread_z(1, 0)
    spread_y(1, 0)
    complete(1, 1)
    spread_z(1, 1)
    spread_y(1, 1)
    for c in in_w:
        c.wait()

    far, pdown, pup, pfar = at(0, 2), at(1, NZ - 1), at(1, 1), at(1, 2)
    early = ((0, 0, whole), (0, 1, whole), (1, 0, left))
    via_up, via_down = slots_for(*pieces[:3]), slots_for(*pieces[:3])

    def relay_side(i):
        t, h, cols = early[i]
        arrive(to_side[t, h], piece(t, h, side))
        pass_on(via_up[t, h], up, t, h, side, cols)
        pass_on(via_down[t, h], down, t, h, side, cols)

    relay_side(0)
    hidden(dp)
    relay_side(1)
    for t, h in pieces[:2]:
        arrive(to_up[t, h], piece(t, h, down))
        arrive(to_down[t, h], piece(t, h, up))
    over = slots_for("d", "dr", "u", "ur", "fl", "fr", "f0")
    two = slots_for("d1l", "d1r", "d0l", "d0r", "x0", "x1", "px0", "px1", "pl", "ph")
    arrive(to_up[1, 0], piece(1, 0, down))
    pass_on(over["dr"], side, 1, 0, down, right)
    arrive(to_down[1, 0], piece(1, 0, up))
    pass_on(over["ur"], side, 1, 0, up, right)
    arrive(to_up[1, 1], piece(1, 1, down))
    pass_on(two["d1l"], up, 1, 1, down, left)
    pass_on(over["d"], side, 1, 1, down)
    arrive(to_down[1, 1], piece(1, 1, up))
    pass_on(two["d1r"], down, 1, 1, up, right)
    pass_on(over["u"], side, 1, 1, up)
    pass_on(two["d0l"], up, 1, 0, down, left)
    pass_on(two["d0r"], down, 1, 0, up, right)
    relay_side(2)
    pass_on(two["x0"], up, 0, 0, down)
    pass_on(two["x1"], down, 0, 1, up)
    hidden(down)
    arrive(to_side[1, 1], piece(1, 1, side))
    hidden(side)
    arrive(via_up[0, 0], piece(0, 0, pdown))
    pass_on(two["px0"], up, 0, 0, pdown)
    arrive(via_down[0, 1], piece(0, 1, pup))
    pass_on(two["px1"], down, 0, 1, pup)
    hidden(up)
    arrive(two["d0r"], piece(1, 0, far, right))
    pass_on(over["f0"], side, 1, 0, far, right)
    arrive(two["d1l"], piece(1, 1, far, left))
    pass_on(over["fl"], side, 1, 1, far, left)
    arrive(two["d1r"], piece(1, 1, far, right))
    pass_on(over["fr"], side, 1, 1, far, right)
    arrive(via_up[1, 0], piece(1, 0, pdown, left))
    pass_on(two["pl"], up, 1, 0, pdown, low)
    arrive(via_down[1, 0], piece(1, 0, pup, left))
    pass_on(two["ph"], down, 1, 0, pup, high)
    arrive(via_up[0, 1], piece(0, 1, pdown))
    arrive(over["dr"], piece(1, 0, pdown, right))
    arrive(over["d"], piece(1, 1, pdown))
    hidden(pdown)
    arrive(via_down[0, 0], piece(0, 0, pup))
    arrive(over["ur"], piece(1, 0, pup, right))
    arrive(over["u"], piece(1, 1, pup))
    hidden(pup)
    arrive(two["d0l"], piece(1, 0, far, left))
    arrive(two["x0"], piece(0, 0, far))
    arrive(two["x1"], piece(0, 1, far))
    hidden(far)
    arrive(over["f0"], piece(1, 0, pfar, right))
    arrive(over["fl"], piece(1, 1, pfar, left))
    arrive(over["fr"], piece(1, 1, pfar, right))
    arrive(two["px0"], piece(0, 0, pfar))
    arrive(two["px1"], piece(0, 1, pfar))
    contract(pfar, True, False)
    arrive(two["pl"], piece(1, 0, pfar, low))
    arrive(two["ph"], piece(1, 0, pfar, high))
    contract(pfar, False, True)
    activate(pfar)
    for c in sent:
        c.wait_send()
    for c in local[-DP:]:
        c.wait()
    tab_copy.wait()


def gather_rows(xt, dt, packed, wg, wu, wd):
    hbm = pl.BlockSpec(memory_space=pl.ANY)
    vmem = pl.BlockSpec(memory_space=pltpu.VMEM)
    rows = DP * SHARD
    return pl.pallas_call(
        gather_kernel,
        out_shape=(
            jax.ShapeDtypeStruct((rows, D), BF),
            jax.ShapeDtypeStruct((rows, HID), BF),
            jax.ShapeDtypeStruct((rows, HID), BF),
            jax.ShapeDtypeStruct((2 * TOP, LOCAL), BF),
        ),
        in_specs=[hbm] * 6,
        out_specs=(hbm, vmem, vmem, hbm),
        scratch_shapes=[
            pltpu.VMEM((2, WIDE, LOCAL), BF),
            pltpu.VMEM((2 * TOP, LOCAL), BF),
            pltpu.VMEM((CHIPS, LOCAL), F32),
            pltpu.VMEM((CHIPS, LOCAL), F32),
            pltpu.VMEM((CHIPS * PIECE, LOCAL // 2), BF),
            pltpu.VMEM((2, 2, CHIPS, PIECE, WIDE), BF),
            pltpu.VMEM((rows, D), BF),
            pltpu.VMEM((rows, D), BF),
            pltpu.VMEM((D, HID), BF),
            pltpu.VMEM((D, HID), BF),
            pltpu.VMEM((HID, D), BF),
            pltpu.VMEM((3, SHARD, HID), F32),
            pltpu.SemaphoreType.DMA((96,)),
            pltpu.SemaphoreType.DMA((96,)),
            pltpu.SemaphoreType.DMA((24,)),
        ],
        compiler_params=pltpu.CompilerParams(
            collective_id=0, has_side_effects=True, vmem_limit_bytes=60 * 1024 * 1024
        ),
        name="gather_rows",
    )(xt, dt, packed, wg, wu, wd)

NA = 2
CA = NA * WIDE
CB = D - CA
LA, RA = slice(0, CA // 2), slice(CA // 2, CA)
ALL_A, ALL_B = slice(0, CA), slice(CA, D)
LB, RB = slice(CA, CA + CB // 2), slice(CA + CB // 2, D)
PART = 512
TILE = 512


def return_kernel(
    dg_ref, du_ref, wg_ref, wu_ref, x_ref, tab_ref,
    out_t, gg_out, gu_out,
    p, wg, wu, xs, gbuf, tabs, code, onehot, got_a, relay_a, fin_a, relay_b, fin_b, got_b, back, outbuf,
    ssem, rsem, lsem,
):
    ex = lax.axis_index("expert")
    dp = lax.axis_index("dp")
    core = ex % 2
    row, z = dp // NZ, dp % NZ

    def at(y, dz):
        return y * NZ + (z + dz) % NZ

    up, down, side = at(row, 1), at(row, NZ - 1), at(1 - row, 0)

    barrier = pltpu.get_barrier_semaphore()
    for r in range(1, EXP):
        pl.semaphore_signal(barrier, inc=1, device_id=((ex + r) % EXP, dp), device_id_type=MESH)
    for peer in (up, down, side):
        pl.semaphore_signal(barrier, inc=1, device_id=(ex, peer), device_id_type=MESH)

    local = []

    def copy(src, dst):
        c = pltpu.make_async_copy(src, dst, lsem.at[len(local)])
        c.start()
        local.append(c)
        return c

    in_w = [copy(wg_ref, wg), copy(wu_ref, wu)]
    in_tab = copy(tab_ref, tabs)
    in_x = copy(x_ref, xs)
    for c in in_w:
        c.wait()

    sent = []
    slots = [0]

    def slot():
        slots[0] += 1
        return slots[0] - 1

    def send(k, src, dst, device):
        c = pltpu.make_async_remote_copy(
            src_ref=src, dst_ref=dst, send_sem=ssem.at[k], recv_sem=rsem.at[k],
            device_id=device, device_id_type=MESH,
        )
        c.start()
        sent.append(c)

    def arrive(k, dst):
        pltpu.make_async_remote_copy(
            src_ref=dst, dst_ref=dst, send_sem=ssem.at[k], recv_sem=rsem.at[k],
            device_id=(ex, side), device_id_type=MESH,
        ).wait_recv()

    def rows_of(s):
        return pl.ds(pl.multiple_of(s * SHARD, SHARD), SHARD)

    def part_of(s, h):
        return pl.ds(pl.multiple_of(s * SHARD + h * PIECE, PIECE), PIECE)

    def partial(dz):
        first, second = rows_of(at(0, dz)), rows_of(at(1, dz))
        g2 = jnp.concatenate([dg_ref[first, :], dg_ref[second, :]], axis=0)
        u2 = jnp.concatenate([du_ref[first, :], du_ref[second, :]], axis=0)

        def body(k, _):
            cols = pl.ds(pl.multiple_of(k * WIDE, WIDE), WIDE)
            v = lax.dot_general(g2, wg[cols, :], NT, preferred_element_type=F32)
            v = (v + lax.dot_general(u2, wu[cols, :], NT, preferred_element_type=F32)).astype(BF)
            p[first, cols] = v[:SHARD]
            p[second, cols] = v[SHARD:]
            return 0

        lax.fori_loop(0, D // WIDE, body, 0)

    def add(s, h, cols, *others):
        def body(i, _):
            here = pl.ds(pl.multiple_of(s * SHARD + h * PIECE + i * 16, 16), 16)
            total = p[here, cols].astype(F32)
            for other in others:
                total = total + other(pl.ds(pl.multiple_of(h * PIECE + i * 16, 16), 16)).astype(F32)
            p[here, cols] = total.astype(BF)
            return 0

        lax.fori_loop(0, PIECE // 16, body, 0)

    half = [slice(h * PIECE, (h + 1) * PIECE) for h in range(2)]
    s_ya = {(h, dz): slot() for h in range(2) for dz in range(NZ)}
    s_relay_b = {(h, y, d): slot() for h in range(2) for y in range(2) for d in range(2)}
    s_fin_l = {(h, y, d): slot() for h in range(2) for y in range(2) for d in range(2)}
    s_fin_r = {(h, y, d): slot() for h in range(2) for y in range(2) for d in range(2)}
    s_relay_a = {(h, d): slot() for h in range(2) for d in range(2)}
    s_fin_a = {(h, d): slot() for h in range(2) for d in range(2)}
    s_yb = [slot(), slot()]
    s_back = [[slot() for _ in range(EXP)] for _ in range(2)]
    rel_l, rel_r = slice(0, CB // 2), slice(CB // 2, CB)

    def over_y(dz, h):
        send(s_ya[h, dz], p.at[part_of(at(1 - row, dz), h), ALL_A], got_a.at[dz, half[h], :], (ex, side))

    def line(j, dz):
        return at((row + 1 + j) % 2, dz)

    def far_b(h):
        for y in range(2):
            src = part_of(line(y, 2), h)
            send(s_relay_b[h, y, 0], p.at[src, LB], relay_b.at[0, y, half[h], :], (ex, up))
            send(s_relay_b[h, y, 1], p.at[src, RB], relay_b.at[1, y, half[h], :], (ex, down))

    def direct_up(h):
        for y in range(2):
            send(s_fin_r[h, y, 0], p.at[part_of(line(y, 1), h), RB], fin_b.at[0, y, half[h], rel_r], (ex, up))

    def direct_down(h):
        for y in range(2):
            send(s_fin_l[h, y, 1], p.at[part_of(line(y, NZ - 1), h), LB], fin_b.at[1, y, half[h], rel_l], (ex, down))

    def combined_b(h):
        for y in range(2):
            arrive(s_relay_b[h, y, 0], relay_b.at[0, y, half[h], :])
            add(line(y, 1), h, LB, lambda r, y=y: relay_b[0, y, r, :])
            send(s_fin_l[h, y, 0], p.at[part_of(line(y, 1), h), LB], fin_b.at[0, y, half[h], rel_l], (ex, up))
            arrive(s_relay_b[h, y, 1], relay_b.at[1, y, half[h], :])
            add(line(y, NZ - 1), h, RB, lambda r, y=y: relay_b[1, y, r, :])
            send(s_fin_r[h, y, 1], p.at[part_of(line(y, NZ - 1), h), RB], fin_b.at[1, y, half[h], rel_r], (ex, down))

    def far_a(h):
        arrive(s_ya[h, 2], got_a.at[2, half[h], :])
        add(at(row, 2), h, ALL_A, lambda r: got_a[2, r, :])
        src = part_of(at(row, 2), h)
        send(s_relay_a[h, 0], p.at[src, LA], relay_a.at[0, half[h], :], (ex, up))
        send(s_relay_a[h, 1], p.at[src, RA], relay_a.at[1, half[h], :], (ex, down))

    def near_a(h):
        for d, dz, peer, mixed in ((0, 1, up, LA), (1, NZ - 1, down, RA)):
            plain = RA if d == 0 else LA
            arrive(s_ya[h, dz], got_a.at[dz, half[h], :])
            add(at(row, dz), h, plain, lambda r, dz=dz: got_a[dz, r, plain])
            arrive(s_relay_a[h, d], relay_a.at[d, half[h], :])
            add(at(row, dz), h, mixed, lambda r, dz=dz: got_a[dz, r, mixed], lambda r, d=d: relay_a[d, r, :])
            send(s_fin_a[h, d], p.at[part_of(at(row, dz), h), ALL_A], fin_a.at[d, half[h], :], (ex, peer))

    def wait_b(h, j):
        for d in range(2):
            arrive(s_fin_l[h, j, d], fin_b.at[d, j, half[h], rel_l])
            arrive(s_fin_r[h, j, d], fin_b.at[d, j, half[h], rel_r])

    def fold_b(h):
        wait_b(h, 0)
        add(side, h, ALL_B, lambda r: fin_b[0, 0, r, :], lambda r: fin_b[1, 0, r, :])
        send(s_yb[h], p.at[part_of(side, h), ALL_B], got_b.at[half[h], :], (ex, side))

    def finish(h):
        arrive(s_ya[h, 0], got_a.at[0, half[h], :])
        for d in range(2):
            arrive(s_fin_a[h, d], fin_a.at[d, half[h], :])
        add(dp, h, ALL_A, lambda r: got_a[0, r, :], lambda r: fin_a[0, r, :], lambda r: fin_a[1, r, :])
        wait_b(h, 1)
        arrive(s_yb[h], got_b.at[half[h], :])
        add(
            dp, h, ALL_B,
            lambda r: fin_b[0, 1, r, :], lambda r: fin_b[1, 1, r, :], lambda r: got_b[r, :],
        )
        where = pl.ds(pl.multiple_of(ex * PIECE, PIECE), PIECE)

        def cols(e):
            return pl.ds(pl.multiple_of(e // 2 * WIDE + e % 2 * 384, 128), PART)

        for r in range(1, EXP):
            to = (ex + r) % EXP
            send(s_back[h][r], p.at[part_of(dp, h), cols(to)], back.at[h, where, :], (to, dp))
        return copy(p.at[part_of(dp, h), cols(ex)], back.at[h, where, :])

    def combine(h, own):
        own.wait()
        for r in range(1, EXP):
            src = (ex + EXP - r) % EXP
            arrive(s_back[h][r], back.at[h, pl.ds(pl.multiple_of(src * PIECE, PIECE), PIECE), :])
        for n in range(0, LOCAL // 2, 256):
            got = lax.dot_general(
                back[h], onehot[h, :, n : n + 256], (((0,), (0,)), ((), ())), preferred_element_type=F32
            )
            outbuf[:, h * (LOCAL // 2) + n : h * (LOCAL // 2) + n + 256] = got.astype(BF)
        lanes = slice(h * (LOCAL // 2), (h + 1) * (LOCAL // 2))
        keep = pl.ds(pl.multiple_of(core * 64, 64), WIDE // 2)
        return copy(outbuf.at[keep, lanes], out_t.at[:, lanes])

    def place_tables():
        in_tab.wait()
        table = tabs[...].astype(F32)[:TOP]
        ids = lax.broadcasted_iota(jnp.int32, (EXP, LOCAL), 0).astype(F32)
        hit = jnp.zeros((EXP, LOCAL), F32)
        for k in range(TOP):
            hit = hit + jnp.where(table[k : k + 1] == ids, 1.0, 0.0)
        stacked = jnp.concatenate([hit[:, b * TOK : (b + 1) * TOK] for b in range(EXP)], axis=0)
        tri = (
            lax.broadcasted_iota(jnp.int32, (TOK, TOK), 0) < lax.broadcasted_iota(jnp.int32, (TOK, TOK), 1)
        ).astype(F32).astype(BF)
        before = jnp.dot(stacked.astype(BF), tri, preferred_element_type=F32)
        for b in range(EXP):
            part = slice(b * EXP, (b + 1) * EXP)
            code[:, b * TOK : (b + 1) * TOK] = jnp.where(
                stacked[part] > 0.0, before[part] + float(CAP * (b % CHIPS)), -1.0
            )
        slot_row = lax.broadcasted_iota(jnp.int32, (PIECE, LOCAL // 2), 0).astype(F32)
        for h in range(2):
            for e in range(EXP):
                equal = code[e : e + 1, h * (LOCAL // 2) : (h + 1) * (LOCAL // 2)] == slot_row
                onehot[h, e * PIECE : (e + 1) * PIECE] = jnp.where(equal, 1.0, 0.0).astype(BF)

    def weight_grads(start, stop):
        def body(i, _):
            cols = pl.ds(pl.multiple_of(i * TILE, TILE), TILE)
            block = xs[:, cols]
            dims = (((0,), (0,)), ((), ()))
            gbuf[0, cols, :] = lax.dot_general(block, dg_ref[...], dims, preferred_element_type=F32).astype(BF)
            gbuf[1, cols, :] = lax.dot_general(block, du_ref[...], dims, preferred_element_type=F32).astype(BF)
            return 0

        lax.fori_loop(start, stop, body, 0)
        span = pl.ds(start * TILE, (stop - start) * TILE)
        return [copy(gbuf.at[j, span, :], out.at[span, :]) for j, out in enumerate((gg_out, gu_out))]

    partial(2)
    pl.semaphore_wait(barrier, EXP - 1 + 3)
    over_y(2, 0)
    far_b(0)
    partial(1)
    over_y(1, 0)
    direct_up(0)
    partial(NZ - 1)
    over_y(NZ - 1, 0)
    direct_down(0)
    partial(0)
    over_y(0, 0)
    far_a(0)
    combined_b(0)
    far_b(1)
    for dz in (2, 1, NZ - 1, 0):
        over_y(dz, 1)
    near_a(0)
    direct_up(1)
    direct_down(1)
    in_x.wait()
    stores = weight_grads(0, 4)
    fold_b(0)
    far_a(1)
    combined_b(1)
    place_tables()
    near_a(1)
    own0 = finish(0)
    stores += weight_grads(4, D // TILE)
    fold_b(1)
    out0 = combine(0, own0)
    own1 = finish(1)
    out1 = combine(1, own1)
    for c in sent:
        c.wait_send()
    for c in stores + [out0, out1]:
        c.wait()


def return_rows(dg, du, wg, wu, x, table):
    hbm = pl.BlockSpec(memory_space=pl.ANY)
    vmem = pl.BlockSpec(memory_space=pltpu.VMEM)
    rows = DP * SHARD
    return pl.pallas_call(
        return_kernel,
        out_shape=(
            jax.ShapeDtypeStruct((WIDE // 2, LOCAL), BF),
            jax.ShapeDtypeStruct((D, HID), BF),
            jax.ShapeDtypeStruct((D, HID), BF),
        ),
        in_specs=[vmem, vmem, hbm, hbm, hbm, hbm],
        out_specs=(hbm, hbm, hbm),
        scratch_shapes=[
            pltpu.VMEM((rows, D), BF),
            pltpu.VMEM((D, HID), BF),
            pltpu.VMEM((D, HID), BF),
            pltpu.VMEM((rows, D), BF),
            pltpu.VMEM((2, D, HID), BF),
            pltpu.VMEM((2 * TOP, LOCAL), BF),
            pltpu.VMEM((EXP, LOCAL), F32),
            pltpu.VMEM((2, EXP * PIECE, LOCAL // 2), BF),
            pltpu.VMEM((NZ, SHARD, CA), BF),
            pltpu.VMEM((2, SHARD, CA // 2), BF),
            pltpu.VMEM((2, SHARD, CA), BF),
            pltpu.VMEM((2, 2, SHARD, CB // 2), BF),
            pltpu.VMEM((2, 2, SHARD, CB), BF),
            pltpu.VMEM((SHARD, CB), BF),
            pltpu.VMEM((2, EXP * PIECE, PART), BF),
            pltpu.VMEM((PART, LOCAL), BF),
            pltpu.SemaphoreType.DMA((100,)),
            pltpu.SemaphoreType.DMA((100,)),
            pltpu.SemaphoreType.DMA((16,)),
        ],
        compiler_params=pltpu.CompilerParams(
            collective_id=1, has_side_effects=True, vmem_limit_bytes=63 * 1024 * 1024
        ),
        name="return_rows",
    )(dg, du, wg, wu, x, table)


def per_device(attn_rows, out_grad, routes, gates, w_gate, w_up, w_down):
    packed = jnp.concatenate([routes.T.astype(BF), gates.T], axis=0)
    gate_mat, up_mat, down_mat = w_gate[0], w_up[0], w_down[0]
    x, dg, du, table = gather_rows(attn_rows.T, out_grad.T, packed, gate_mat, up_mat, down_mat)
    grad_t, g_gate, g_up = return_rows(dg, du, gate_mat, up_mat, x, table)
    return grad_t.T, g_gate[None], g_up[None]


def solution(mesh):
    return jax.shard_map(
        per_device,
        mesh=mesh,
        in_specs=(
            P("dp", "expert"),
            P("dp", "expert"),
            P(("dp", "expert"), None),
            P(("dp", "expert"), None),
            P("expert", None, "dp"),
            P("expert", None, "dp"),
            P("expert", "dp", None),
        ),
        out_specs=(P("dp", "expert"), P("expert", None, "dp"), P("expert", None, "dp")),
        check_vma=False,
    )
```

```python
import jax
import jax.numpy as jnp
from jax import lax
from jax.experimental import pallas as pl
from jax.experimental.pallas import tpu as pltpu
from jax.sharding import PartitionSpec as P

BF = jnp.bfloat16
F32 = jnp.float32
MESH = pl.DeviceIdType.MESH
NT = (((1,), (1,)), ((), ()))
EXP, DP, NZ, CHIPS = 16, 8, 4, 8
TOK, TOP, CAP = 128, 8, 6
LOCAL = EXP * TOK
WIDE, D, HID = 896, 7168, 256
PIECE = 48
SHARD = 96
STEP = 1024


NA = 2
CA = NA * WIDE
CB = D - CA
LA, RA = slice(0, CA // 2), slice(CA // 2, CA)
ALL_A, ALL_B = slice(0, CA), slice(CA, D)
LB, RB = slice(CA, CA + CB // 2), slice(CA + CB // 2, D)
PART = 512
TILE = 512


def layer_kernel(
    xt_ref, dt_ref, pk_ref, wg_ref, wu_ref, wd_ref,
    out_t, gg_out, gu_out,
    raw, tabs, code, coef, onehot, pay, xall, dall, wg, wu, wd, acc, dg_ref, du_ref,
    spots, places, got_a, relay_a, fin_a, relay_b, fin_b, got_b, back, outbuf, gbuf,
    ssem, rsem, lsem, gsem,
):
    ex = lax.axis_index("expert")
    dp = lax.axis_index("dp")
    core = ex % 2
    chip = ex // 2
    row, z = dp // NZ, dp % NZ

    def at(dy, dz):
        return (row + dy) % 2 * NZ + (z + dz) % NZ

    up, down, side = at(0, 1), at(0, NZ - 1), at(1, 0)
    bufs = (xall, dall)

    barrier = pltpu.get_barrier_semaphore()
    for r in range(1, EXP):
        pl.semaphore_signal(barrier, inc=1, device_id=((ex + r) % EXP, dp), device_id_type=MESH)
    for peer in (up, down, side):
        pl.semaphore_signal(barrier, inc=1, device_id=(ex, peer), device_id_type=MESH)

    local = []

    def copy_in(src, dst):
        c = pltpu.make_async_copy(src, dst, lsem.at[len(local)])
        c.start()
        local.append(c)
        return c

    mine = pl.ds(pl.multiple_of(core * (WIDE // 2), WIDE // 2), WIDE // 2)
    lanes = pl.ds(pl.multiple_of(ex * TOK, TOK), TOK)
    in_tab = copy_in(pk_ref, tabs.at[:, lanes])
    in_raw = [copy_in(ref, raw.at[t, mine, :]) for t, ref in enumerate((xt_ref, dt_ref))]
    in_w = [copy_in(wg_ref, wg), copy_in(wu_ref, wu), copy_in(wd_ref, wd)]

    pl.semaphore_wait(barrier, EXP - 1 + 3)

    sent = {}
    slots = [0]

    def slot():
        slots[0] += 1
        return slots[0] - 1

    def send(k, src, dst, device):
        c = pltpu.make_async_remote_copy(
            src_ref=src, dst_ref=dst, send_sem=ssem.at[k], recv_sem=rsem.at[k],
            device_id=device, device_id_type=MESH,
        )
        c.start()
        sent[k] = c

    def flush(*keys):
        for k in keys:
            sent.pop(k).wait_send()

    def arrive(k, dst):
        pltpu.make_async_remote_copy(
            src_ref=dst, dst_ref=dst, send_sem=ssem.at[k], recv_sem=rsem.at[k],
            device_id=(ex, side), device_id_type=MESH,
        ).wait_recv()

    other = pl.ds(pl.multiple_of((1 - core) * (WIDE // 2), WIDE // 2), WIDE // 2)
    tab_slot = [slot() for _ in range(EXP)]
    for r in range(1, EXP):
        send(tab_slot[r], pk_ref, tabs.at[:, lanes], ((ex + r) % EXP, dp))
    raw_slot = [slot(), slot()]
    sibling = (chip * 2 + 1 - core, dp)
    for t, ref in enumerate((xt_ref, dt_ref)):
        send(raw_slot[t], ref, raw.at[t, mine, :], sibling)

    in_tab.wait()
    for r in range(1, EXP):
        src = (ex + EXP - r) % EXP
        arrive(tab_slot[r], tabs.at[:, pl.ds(pl.multiple_of(src * TOK, TOK), TOK)])

    table = tabs[...].astype(F32)
    route, gate = table[:TOP], table[TOP:]
    ids = (lax.broadcasted_iota(jnp.int32, (CHIPS, LOCAL), 0) * 2 + core).astype(F32)
    hit = jnp.zeros((CHIPS, LOCAL), F32)
    weight = jnp.zeros((CHIPS, LOCAL), F32)
    for k in range(TOP):
        same = route[k : k + 1] == ids
        hit = hit + jnp.where(same, 1.0, 0.0)
        weight = weight + jnp.where(same, gate[k : k + 1], 0.0)
    coef[...] = weight
    stacked = jnp.concatenate([hit[:, b * TOK : (b + 1) * TOK] for b in range(EXP)], axis=0)
    tri = (
        lax.broadcasted_iota(jnp.int32, (TOK, TOK), 0) < lax.broadcasted_iota(jnp.int32, (TOK, TOK), 1)
    ).astype(F32).astype(BF)
    before = jnp.dot(stacked.astype(BF), tri, preferred_element_type=F32)
    for b in range(EXP):
        part = slice(b * CHIPS, (b + 1) * CHIPS)
        code[:, b * TOK : (b + 1) * TOK] = jnp.where(
            stacked[part] > 0.0, before[part] + float(CAP * (b % CHIPS)), -1.0
        )

    slot_row = lax.broadcasted_iota(jnp.int32, (PIECE, LOCAL // 2), 0).astype(F32)
    own_rows = [pl.ds(pl.multiple_of(dp * SHARD + h * PIECE, PIECE), PIECE) for h in range(2)]
    chip_cols = pl.ds(pl.multiple_of(chip * WIDE, WIDE), WIDE)
    a2a_slot = [[[slot() for _ in range(CHIPS)] for _ in range(2)] for _ in range(2)]
    a2a_self = [[None, None], [None, None]]

    def dispatch(t, h):
        half = slice(h * (LOCAL // 2), (h + 1) * (LOCAL // 2))
        for i in range(CHIPS):
            equal = code[i : i + 1, half] == slot_row
            value = 1.0 if t == 0 else coef[i : i + 1, half]
            onehot[i * PIECE : (i + 1) * PIECE] = jnp.where(equal, value, 0.0).astype(BF)
        for n in range(0, WIDE, 128):
            got = lax.dot_general(onehot[...], raw[t, n : n + 128, half], NT, preferred_element_type=F32)
            pay[t, h, :, :, n : n + 128] = got.astype(BF).reshape(CHIPS, PIECE, 128)
        where = bufs[t].at[own_rows[h], chip_cols]
        for r in range(1, CHIPS):
            to = (chip + r) % CHIPS
            send(a2a_slot[t][h][r], pay.at[t, h, to], where, (to * 2 + core, dp))
        a2a_self[t][h] = copy_in(pay.at[t, h, chip], where)

    def complete(t, h):
        a2a_self[t][h].wait()
        for r in range(1, CHIPS):
            src = (chip + CHIPS - r) % CHIPS
            arrive(a2a_slot[t][h][r], bufs[t].at[own_rows[h], pl.ds(pl.multiple_of(src * WIDE, WIDE), WIDE)])

    def rows_of(s):
        return pl.ds(pl.multiple_of(s * SHARD, SHARD), SHARD)

    def contract(s, with_x, with_d):
        rows = rows_of(s)
        if with_x:
            acc[0:2] = jnp.zeros((2, SHARD, HID), F32)
        if with_d:
            acc[2] = jnp.zeros((SHARD, HID), F32)

        def body(k, _):
            cols = pl.ds(pl.multiple_of(k * STEP, STEP), STEP)
            if with_x:
                xs = xall[rows, cols]
                acc[0] += jnp.dot(xs, wg[cols, :], preferred_element_type=F32)
                acc[1] += jnp.dot(xs, wu[cols, :], preferred_element_type=F32)
            if with_d:
                acc[2] += lax.dot_general(dall[rows, cols], wd[:, cols], NT, preferred_element_type=F32)
            return 0

        lax.fori_loop(0, D // STEP, body, 0)

    def activate(s):
        rows = rows_of(s)
        g, u, q = acc[0], acc[1], acc[2]
        sig = jax.nn.sigmoid(g)
        dg_ref[rows, :] = (q * u * sig * (1.0 + g * (1.0 - sig))).astype(BF)
        du_ref[rows, :] = (q * (g * sig)).astype(BF)

    def hidden(s):
        contract(s, True, True)
        activate(s)

    half = D // 2
    left, right, whole = slice(0, half), slice(half, D), slice(0, D)
    low, high = slice(0, half // 2), slice(half // 2, half)

    def piece(t, h, s, cols=whole):
        return bufs[t].at[pl.ds(pl.multiple_of(s * SHARD + h * PIECE, PIECE), PIECE), cols]

    def pass_on(k, to, t, h, s, cols=whole):
        send(k, piece(t, h, s, cols), piece(t, h, s, cols), (ex, to))

    def slots_for(*names):
        return {name: slot() for name in names}

    pieces = ((0, 0), (0, 1), (1, 0), (1, 1))
    to_up, to_down, to_side = slots_for(*pieces), slots_for(*pieces), slots_for(*pieces)

    def spread_z(t, h):
        pass_on(to_up[t, h], up, t, h, dp)
        pass_on(to_down[t, h], down, t, h, dp)

    def spread_y(t, h):
        pass_on(to_side[t, h], side, t, h, dp)

    in_raw[0].wait()
    arrive(raw_slot[0], raw.at[0, other, :])
    dispatch(0, 0)
    dispatch(0, 1)
    complete(0, 0)
    spread_z(0, 0)
    in_raw[1].wait()
    arrive(raw_slot[1], raw.at[1, other, :])
    dispatch(1, 0)
    complete(0, 1)
    spread_z(0, 1)
    dispatch(1, 1)
    spread_y(0, 0)
    spread_y(0, 1)
    complete(1, 0)
    spread_z(1, 0)
    spread_y(1, 0)
    complete(1, 1)
    spread_z(1, 1)
    spread_y(1, 1)
    for c in in_w:
        c.wait()

    far, pdown, pup, pfar = at(0, 2), at(1, NZ - 1), at(1, 1), at(1, 2)
    early = ((0, 0, whole), (0, 1, whole), (1, 0, left))
    via_up, via_down = slots_for(*pieces[:3]), slots_for(*pieces[:3])

    def relay_side(i):
        t, h, cols = early[i]
        arrive(to_side[t, h], piece(t, h, side))
        pass_on(via_up[t, h], up, t, h, side, cols)
        pass_on(via_down[t, h], down, t, h, side, cols)

    relay_side(0)
    hidden(dp)
    relay_side(1)
    for t, h in pieces[:2]:
        arrive(to_up[t, h], piece(t, h, down))
        arrive(to_down[t, h], piece(t, h, up))
    over = slots_for("d", "dr", "u", "ur", "fl", "fr", "f0")
    two = slots_for("d1l", "d1r", "d0l", "d0r", "x0", "x1", "px0", "px1", "pl", "ph")
    arrive(to_up[1, 0], piece(1, 0, down))
    pass_on(over["dr"], side, 1, 0, down, right)
    arrive(to_down[1, 0], piece(1, 0, up))
    pass_on(over["ur"], side, 1, 0, up, right)
    arrive(to_up[1, 1], piece(1, 1, down))
    pass_on(two["d1l"], up, 1, 1, down, left)
    pass_on(over["d"], side, 1, 1, down)
    arrive(to_down[1, 1], piece(1, 1, up))
    pass_on(two["d1r"], down, 1, 1, up, right)
    pass_on(over["u"], side, 1, 1, up)
    pass_on(two["d0l"], up, 1, 0, down, left)
    pass_on(two["d0r"], down, 1, 0, up, right)
    relay_side(2)
    pass_on(two["x0"], up, 0, 0, down)
    pass_on(two["x1"], down, 0, 1, up)
    hidden(down)
    arrive(to_side[1, 1], piece(1, 1, side))
    hidden(side)
    hidden(up)
    arrive(via_up[1, 0], piece(1, 0, pdown, left))
    pass_on(two["pl"], up, 1, 0, pdown, low)
    arrive(via_down[1, 0], piece(1, 0, pup, left))
    pass_on(two["ph"], down, 1, 0, pup, high)
    arrive(via_up[0, 0], piece(0, 0, pdown))
    pass_on(two["px0"], up, 0, 0, pdown)
    arrive(via_down[0, 1], piece(0, 1, pup))
    pass_on(two["px1"], down, 0, 1, pup)
    arrive(two["d0r"], piece(1, 0, far, right))
    pass_on(over["f0"], side, 1, 0, far, right)
    arrive(two["d1l"], piece(1, 1, far, left))
    pass_on(over["fl"], side, 1, 1, far, left)
    arrive(two["d1r"], piece(1, 1, far, right))
    pass_on(over["fr"], side, 1, 1, far, right)
    arrive(via_up[0, 1], piece(0, 1, pdown))
    arrive(over["dr"], piece(1, 0, pdown, right))
    arrive(over["d"], piece(1, 1, pdown))
    hidden(pdown)
    arrive(via_down[0, 0], piece(0, 0, pup))
    arrive(over["ur"], piece(1, 0, pup, right))
    arrive(over["u"], piece(1, 1, pup))
    hidden(pup)
    def part_of(s, h):
        return pl.ds(pl.multiple_of(s * SHARD + h * PIECE, PIECE), PIECE)

    def partial(dz):
        first, second = rows_of(at(0, dz)), rows_of(at(1, dz))
        g2 = jnp.concatenate([dg_ref[first, :], dg_ref[second, :]], axis=0)
        u2 = jnp.concatenate([du_ref[first, :], du_ref[second, :]], axis=0)

        def body(k, _):
            cols = pl.ds(pl.multiple_of(k * WIDE, WIDE), WIDE)
            v = lax.dot_general(g2, wg[cols, :], NT, preferred_element_type=F32)
            v = (v + lax.dot_general(u2, wu[cols, :], NT, preferred_element_type=F32)).astype(BF)
            dall[first, cols] = v[:SHARD]
            dall[second, cols] = v[SHARD:]
            return 0

        lax.fori_loop(0, D // WIDE, body, 0)

    def add(s, h, cols, *others):
        def body(i, _):
            here = pl.ds(pl.multiple_of(s * SHARD + h * PIECE + i * 16, 16), 16)
            total = dall[here, cols].astype(F32)
            for other in others:
                total = total + other(pl.ds(pl.multiple_of(h * PIECE + i * 16, 16), 16)).astype(F32)
            dall[here, cols] = total.astype(BF)
            return 0

        lax.fori_loop(0, PIECE // 16, body, 0)

    rows48 = [slice(h * PIECE, (h + 1) * PIECE) for h in range(2)]
    s_ya = {(h, dz): slot() for h in range(2) for dz in range(NZ)}
    s_relay_b = {(h, y, d): slot() for h in range(2) for y in range(2) for d in range(2)}
    s_fin_l = {(h, y, d): slot() for h in range(2) for y in range(2) for d in range(2)}
    s_fin_r = {(h, y, d): slot() for h in range(2) for y in range(2) for d in range(2)}
    s_relay_a = {(h, d): slot() for h in range(2) for d in range(2)}
    s_fin_a = {(h, d): slot() for h in range(2) for d in range(2)}
    s_yb = [slot(), slot()]
    s_back = [[slot() for _ in range(EXP)] for _ in range(2)]
    rel_l, rel_r = slice(0, CB // 2), slice(CB // 2, CB)

    def over_y(dz, h):
        send(s_ya[h, dz], dall.at[part_of(at(1, dz), h), ALL_A], got_a.at[dz, rows48[h], :], (ex, side))

    def line(j, dz):
        return at(1 - j, dz)

    def far_b(h):
        for y in range(2):
            src = part_of(line(y, 2), h)
            send(s_relay_b[h, y, 0], dall.at[src, LB], relay_b.at[0, y, rows48[h], :], (ex, up))
            send(s_relay_b[h, y, 1], dall.at[src, RB], relay_b.at[1, y, rows48[h], :], (ex, down))

    def direct_up(h):
        for y in range(2):
            send(s_fin_r[h, y, 0], dall.at[part_of(line(y, 1), h), RB], fin_b.at[0, y, rows48[h], rel_r], (ex, up))

    def direct_down(h):
        for y in range(2):
            send(s_fin_l[h, y, 1], dall.at[part_of(line(y, NZ - 1), h), LB], fin_b.at[1, y, rows48[h], rel_l], (ex, down))

    def combined_b(h):
        for y in range(2):
            arrive(s_relay_b[h, y, 0], relay_b.at[0, y, rows48[h], :])
            add(line(y, 1), h, LB, lambda r, y=y: relay_b[0, y, r, :])
            send(s_fin_l[h, y, 0], dall.at[part_of(line(y, 1), h), LB], fin_b.at[0, y, rows48[h], rel_l], (ex, up))
            arrive(s_relay_b[h, y, 1], relay_b.at[1, y, rows48[h], :])
            add(line(y, NZ - 1), h, RB, lambda r, y=y: relay_b[1, y, r, :])
            send(s_fin_r[h, y, 1], dall.at[part_of(line(y, NZ - 1), h), RB], fin_b.at[1, y, rows48[h], rel_r], (ex, down))

    def far_a(h):
        arrive(s_ya[h, 2], got_a.at[2, rows48[h], :])
        add(at(0, 2), h, ALL_A, lambda r: got_a[2, r, :])
        src = part_of(at(0, 2), h)
        send(s_relay_a[h, 0], dall.at[src, LA], relay_a.at[0, rows48[h], :], (ex, up))
        send(s_relay_a[h, 1], dall.at[src, RA], relay_a.at[1, rows48[h], :], (ex, down))

    def near_a(h):
        for d, dz, peer, mixed in ((0, 1, up, LA), (1, NZ - 1, down, RA)):
            plain = RA if d == 0 else LA
            arrive(s_ya[h, dz], got_a.at[dz, rows48[h], :])
            add(at(0, dz), h, plain, lambda r, dz=dz: got_a[dz, r, plain])
            arrive(s_relay_a[h, d], relay_a.at[d, rows48[h], :])
            add(at(0, dz), h, mixed, lambda r, dz=dz: got_a[dz, r, mixed], lambda r, d=d: relay_a[d, r, :])
            send(s_fin_a[h, d], dall.at[part_of(at(0, dz), h), ALL_A], fin_a.at[d, rows48[h], :], (ex, peer))

    def wait_b(h, j):
        for d in range(2):
            arrive(s_fin_l[h, j, d], fin_b.at[d, j, rows48[h], rel_l])
            arrive(s_fin_r[h, j, d], fin_b.at[d, j, rows48[h], rel_r])

    def fold_b(h):
        wait_b(h, 0)
        add(side, h, ALL_B, lambda r: fin_b[0, 0, r, :], lambda r: fin_b[1, 0, r, :])
        send(s_yb[h], dall.at[part_of(side, h), ALL_B], got_b.at[rows48[h], :], (ex, side))

    def finish(h):
        arrive(s_ya[h, 0], got_a.at[0, rows48[h], :])
        for d in range(2):
            arrive(s_fin_a[h, d], fin_a.at[d, rows48[h], :])
        add(dp, h, ALL_A, lambda r: got_a[0, r, :], lambda r: fin_a[0, r, :], lambda r: fin_a[1, r, :])
        wait_b(h, 1)
        arrive(s_yb[h], got_b.at[rows48[h], :])
        add(
            dp, h, ALL_B,
            lambda r: fin_b[0, 1, r, :], lambda r: fin_b[1, 1, r, :], lambda r: got_b[r, :],
        )
        where = pl.ds(pl.multiple_of(ex * PIECE, PIECE), PIECE)

        def cols(e):
            return pl.ds(pl.multiple_of(e // 2 * WIDE + e % 2 * 384, 128), PART)

        for r in range(1, EXP):
            to = (ex + r) % EXP
            send(s_back[h][r], dall.at[part_of(dp, h), cols(to)], back.at[h, where, :], (to, dp))
        return copy_in(dall.at[part_of(dp, h), cols(ex)], back.at[h, where, :])

    def combine(h, own):
        own.wait()
        for r in range(1, EXP):
            src = (ex + EXP - r) % EXP
            arrive(s_back[h][r], back.at[h, pl.ds(pl.multiple_of(src * PIECE, PIECE), PIECE), :])
        for n in range(0, LOCAL // 2, 256):
            got = lax.dot_general(
                back[h], places[h, :, n : n + 256], (((0,), (0,)), ((), ())), preferred_element_type=F32
            )
            outbuf[:, h * (LOCAL // 2) + n : h * (LOCAL // 2) + n + 256] = got.astype(BF)
        lanes = slice(h * (LOCAL // 2), (h + 1) * (LOCAL // 2))
        keep = pl.ds(pl.multiple_of(core * 64, 64), WIDE // 2)
        return copy_in(outbuf.at[keep, lanes], out_t.at[:, lanes])

    def place_tables():
        table = tabs[...].astype(F32)[:TOP]
        ids = lax.broadcasted_iota(jnp.int32, (EXP, LOCAL), 0).astype(F32)
        hit = jnp.zeros((EXP, LOCAL), F32)
        for k in range(TOP):
            hit = hit + jnp.where(table[k : k + 1] == ids, 1.0, 0.0)
        stacked = jnp.concatenate([hit[:, b * TOK : (b + 1) * TOK] for b in range(EXP)], axis=0)
        tri = (
            lax.broadcasted_iota(jnp.int32, (TOK, TOK), 0) < lax.broadcasted_iota(jnp.int32, (TOK, TOK), 1)
        ).astype(F32).astype(BF)
        before = jnp.dot(stacked.astype(BF), tri, preferred_element_type=F32)
        for b in range(EXP):
            part = slice(b * EXP, (b + 1) * EXP)
            spots[:, b * TOK : (b + 1) * TOK] = jnp.where(
                stacked[part] > 0.0, before[part] + float(CAP * (b % CHIPS)), -1.0
            )
        slot_row = lax.broadcasted_iota(jnp.int32, (PIECE, LOCAL // 2), 0).astype(F32)
        for h in range(2):
            for e in range(EXP):
                equal = spots[e : e + 1, h * (LOCAL // 2) : (h + 1) * (LOCAL // 2)] == slot_row
                places[h, e * PIECE : (e + 1) * PIECE] = jnp.where(equal, 1.0, 0.0).astype(BF)

    def grad_copy(j, i):
        cols = pl.ds(pl.multiple_of(i * TILE, TILE), TILE)
        out = gg_out if j == 0 else gu_out
        return pltpu.make_async_copy(gbuf.at[j, i % 2], out.at[cols, :], gsem.at[j, i % 2])

    def weight_grads(start, stop):
        def body(i, _):
            cols = pl.ds(pl.multiple_of(i * TILE, TILE), TILE)
            block = xall[:, cols]
            dims = (((0,), (0,)), ((), ()))
            for j, grad in enumerate((dg_ref, du_ref)):
                @pl.when(i >= 2)
                def _():
                    grad_copy(j, i - 2).wait()

                gbuf[j, i % 2] = lax.dot_general(
                    block, grad[...], dims, preferred_element_type=F32
                ).astype(BF)
                grad_copy(j, i).start()
            return 0

        lax.fori_loop(start, stop, body, 0)

    place_tables()
    flush(*(k[q] for k in (to_up, to_down, to_side) for q in pieces[2:]))
    flush(via_up[1, 0], via_down[1, 0])
    partial(0)
    flush(two["d1r"], two["d0r"], over["u"], over["ur"], two["ph"])
    partial(1)
    direct_up(0)
    flush(two["d1l"], two["d0l"], over["d"], over["dr"], two["pl"])
    partial(NZ - 1)
    direct_down(0)
    arrive(two["d0l"], piece(1, 0, far, left))
    arrive(two["x0"], piece(0, 0, far))
    arrive(two["x1"], piece(0, 1, far))
    hidden(far)
    arrive(two["px0"], piece(0, 0, pfar))
    arrive(two["px1"], piece(0, 1, pfar))
    contract(pfar, True, False)
    arrive(two["pl"], piece(1, 0, pfar, low))
    arrive(two["ph"], piece(1, 0, pfar, high))
    arrive(over["f0"], piece(1, 0, pfar, right))
    arrive(over["fl"], piece(1, 1, pfar, left))
    arrive(over["fr"], piece(1, 1, pfar, right))
    contract(pfar, False, True)
    activate(pfar)
    flush(over["f0"], over["fl"], over["fr"])
    partial(2)
    over_y(2, 0)
    far_b(0)
    for dz in (1, NZ - 1, 0):
        over_y(dz, 0)
    direct_up(1)
    direct_down(1)
    far_a(0)
    far_b(1)
    for dz in (2, 1, NZ - 1, 0):
        over_y(dz, 1)
    combined_b(0)
    near_a(0)
    weight_grads(0, 4)
    far_a(1)
    fold_b(0)
    combined_b(1)
    near_a(1)
    own0 = finish(0)
    weight_grads(4, D // TILE)
    fold_b(1)
    out0 = combine(0, own0)
    own1 = finish(1)
    out1 = combine(1, own1)
    flush(*list(sent))
    for c in (out0, out1):
        c.wait()
    for j in range(2):
        for i in (D // TILE - 2, D // TILE - 1):
            grad_copy(j, i).wait()


def layer(xt, dt, packed, wg, wu, wd):
    hbm = pl.BlockSpec(memory_space=pl.ANY)
    rows = DP * SHARD
    return pl.pallas_call(
        layer_kernel,
        out_shape=(
            jax.ShapeDtypeStruct((WIDE // 2, LOCAL), BF),
            jax.ShapeDtypeStruct((D, HID), BF),
            jax.ShapeDtypeStruct((D, HID), BF),
        ),
        in_specs=[hbm] * 6,
        out_specs=(hbm, hbm, hbm),
        scratch_shapes=[
            pltpu.VMEM((2, WIDE, LOCAL), BF),
            pltpu.VMEM((2 * TOP, LOCAL), BF),
            pltpu.VMEM((CHIPS, LOCAL), F32),
            pltpu.VMEM((CHIPS, LOCAL), F32),
            pltpu.VMEM((CHIPS * PIECE, LOCAL // 2), BF),
            pltpu.VMEM((2, 2, CHIPS, PIECE, WIDE), BF),
            pltpu.VMEM((rows, D), BF),
            pltpu.VMEM((rows, D), BF),
            pltpu.VMEM((D, HID), BF),
            pltpu.VMEM((D, HID), BF),
            pltpu.VMEM((HID, D), BF),
            pltpu.VMEM((3, SHARD, HID), F32),
            pltpu.VMEM((rows, HID), BF),
            pltpu.VMEM((rows, HID), BF),
            pltpu.VMEM((EXP, LOCAL), F32),
            pltpu.VMEM((2, EXP * PIECE, LOCAL // 2), BF),
            pltpu.VMEM((NZ, SHARD, CA), BF),
            pltpu.VMEM((2, SHARD, CA // 2), BF),
            pltpu.VMEM((2, SHARD, CA), BF),
            pltpu.VMEM((2, 2, SHARD, CB // 2), BF),
            pltpu.VMEM((2, 2, SHARD, CB), BF),
            pltpu.VMEM((SHARD, CB), BF),
            pltpu.VMEM((2, EXP * PIECE, PART), BF),
            pltpu.VMEM((PART, LOCAL), BF),
            pltpu.VMEM((2, 2, TILE, HID), BF),
            pltpu.SemaphoreType.DMA((176,)),
            pltpu.SemaphoreType.DMA((176,)),
            pltpu.SemaphoreType.DMA((24,)),
            pltpu.SemaphoreType.DMA((2, 2)),
        ],
        compiler_params=pltpu.CompilerParams(
            collective_id=0, has_side_effects=True, vmem_limit_bytes=67_000_000
        ),
        name="layer",
    )(xt, dt, packed, wg, wu, wd)


def per_device(attn_rows, out_grad, routes, gates, w_gate, w_up, w_down):
    packed = jnp.concatenate([routes.T.astype(BF), gates.T], axis=0)
    grad_t, g_gate, g_up = layer(attn_rows.T, out_grad.T, packed, w_gate[0], w_up[0], w_down[0])
    return grad_t.T, g_gate[None], g_up[None]


def solution(mesh):
    return jax.shard_map(
        per_device,
        mesh=mesh,
        in_specs=(
            P("dp", "expert"),
            P("dp", "expert"),
            P(("dp", "expert"), None),
            P(("dp", "expert"), None),
            P("expert", None, "dp"),
            P("expert", None, "dp"),
            P("expert", "dp", None),
        ),
        out_specs=(P("dp", "expert"), P("expert", None, "dp"), P("expert", None, "dp")),
        check_vma=False,
    )
```

```python
import jax
import jax.numpy as jnp
from jax import lax
from jax.experimental import pallas as pl
from jax.experimental.pallas import tpu as pltpu
from jax.sharding import PartitionSpec as P

BF = jnp.bfloat16
F32 = jnp.float32
MESH = pl.DeviceIdType.MESH
NT = (((1,), (1,)), ((), ()))
EXP, DP, NZ, CHIPS = 16, 8, 4, 8
TOK, TOP, CAP = 128, 8, 6
LOCAL = EXP * TOK
WIDE, D, HID = 896, 7168, 256
PIECE = 48
SHARD = 96
STEP = 1024


NA = 2
CA = NA * WIDE
CB = D - CA
LA, RA = slice(0, CA // 2), slice(CA // 2, CA)
ALL_A, ALL_B = slice(0, CA), slice(CA, D)
LB, RB = slice(CA, CA + CB // 2), slice(CA + CB // 2, D)
PART = 512
TILE = 512


def combine(back, places, out, width=256):
    for n in range(0, LOCAL // 2, width):
        got = lax.dot_general(
            back[...], places[:, n : n + width], (((0,), (0,)), ((), ())), preferred_element_type=F32
        )
        out[:, n : n + width] = got.astype(BF)


def layer_kernel(
    xt_ref, dt_ref, rt_ref, gt_ref, wg_ref, wu_ref, wd_ref,
    first_out, back_out, place_out, gg_out, gu_out,
    raw, tab_r, tab_g, code, coef, onehot, pay, xall, dall, wg, wu, wd, acc, dg_ref, du_ref,
    spots, places, got_a, relay_a, fin_a, relay_b, fin_b, got_b, back, outbuf, gbuf,
    ssem, rsem, lsem, gsem,
):
    ex = lax.axis_index("expert")
    dp = lax.axis_index("dp")
    core = ex % 2
    chip = ex // 2
    row, z = dp // NZ, dp % NZ

    def at(dy, dz):
        return (row + dy) % 2 * NZ + (z + dz) % NZ

    up, down, side = at(0, 1), at(0, NZ - 1), at(1, 0)
    bufs = (xall, dall)

    barrier = pltpu.get_barrier_semaphore()
    for r in range(1, EXP):
        pl.semaphore_signal(barrier, inc=1, device_id=((ex + r) % EXP, dp), device_id_type=MESH)
    for peer in (up, down, side):
        pl.semaphore_signal(barrier, inc=1, device_id=(ex, peer), device_id_type=MESH)

    local = []

    def copy_in(src, dst):
        c = pltpu.make_async_copy(src, dst, lsem.at[len(local)])
        c.start()
        local.append(c)
        return c

    mine = pl.ds(pl.multiple_of(core * (WIDE // 2), WIDE // 2), WIDE // 2)
    lanes = pl.ds(pl.multiple_of(ex * TOK, TOK), TOK)
    in_tab = [copy_in(rt_ref, tab_r.at[:, lanes]), copy_in(gt_ref, tab_g.at[:, lanes])]
    in_raw = [copy_in(ref, raw.at[t, mine, :]) for t, ref in enumerate((xt_ref, dt_ref))]
    in_w = [copy_in(wg_ref, wg), copy_in(wu_ref, wu), copy_in(wd_ref, wd)]

    pl.semaphore_wait(barrier, EXP - 1 + 3)

    sent = {}
    slots = [0]

    def slot():
        slots[0] += 1
        return slots[0] - 1

    def send(k, src, dst, device):
        c = pltpu.make_async_remote_copy(
            src_ref=src, dst_ref=dst, send_sem=ssem.at[k], recv_sem=rsem.at[k],
            device_id=device, device_id_type=MESH,
        )
        c.start()
        sent[k] = c

    def flush(*keys):
        for k in keys:
            sent.pop(k).wait_send()

    def arrive(k, dst):
        pltpu.make_async_remote_copy(
            src_ref=dst, dst_ref=dst, send_sem=ssem.at[k], recv_sem=rsem.at[k],
            device_id=(ex, side), device_id_type=MESH,
        ).wait_recv()

    other = pl.ds(pl.multiple_of((1 - core) * (WIDE // 2), WIDE // 2), WIDE // 2)
    tab_slot = [(slot(), slot()) for _ in range(EXP)]
    for r in range(1, EXP):
        send(tab_slot[r][0], rt_ref, tab_r.at[:, lanes], ((ex + r) % EXP, dp))
        send(tab_slot[r][1], gt_ref, tab_g.at[:, lanes], ((ex + r) % EXP, dp))
    raw_slot = [slot(), slot()]
    sibling = (chip * 2 + 1 - core, dp)
    for t, ref in enumerate((xt_ref, dt_ref)):
        send(raw_slot[t], ref, raw.at[t, mine, :], sibling)

    for c in in_tab:
        c.wait()
    for r in range(1, EXP):
        theirs = pl.ds(pl.multiple_of((ex + EXP - r) % EXP * TOK, TOK), TOK)
        arrive(tab_slot[r][0], tab_r.at[:, theirs])
        arrive(tab_slot[r][1], tab_g.at[:, theirs])

    route, gate = tab_r[...].astype(F32), tab_g[...].astype(F32)
    ids = (lax.broadcasted_iota(jnp.int32, (CHIPS, LOCAL), 0) * 2 + core).astype(F32)
    hit = jnp.zeros((CHIPS, LOCAL), F32)
    weight = jnp.zeros((CHIPS, LOCAL), F32)
    for k in range(TOP):
        same = route[k : k + 1] == ids
        hit = hit + jnp.where(same, 1.0, 0.0)
        weight = weight + jnp.where(same, gate[k : k + 1], 0.0)
    coef[...] = weight
    stacked = jnp.concatenate([hit[:, b * TOK : (b + 1) * TOK] for b in range(EXP)], axis=0)
    tri = (
        lax.broadcasted_iota(jnp.int32, (TOK, TOK), 0) < lax.broadcasted_iota(jnp.int32, (TOK, TOK), 1)
    ).astype(F32).astype(BF)
    before = jnp.dot(stacked.astype(BF), tri, preferred_element_type=F32)
    for b in range(EXP):
        part = slice(b * CHIPS, (b + 1) * CHIPS)
        code[:, b * TOK : (b + 1) * TOK] = jnp.where(
            stacked[part] > 0.0, before[part] + float(CAP * (b % CHIPS)), -1.0
        )

    slot_row = lax.broadcasted_iota(jnp.int32, (PIECE, LOCAL // 2), 0).astype(F32)
    own_rows = [pl.ds(pl.multiple_of(dp * SHARD + h * PIECE, PIECE), PIECE) for h in range(2)]
    chip_cols = pl.ds(pl.multiple_of(chip * WIDE, WIDE), WIDE)
    a2a_slot = [[[slot() for _ in range(CHIPS)] for _ in range(2)] for _ in range(2)]
    a2a_self = [[None, None], [None, None]]

    def dispatch(t, h):
        half = slice(h * (LOCAL // 2), (h + 1) * (LOCAL // 2))
        for i in range(CHIPS):
            equal = code[i : i + 1, half] == slot_row
            value = 1.0 if t == 0 else coef[i : i + 1, half]
            onehot[i * PIECE : (i + 1) * PIECE] = jnp.where(equal, value, 0.0).astype(BF)
        for n in range(0, WIDE, 128):
            got = lax.dot_general(onehot[...], raw[t, n : n + 128, half], NT, preferred_element_type=F32)
            pay[t, h, :, :, n : n + 128] = got.astype(BF).reshape(CHIPS, PIECE, 128)
        where = bufs[t].at[own_rows[h], chip_cols]
        for r in range(1, CHIPS):
            to = (chip + r) % CHIPS
            send(a2a_slot[t][h][r], pay.at[t, h, to], where, (to * 2 + core, dp))
        a2a_self[t][h] = copy_in(pay.at[t, h, chip], where)

    def complete(t, h):
        a2a_self[t][h].wait()
        for r in range(1, CHIPS):
            src = (chip + CHIPS - r) % CHIPS
            arrive(a2a_slot[t][h][r], bufs[t].at[own_rows[h], pl.ds(pl.multiple_of(src * WIDE, WIDE), WIDE)])

    def rows_of(s):
        return pl.ds(pl.multiple_of(s * SHARD, SHARD), SHARD)

    def contract(s, with_x, with_d):
        rows = rows_of(s)
        if with_x:
            acc[0:2] = jnp.zeros((2, SHARD, HID), F32)
        if with_d:
            acc[2] = jnp.zeros((SHARD, HID), F32)

        def body(k, _):
            cols = pl.ds(pl.multiple_of(k * STEP, STEP), STEP)
            if with_x:
                xs = xall[rows, cols]
                acc[0] += jnp.dot(xs, wg[cols, :], preferred_element_type=F32)
                acc[1] += jnp.dot(xs, wu[cols, :], preferred_element_type=F32)
            if with_d:
                acc[2] += lax.dot_general(dall[rows, cols], wd[:, cols], NT, preferred_element_type=F32)
            return 0

        lax.fori_loop(0, D // STEP, body, 0)

    def activate(s):
        rows = rows_of(s)
        g, u, q = acc[0], acc[1], acc[2]
        sig = jax.nn.sigmoid(g)
        dg_ref[rows, :] = (q * u * sig * (1.0 + g * (1.0 - sig))).astype(BF)
        du_ref[rows, :] = (q * (g * sig)).astype(BF)

    def hidden(s):
        contract(s, True, True)
        activate(s)

    half = D // 2
    left, right, whole = slice(0, half), slice(half, D), slice(0, D)
    low, high = slice(0, half // 2), slice(half // 2, half)

    def piece(t, h, s, cols=whole):
        return bufs[t].at[pl.ds(pl.multiple_of(s * SHARD + h * PIECE, PIECE), PIECE), cols]

    def pass_on(k, to, t, h, s, cols=whole):
        send(k, piece(t, h, s, cols), piece(t, h, s, cols), (ex, to))

    def slots_for(*names):
        return {name: slot() for name in names}

    pieces = ((0, 0), (0, 1), (1, 0), (1, 1))
    to_up, to_down, to_side = slots_for(*pieces), slots_for(*pieces), slots_for(*pieces)

    def spread_z(t, h):
        pass_on(to_up[t, h], up, t, h, dp)
        pass_on(to_down[t, h], down, t, h, dp)

    first_up, first_down = [slot() for _ in range(CHIPS)], [slot() for _ in range(CHIPS)]
    order = (0, 2, 6, 1, 7, 3, 5, 4)

    def chunk(r, s):
        src = (chip + CHIPS - r) % CHIPS
        rows = pl.ds(pl.multiple_of(s * SHARD, SHARD), PIECE)
        return xall.at[rows, pl.ds(pl.multiple_of(src * WIDE, WIDE), WIDE)]

    def spread_first(some):
        for r in some:
            if r == 0:
                a2a_self[0][0].wait()
            else:
                arrive(a2a_slot[0][0][r], chunk(r, dp))
            send(first_up[r], chunk(r, dp), chunk(r, dp), (ex, up))
            send(first_down[r], chunk(r, dp), chunk(r, dp), (ex, down))

    def spread_y(t, h):
        pass_on(to_side[t, h], side, t, h, dp)

    in_raw[0].wait()
    arrive(raw_slot[0], raw.at[0, other, :])
    dispatch(0, 0)
    spread_first(order[:1])
    dispatch(0, 1)
    spread_first(order[1:])
    in_raw[1].wait()
    arrive(raw_slot[1], raw.at[1, other, :])
    dispatch(1, 0)
    complete(0, 1)
    spread_z(0, 1)
    dispatch(1, 1)
    spread_y(0, 0)
    spread_y(0, 1)
    complete(1, 0)
    spread_z(1, 0)
    spread_y(1, 0)
    complete(1, 1)
    spread_z(1, 1)
    spread_y(1, 1)
    for c in in_w:
        c.wait()

    far, pdown, pup, pfar = at(0, 2), at(1, NZ - 1), at(1, 1), at(1, 2)
    early = ((0, 0, whole), (0, 1, whole), (1, 0, left))
    via_up, via_down = slots_for(*pieces[:3]), slots_for(*pieces[:3])

    def relay_side(i):
        t, h, cols = early[i]
        arrive(to_side[t, h], piece(t, h, side))
        pass_on(via_up[t, h], up, t, h, side, cols)
        pass_on(via_down[t, h], down, t, h, side, cols)

    relay_side(0)
    hidden(dp)
    relay_side(1)
    for r in order:
        arrive(first_up[r], chunk(r, down))
        arrive(first_down[r], chunk(r, up))
    arrive(to_up[0, 1], piece(0, 1, down))
    arrive(to_down[0, 1], piece(0, 1, up))
    over = slots_for("d", "dr", "u", "ur", "fl", "fr", "f0")
    two = slots_for("d1l", "d1r", "d0l", "d0r", "x0", "x1", "px0", "px1", "pl", "ph")
    arrive(to_up[1, 0], piece(1, 0, down))
    pass_on(over["dr"], side, 1, 0, down, right)
    arrive(to_down[1, 0], piece(1, 0, up))
    pass_on(over["ur"], side, 1, 0, up, right)
    arrive(to_up[1, 1], piece(1, 1, down))
    pass_on(two["d1l"], up, 1, 1, down, left)
    pass_on(over["d"], side, 1, 1, down)
    arrive(to_down[1, 1], piece(1, 1, up))
    pass_on(two["d1r"], down, 1, 1, up, right)
    pass_on(over["u"], side, 1, 1, up)
    pass_on(two["d0l"], up, 1, 0, down, left)
    pass_on(two["d0r"], down, 1, 0, up, right)
    relay_side(2)
    pass_on(two["x0"], up, 0, 0, down)
    pass_on(two["x1"], down, 0, 1, up)
    hidden(down)
    arrive(to_side[1, 1], piece(1, 1, side))
    hidden(side)
    hidden(up)
    arrive(via_up[1, 0], piece(1, 0, pdown, left))
    pass_on(two["pl"], up, 1, 0, pdown, low)
    arrive(via_down[1, 0], piece(1, 0, pup, left))
    pass_on(two["ph"], down, 1, 0, pup, high)
    arrive(via_up[0, 0], piece(0, 0, pdown))
    pass_on(two["px0"], up, 0, 0, pdown)
    arrive(via_down[0, 1], piece(0, 1, pup))
    pass_on(two["px1"], down, 0, 1, pup)
    arrive(two["d0r"], piece(1, 0, far, right))
    pass_on(over["f0"], side, 1, 0, far, right)
    arrive(two["d1l"], piece(1, 1, far, left))
    pass_on(over["fl"], side, 1, 1, far, left)
    arrive(two["d1r"], piece(1, 1, far, right))
    pass_on(over["fr"], side, 1, 1, far, right)
    arrive(via_up[0, 1], piece(0, 1, pdown))
    arrive(over["dr"], piece(1, 0, pdown, right))
    arrive(over["d"], piece(1, 1, pdown))
    hidden(pdown)
    arrive(via_down[0, 0], piece(0, 0, pup))
    arrive(over["ur"], piece(1, 0, pup, right))
    arrive(over["u"], piece(1, 1, pup))
    hidden(pup)
    def part_of(s, h):
        return pl.ds(pl.multiple_of(s * SHARD + h * PIECE, PIECE), PIECE)

    def partial(dz):
        first, second = rows_of(at(0, dz)), rows_of(at(1, dz))
        g2 = jnp.concatenate([dg_ref[first, :], dg_ref[second, :]], axis=0)
        u2 = jnp.concatenate([du_ref[first, :], du_ref[second, :]], axis=0)

        def body(k, _):
            cols = pl.ds(pl.multiple_of(k * WIDE, WIDE), WIDE)
            v = lax.dot_general(g2, wg[cols, :], NT, preferred_element_type=F32)
            v = (v + lax.dot_general(u2, wu[cols, :], NT, preferred_element_type=F32)).astype(BF)
            dall[first, cols] = v[:SHARD]
            dall[second, cols] = v[SHARD:]
            return 0

        lax.fori_loop(0, D // WIDE, body, 0)

    def add(s, h, cols, *others):
        def body(i, _):
            here = pl.ds(pl.multiple_of(s * SHARD + h * PIECE + i * 16, 16), 16)
            total = dall[here, cols].astype(F32)
            for other in others:
                total = total + other(pl.ds(pl.multiple_of(h * PIECE + i * 16, 16), 16)).astype(F32)
            dall[here, cols] = total.astype(BF)
            return 0

        lax.fori_loop(0, PIECE // 16, body, 0)

    rows48 = [slice(h * PIECE, (h + 1) * PIECE) for h in range(2)]
    s_ya = {(h, dz): slot() for h in range(2) for dz in range(NZ)}
    s_relay_b = {(h, y, d): slot() for h in range(2) for y in range(2) for d in range(2)}
    s_fin_l = {(h, y, d): slot() for h in range(2) for y in range(2) for d in range(2)}
    s_fin_r = {(h, y, d): slot() for h in range(2) for y in range(2) for d in range(2)}
    s_relay_a = {(h, d): slot() for h in range(2) for d in range(2)}
    s_fin_a = {(h, d): slot() for h in range(2) for d in range(2)}
    s_yb = [slot(), slot()]
    s_back = [[slot() for _ in range(EXP)] for _ in range(2)]
    rel_l, rel_r = slice(0, CB // 2), slice(CB // 2, CB)

    def over_y(dz, h):
        send(s_ya[h, dz], dall.at[part_of(at(1, dz), h), ALL_A], got_a.at[dz, rows48[h], :], (ex, side))

    def line(j, dz):
        return at(1 - j, dz)

    def far_b(h):
        for y in range(2):
            src = part_of(line(y, 2), h)
            send(s_relay_b[h, y, 0], dall.at[src, LB], relay_b.at[0, y, rows48[h], :], (ex, up))
            send(s_relay_b[h, y, 1], dall.at[src, RB], relay_b.at[1, y, rows48[h], :], (ex, down))

    def direct_up(h):
        for y in range(2):
            send(s_fin_r[h, y, 0], dall.at[part_of(line(y, 1), h), RB], fin_b.at[0, y, rows48[h], rel_r], (ex, up))

    def direct_down(h):
        for y in range(2):
            send(s_fin_l[h, y, 1], dall.at[part_of(line(y, NZ - 1), h), LB], fin_b.at[1, y, rows48[h], rel_l], (ex, down))

    def combined_b(h):
        for y in range(2):
            arrive(s_relay_b[h, y, 0], relay_b.at[0, y, rows48[h], :])
            add(line(y, 1), h, LB, lambda r, y=y: relay_b[0, y, r, :])
            send(s_fin_l[h, y, 0], dall.at[part_of(line(y, 1), h), LB], fin_b.at[0, y, rows48[h], rel_l], (ex, up))
            arrive(s_relay_b[h, y, 1], relay_b.at[1, y, rows48[h], :])
            add(line(y, NZ - 1), h, RB, lambda r, y=y: relay_b[1, y, r, :])
            send(s_fin_r[h, y, 1], dall.at[part_of(line(y, NZ - 1), h), RB], fin_b.at[1, y, rows48[h], rel_r], (ex, down))

    def far_a(h):
        arrive(s_ya[h, 2], got_a.at[2, rows48[h], :])
        add(at(0, 2), h, ALL_A, lambda r: got_a[2, r, :])
        src = part_of(at(0, 2), h)
        send(s_relay_a[h, 0], dall.at[src, LA], relay_a.at[0, rows48[h], :], (ex, up))
        send(s_relay_a[h, 1], dall.at[src, RA], relay_a.at[1, rows48[h], :], (ex, down))

    def near_a(h):
        for d, dz, peer, mixed in ((0, 1, up, LA), (1, NZ - 1, down, RA)):
            plain = RA if d == 0 else LA
            arrive(s_ya[h, dz], got_a.at[dz, rows48[h], :])
            add(at(0, dz), h, plain, lambda r, dz=dz: got_a[dz, r, plain])
            arrive(s_relay_a[h, d], relay_a.at[d, rows48[h], :])
            add(at(0, dz), h, mixed, lambda r, dz=dz: got_a[dz, r, mixed], lambda r, d=d: relay_a[d, r, :])
            send(s_fin_a[h, d], dall.at[part_of(at(0, dz), h), ALL_A], fin_a.at[d, rows48[h], :], (ex, peer))

    def wait_b(h, j):
        for d in range(2):
            arrive(s_fin_l[h, j, d], fin_b.at[d, j, rows48[h], rel_l])
            arrive(s_fin_r[h, j, d], fin_b.at[d, j, rows48[h], rel_r])

    def fold_b(h):
        wait_b(h, 0)
        add(side, h, ALL_B, lambda r: fin_b[0, 0, r, :], lambda r: fin_b[1, 0, r, :])
        send(s_yb[h], dall.at[part_of(side, h), ALL_B], got_b.at[rows48[h], :], (ex, side))

    backs = (back, back_out)

    def finish(h):
        arrive(s_ya[h, 0], got_a.at[0, rows48[h], :])
        for d in range(2):
            arrive(s_fin_a[h, d], fin_a.at[d, rows48[h], :])
        add(dp, h, ALL_A, lambda r: got_a[0, r, :], lambda r: fin_a[0, r, :], lambda r: fin_a[1, r, :])
        wait_b(h, 1)
        arrive(s_yb[h], got_b.at[rows48[h], :])
        add(
            dp, h, ALL_B,
            lambda r: fin_b[0, 1, r, :], lambda r: fin_b[1, 1, r, :], lambda r: got_b[r, :],
        )
        where = pl.ds(pl.multiple_of(ex * PIECE, PIECE), PIECE)

        def cols(e):
            return pl.ds(pl.multiple_of(e // 2 * WIDE + e % 2 * 384, 128), PART)

        for r in range(1, EXP):
            to = (ex + r) % EXP
            send(s_back[h][r], dall.at[part_of(dp, h), cols(to)], backs[h].at[where, :], (to, dp))
        return copy_in(dall.at[part_of(dp, h), cols(ex)], backs[h].at[where, :])

    def returned(h, own):
        own.wait()
        for r in range(1, EXP):
            src = (ex + EXP - r) % EXP
            arrive(s_back[h][r], backs[h].at[pl.ds(pl.multiple_of(src * PIECE, PIECE), PIECE), :])

    def place_tables():
        table = tab_r[...].astype(F32)
        ids = lax.broadcasted_iota(jnp.int32, (EXP, LOCAL), 0).astype(F32)
        hit = jnp.zeros((EXP, LOCAL), F32)
        for k in range(TOP):
            hit = hit + jnp.where(table[k : k + 1] == ids, 1.0, 0.0)
        stacked = jnp.concatenate([hit[:, b * TOK : (b + 1) * TOK] for b in range(EXP)], axis=0)
        tri = (
            lax.broadcasted_iota(jnp.int32, (TOK, TOK), 0) < lax.broadcasted_iota(jnp.int32, (TOK, TOK), 1)
        ).astype(F32).astype(BF)
        before = jnp.dot(stacked.astype(BF), tri, preferred_element_type=F32)
        for b in range(EXP):
            part = slice(b * EXP, (b + 1) * EXP)
            spots[:, b * TOK : (b + 1) * TOK] = jnp.where(
                stacked[part] > 0.0, before[part] + float(CAP * (b % CHIPS)), -1.0
            )
        slot_row = lax.broadcasted_iota(jnp.int32, (PIECE, LOCAL // 2), 0).astype(F32)
        for h in range(2):
            for e in range(EXP):
                equal = spots[e : e + 1, h * (LOCAL // 2) : (h + 1) * (LOCAL // 2)] == slot_row
                places[h, e * PIECE : (e + 1) * PIECE] = jnp.where(equal, 1.0, 0.0).astype(BF)

    def grad_copy(j, i):
        cols = pl.ds(pl.multiple_of(i * TILE, TILE), TILE)
        out = gg_out if j == 0 else gu_out
        return pltpu.make_async_copy(gbuf.at[j, i % 2], out.at[cols, :], gsem.at[j, i % 2])

    def weight_grads(start, stop):
        def body(i, _):
            cols = pl.ds(pl.multiple_of(i * TILE, TILE), TILE)
            block = xall[:, cols]
            dims = (((0,), (0,)), ((), ()))
            for j, grad in enumerate((dg_ref, du_ref)):
                @pl.when(i >= 2)
                def _():
                    grad_copy(j, i - 2).wait()

                gbuf[j, i % 2] = lax.dot_general(
                    block, grad[...], dims, preferred_element_type=F32
                ).astype(BF)
                grad_copy(j, i).start()
            return 0

        lax.fori_loop(start, stop, body, 0)

    place_tables()
    place_copy = copy_in(places.at[1], place_out)
    flush(*(k[q] for k in (to_up, to_down, to_side) for q in pieces[2:]))
    flush(via_up[1, 0], via_down[1, 0])
    partial(0)
    flush(two["d1r"], two["d0r"], over["u"], over["ur"], two["ph"])
    partial(1)
    direct_up(0)
    flush(two["d1l"], two["d0l"], over["d"], over["dr"], two["pl"])
    partial(NZ - 1)
    direct_down(0)
    arrive(two["d0l"], piece(1, 0, far, left))
    arrive(two["x0"], piece(0, 0, far))
    arrive(two["x1"], piece(0, 1, far))
    hidden(far)
    arrive(two["px0"], piece(0, 0, pfar))
    arrive(two["px1"], piece(0, 1, pfar))
    contract(pfar, True, False)
    arrive(two["pl"], piece(1, 0, pfar, low))
    arrive(two["ph"], piece(1, 0, pfar, high))
    arrive(over["f0"], piece(1, 0, pfar, right))
    arrive(over["fl"], piece(1, 1, pfar, left))
    arrive(over["fr"], piece(1, 1, pfar, right))
    contract(pfar, False, True)
    activate(pfar)
    flush(over["f0"], over["fl"], over["fr"])
    partial(2)
    over_y(2, 0)
    far_b(0)
    for dz in (1, NZ - 1, 0):
        over_y(dz, 0)
    direct_up(1)
    direct_down(1)
    far_a(0)
    far_b(1)
    for dz in (2, 1, NZ - 1, 0):
        over_y(dz, 1)
    combined_b(0)
    near_a(0)
    weight_grads(0, 4)
    far_a(1)
    fold_b(0)
    combined_b(1)
    near_a(1)
    own0 = finish(0)
    weight_grads(4, D // TILE)
    fold_b(1)
    own1 = finish(1)
    returned(0, own0)
    combine(back, places.at[0], outbuf)
    keep = pl.ds(pl.multiple_of(core * 64, 64), WIDE // 2)
    out0 = copy_in(outbuf.at[keep, :], first_out)
    returned(1, own1)
    flush(*list(sent))
    out0.wait()
    place_copy.wait()
    for j in range(2):
        for i in (D // TILE - 2, D // TILE - 1):
            grad_copy(j, i).wait()


def layer(xt, dt, rt, gt, wg, wu, wd):
    hbm = pl.BlockSpec(memory_space=pl.ANY)
    rows = DP * SHARD
    return pl.pallas_call(
        layer_kernel,
        out_shape=(
            jax.ShapeDtypeStruct((WIDE // 2, LOCAL // 2), BF),
            jax.ShapeDtypeStruct((EXP * PIECE, PART), BF),
            jax.ShapeDtypeStruct((EXP * PIECE, LOCAL // 2), BF),
            jax.ShapeDtypeStruct((D, HID), BF),
            jax.ShapeDtypeStruct((D, HID), BF),
        ),
        in_specs=[hbm] * 7,
        out_specs=(hbm,) * 5,
        scratch_shapes=[
            pltpu.VMEM((2, WIDE, LOCAL), BF),
            pltpu.VMEM((TOP, LOCAL), jnp.int32),
            pltpu.VMEM((TOP, LOCAL), BF),
            pltpu.VMEM((CHIPS, LOCAL), F32),
            pltpu.VMEM((CHIPS, LOCAL), F32),
            pltpu.VMEM((CHIPS * PIECE, LOCAL // 2), BF),
            pltpu.VMEM((2, 2, CHIPS, PIECE, WIDE), BF),
            pltpu.VMEM((rows, D), BF),
            pltpu.VMEM((rows, D), BF),
            pltpu.VMEM((D, HID), BF),
            pltpu.VMEM((D, HID), BF),
            pltpu.VMEM((HID, D), BF),
            pltpu.VMEM((3, SHARD, HID), F32),
            pltpu.VMEM((rows, HID), BF),
            pltpu.VMEM((rows, HID), BF),
            pltpu.VMEM((EXP, LOCAL), F32),
            pltpu.VMEM((2, EXP * PIECE, LOCAL // 2), BF),
            pltpu.VMEM((NZ, SHARD, CA), BF),
            pltpu.VMEM((2, SHARD, CA // 2), BF),
            pltpu.VMEM((2, SHARD, CA), BF),
            pltpu.VMEM((2, 2, SHARD, CB // 2), BF),
            pltpu.VMEM((2, 2, SHARD, CB), BF),
            pltpu.VMEM((SHARD, CB), BF),
            pltpu.VMEM((EXP * PIECE, PART), BF),
            pltpu.VMEM((PART, LOCAL // 2), BF),
            pltpu.VMEM((2, 2, TILE, HID), BF),
            pltpu.SemaphoreType.DMA((208,)),
            pltpu.SemaphoreType.DMA((208,)),
            pltpu.SemaphoreType.DMA((24,)),
            pltpu.SemaphoreType.DMA((2, 2)),
        ],
        compiler_params=pltpu.CompilerParams(
            collective_id=0, has_side_effects=True, vmem_limit_bytes=67_000_000
        ),
        name="layer",
    )(xt, dt, rt, gt, wg, wu, wd)


PARTS = 4


def last_kernel(
    first_ref, back_ref, place_ref, gg_ref, gu_ref,
    out_t, gg_out, gu_out,
    first, back, places, out, grads, lsem, gsem, osem,
):
    core = lax.axis_index("expert") % 2
    span = D // PARTS
    loads = [
        pltpu.make_async_copy(src, dst, lsem.at[i])
        for i, (src, dst) in enumerate(((back_ref, back), (place_ref, places), (first_ref, first)))
    ]
    pairs = ((gg_ref, gg_out), (gu_ref, gu_out))
    rows = [slice(n * span, (n + 1) * span) for n in range(PARTS)]
    takes = [[pltpu.make_async_copy(src.at[r, :], grads.at[j, r, :], gsem.at[0, j, n]) for n, r in enumerate(rows)]
             for j, (src, _) in enumerate(pairs)]
    gives = [[pltpu.make_async_copy(grads.at[j, r, :], dst.at[r, :], gsem.at[1, j, n]) for n, r in enumerate(rows)]
             for j, (_, dst) in enumerate(pairs)]
    for c in loads:
        c.start()
    for n in range(PARTS):
        for j in range(2):
            takes[j][n].start()
    half = LOCAL // 2
    keep = pl.ds(pl.multiple_of(core * 64, 64), WIDE // 2)
    for c in loads:
        c.wait()
    early = pltpu.make_async_copy(first, out_t.at[:, :half], osem.at[0])
    late = pltpu.make_async_copy(out.at[keep, :], out_t.at[:, half:], osem.at[1])
    early.start()
    width = half // PARTS
    for n in range(PARTS):
        cols = slice(n * width, (n + 1) * width)
        got = lax.dot_general(
            back[...], places[:, cols], (((0,), (0,)), ((), ())), preferred_element_type=F32
        )
        out[:, cols] = got.astype(BF)
        for j in range(2):
            takes[j][n].wait()
            gives[j][n].start()
    late.start()
    for n in range(PARTS):
        for j in range(2):
            gives[j][n].wait()
    early.wait()
    late.wait()


def last(first, back, places, gg, gu):
    hbm = pl.BlockSpec(memory_space=pl.ANY)
    return pl.pallas_call(
        last_kernel,
        out_shape=(
            jax.ShapeDtypeStruct((WIDE // 2, LOCAL), BF),
            jax.ShapeDtypeStruct((D, HID), BF),
            jax.ShapeDtypeStruct((D, HID), BF),
        ),
        in_specs=[hbm] * 5,
        out_specs=(hbm,) * 3,
        scratch_shapes=[
            pltpu.VMEM((WIDE // 2, LOCAL // 2), BF),
            pltpu.VMEM((EXP * PIECE, PART), BF),
            pltpu.VMEM((EXP * PIECE, LOCAL // 2), BF),
            pltpu.VMEM((PART, LOCAL // 2), BF),
            pltpu.VMEM((2, D, HID), BF),
            pltpu.SemaphoreType.DMA((3,)),
            pltpu.SemaphoreType.DMA((2, 2, PARTS)),
            pltpu.SemaphoreType.DMA((2,)),
        ],
        compiler_params=pltpu.CompilerParams(vmem_limit_bytes=60 * 1024 * 1024),
        name="last",
    )(first, back, places, gg, gu)


def per_device(attn_rows, out_grad, routes, gates, w_gate, w_up, w_down):
    results = layer(attn_rows.T, out_grad.T, routes.T, gates.T, w_gate[0], w_up[0], w_down[0])
    grad_t, g_gate, g_up = last(*results)
    return grad_t.T, g_gate[None], g_up[None]


def solution(mesh):
    return jax.shard_map(
        per_device,
        mesh=mesh,
        in_specs=(
            P("dp", "expert"),
            P("dp", "expert"),
            P(("dp", "expert"), None),
            P(("dp", "expert"), None),
            P("expert", None, "dp"),
            P("expert", None, "dp"),
            P("expert", "dp", None),
        ),
        out_specs=(P("dp", "expert"), P("expert", None, "dp"), P("expert", None, "dp")),
        check_vma=False,
    )
```

```python
import jax
import jax.numpy as jnp
from jax import lax
from jax.experimental import pallas as pl
from jax.experimental.pallas import tpu as pltpu
from jax.sharding import PartitionSpec as P

BF = jnp.bfloat16
F32 = jnp.float32
MESH = pl.DeviceIdType.MESH
NT = (((1,), (1,)), ((), ()))
EXP, DP, NZ, CHIPS = 16, 8, 4, 8
TOK, TOP, CAP = 128, 8, 6
LOCAL = EXP * TOK
WIDE, D, HID = 896, 7168, 256
PIECE = 48
SHARD = 96
STEP = 1024


NA = 2
CA = NA * WIDE
CB = D - CA
LA, RA = slice(0, CA // 2), slice(CA // 2, CA)
ALL_A, ALL_B = slice(0, CA), slice(CA, D)
LB, RB = slice(CA, CA + CB // 2), slice(CA + CB // 2, D)
PART = 512
TILE = 512


def combine(back, places, out, width=256):
    for n in range(0, LOCAL // 2, width):
        got = lax.dot_general(
            back[...], places[:, n : n + width], (((0,), (0,)), ((), ())), preferred_element_type=F32
        )
        out[:, n : n + width] = got.astype(BF)


def layer_kernel(
    xt_ref, dt_ref, rt_ref, gt_ref, wg_ref, wu_ref, wd_ref,
    first_out, back_out, place_out, gg_out, gu_out,
    raw, tab_r, tab_g, code, coef, onehot, pay, xall, dall, wg, wu, wd, acc, dg_ref, du_ref,
    spots, places, got_a, relay_a, fin_a, relay_b, fin_b, got_b, back, outbuf, gbuf,
    ssem, rsem, lsem, gsem,
):
    ex = lax.axis_index("expert")
    dp = lax.axis_index("dp")
    core = ex % 2
    chip = ex // 2
    row, z = dp // NZ, dp % NZ

    def at(dy, dz):
        return (row + dy) % 2 * NZ + (z + dz) % NZ

    up, down, side = at(0, 1), at(0, NZ - 1), at(1, 0)
    bufs = (xall, dall)

    barrier = pltpu.get_barrier_semaphore()
    for r in range(1, EXP):
        pl.semaphore_signal(barrier, inc=1, device_id=((ex + r) % EXP, dp), device_id_type=MESH)
    for peer in (up, down, side):
        pl.semaphore_signal(barrier, inc=1, device_id=(ex, peer), device_id_type=MESH)

    local = []

    def copy_in(src, dst):
        c = pltpu.make_async_copy(src, dst, lsem.at[len(local)])
        c.start()
        local.append(c)
        return c

    mine = pl.ds(pl.multiple_of(core * (WIDE // 2), WIDE // 2), WIDE // 2)
    lanes = pl.ds(pl.multiple_of(ex * TOK, TOK), TOK)
    in_tab = [copy_in(rt_ref, tab_r.at[:, lanes]), copy_in(gt_ref, tab_g.at[:, lanes])]
    in_raw = [copy_in(ref, raw.at[t, mine, :]) for t, ref in enumerate((xt_ref, dt_ref))]
    in_w = [copy_in(wg_ref, wg), copy_in(wu_ref, wu), copy_in(wd_ref, wd)]

    pl.semaphore_wait(barrier, EXP - 1 + 3)

    sent = {}
    slots = [0]

    def slot():
        slots[0] += 1
        return slots[0] - 1

    def send(k, src, dst, device):
        c = pltpu.make_async_remote_copy(
            src_ref=src, dst_ref=dst, send_sem=ssem.at[k], recv_sem=rsem.at[k],
            device_id=device, device_id_type=MESH,
        )
        c.start()
        sent[k] = c

    def flush(*keys):
        for k in keys:
            sent.pop(k).wait_send()

    def arrive(k, dst):
        pltpu.make_async_remote_copy(
            src_ref=dst, dst_ref=dst, send_sem=ssem.at[k], recv_sem=rsem.at[k],
            device_id=(ex, side), device_id_type=MESH,
        ).wait_recv()

    other = pl.ds(pl.multiple_of((1 - core) * (WIDE // 2), WIDE // 2), WIDE // 2)
    tab_slot = [(slot(), slot()) for _ in range(EXP)]
    for r in range(1, EXP):
        send(tab_slot[r][0], rt_ref, tab_r.at[:, lanes], ((ex + r) % EXP, dp))
        send(tab_slot[r][1], gt_ref, tab_g.at[:, lanes], ((ex + r) % EXP, dp))
    raw_slot = [slot(), slot()]
    sibling = (chip * 2 + 1 - core, dp)
    for t, ref in enumerate((xt_ref, dt_ref)):
        send(raw_slot[t], ref, raw.at[t, mine, :], sibling)

    for c in in_tab:
        c.wait()
    for r in range(1, EXP):
        theirs = pl.ds(pl.multiple_of((ex + EXP - r) % EXP * TOK, TOK), TOK)
        arrive(tab_slot[r][0], tab_r.at[:, theirs])
        arrive(tab_slot[r][1], tab_g.at[:, theirs])

    route, gate = tab_r[...].astype(F32), tab_g[...].astype(F32)
    ids = (lax.broadcasted_iota(jnp.int32, (CHIPS, LOCAL), 0) * 2 + core).astype(F32)
    hit = jnp.zeros((CHIPS, LOCAL), F32)
    weight = jnp.zeros((CHIPS, LOCAL), F32)
    for k in range(TOP):
        same = route[k : k + 1] == ids
        hit = hit + jnp.where(same, 1.0, 0.0)
        weight = weight + jnp.where(same, gate[k : k + 1], 0.0)
    coef[...] = weight
    stacked = jnp.concatenate([hit[:, b * TOK : (b + 1) * TOK] for b in range(EXP)], axis=0)
    tri = (
        lax.broadcasted_iota(jnp.int32, (TOK, TOK), 0) < lax.broadcasted_iota(jnp.int32, (TOK, TOK), 1)
    ).astype(F32).astype(BF)
    before = jnp.dot(stacked.astype(BF), tri, preferred_element_type=F32)
    for b in range(EXP):
        part = slice(b * CHIPS, (b + 1) * CHIPS)
        code[:, b * TOK : (b + 1) * TOK] = jnp.where(
            stacked[part] > 0.0, before[part] + float(CAP * (b % CHIPS)), -1.0
        )

    slot_row = lax.broadcasted_iota(jnp.int32, (PIECE, LOCAL // 2), 0).astype(F32)
    own_rows = [pl.ds(pl.multiple_of(dp * SHARD + h * PIECE, PIECE), PIECE) for h in range(2)]
    chip_cols = pl.ds(pl.multiple_of(chip * WIDE, WIDE), WIDE)
    a2a_slot = [[[slot() for _ in range(CHIPS)] for _ in range(2)] for _ in range(2)]
    a2a_self = [[None, None], [None, None]]

    def dispatch(t, h):
        half = slice(h * (LOCAL // 2), (h + 1) * (LOCAL // 2))
        for i in range(CHIPS):
            equal = code[i : i + 1, half] == slot_row
            value = 1.0 if t == 0 else coef[i : i + 1, half]
            onehot[i * PIECE : (i + 1) * PIECE] = jnp.where(equal, value, 0.0).astype(BF)
        for n in range(0, WIDE, 128):
            got = lax.dot_general(onehot[...], raw[t, n : n + 128, half], NT, preferred_element_type=F32)
            pay[t, h, :, :, n : n + 128] = got.astype(BF).reshape(CHIPS, PIECE, 128)
        where = bufs[t].at[own_rows[h], chip_cols]
        for r in range(1, CHIPS):
            to = (chip + r) % CHIPS
            send(a2a_slot[t][h][r], pay.at[t, h, to], where, (to * 2 + core, dp))
        a2a_self[t][h] = copy_in(pay.at[t, h, chip], where)

    def complete(t, h):
        a2a_self[t][h].wait()
        for r in range(1, CHIPS):
            src = (chip + CHIPS - r) % CHIPS
            arrive(a2a_slot[t][h][r], bufs[t].at[own_rows[h], pl.ds(pl.multiple_of(src * WIDE, WIDE), WIDE)])

    def rows_of(s):
        return pl.ds(pl.multiple_of(s * SHARD, SHARD), SHARD)

    def contract(s, with_x, with_d):
        rows = rows_of(s)
        if with_x:
            acc[0:2] = jnp.zeros((2, SHARD, HID), F32)
        if with_d:
            acc[2] = jnp.zeros((SHARD, HID), F32)

        def body(k, _):
            cols = pl.ds(pl.multiple_of(k * STEP, STEP), STEP)
            if with_x:
                xs = xall[rows, cols]
                acc[0] += jnp.dot(xs, wg[cols, :], preferred_element_type=F32)
                acc[1] += jnp.dot(xs, wu[cols, :], preferred_element_type=F32)
            if with_d:
                acc[2] += lax.dot_general(dall[rows, cols], wd[:, cols], NT, preferred_element_type=F32)
            return 0

        lax.fori_loop(0, D // STEP, body, 0)

    def activate(s):
        rows = rows_of(s)
        g, u, q = acc[0], acc[1], acc[2]
        sig = jax.nn.sigmoid(g)
        dg_ref[rows, :] = (q * u * sig * (1.0 + g * (1.0 - sig))).astype(BF)
        du_ref[rows, :] = (q * (g * sig)).astype(BF)

    def hidden(s):
        contract(s, True, True)
        activate(s)

    half = D // 2
    left, right, whole = slice(0, half), slice(half, D), slice(0, D)
    low, high = slice(0, half // 2), slice(half // 2, half)

    def piece(t, h, s, cols=whole):
        return bufs[t].at[pl.ds(pl.multiple_of(s * SHARD + h * PIECE, PIECE), PIECE), cols]

    def pass_on(k, to, t, h, s, cols=whole):
        send(k, piece(t, h, s, cols), piece(t, h, s, cols), (ex, to))

    def slots_for(*names):
        return {name: slot() for name in names}

    pieces = ((0, 0), (0, 1), (1, 0), (1, 1))
    to_up, to_down, to_side = slots_for(*pieces), slots_for(*pieces), slots_for(*pieces)

    def spread_z(t, h):
        pass_on(to_up[t, h], up, t, h, dp)
        pass_on(to_down[t, h], down, t, h, dp)

    first_up, first_down = [slot() for _ in range(CHIPS)], [slot() for _ in range(CHIPS)]
    order = (0, 2, 6, 1, 7, 3, 5, 4)

    def chunk(r, s):
        src = (chip + CHIPS - r) % CHIPS
        rows = pl.ds(pl.multiple_of(s * SHARD, SHARD), PIECE)
        return xall.at[rows, pl.ds(pl.multiple_of(src * WIDE, WIDE), WIDE)]

    def spread_first(some):
        for r in some:
            if r == 0:
                a2a_self[0][0].wait()
            else:
                arrive(a2a_slot[0][0][r], chunk(r, dp))
            send(first_up[r], chunk(r, dp), chunk(r, dp), (ex, up))
            send(first_down[r], chunk(r, dp), chunk(r, dp), (ex, down))

    def spread_y(t, h):
        pass_on(to_side[t, h], side, t, h, dp)

    in_raw[0].wait()
    arrive(raw_slot[0], raw.at[0, other, :])
    dispatch(0, 0)
    spread_first(order[:1])
    dispatch(0, 1)
    spread_first(order[1:])
    in_raw[1].wait()
    arrive(raw_slot[1], raw.at[1, other, :])
    dispatch(1, 0)
    complete(0, 1)
    spread_z(0, 1)
    dispatch(1, 1)
    spread_y(0, 0)
    spread_y(0, 1)
    complete(1, 0)
    spread_z(1, 0)
    spread_y(1, 0)
    complete(1, 1)
    spread_z(1, 1)
    spread_y(1, 1)
    for c in in_w:
        c.wait()

    far, pdown, pup, pfar = at(0, 2), at(1, NZ - 1), at(1, 1), at(1, 2)
    early = ((0, 0, whole), (0, 1, whole), (1, 0, left))
    via_up, via_down = slots_for(*pieces[:3]), slots_for(*pieces[:3])

    def relay_side(i):
        t, h, cols = early[i]
        arrive(to_side[t, h], piece(t, h, side))
        pass_on(via_up[t, h], up, t, h, side, cols)
        pass_on(via_down[t, h], down, t, h, side, cols)

    relay_side(0)
    hidden(dp)
    relay_side(1)
    for r in order:
        arrive(first_up[r], chunk(r, down))
        arrive(first_down[r], chunk(r, up))
    arrive(to_up[0, 1], piece(0, 1, down))
    arrive(to_down[0, 1], piece(0, 1, up))
    over = slots_for("d", "dr", "u", "ur", "fl", "fr", "f0")
    two = slots_for("d1l", "d1r", "d0l", "d0r", "x0", "x1", "px0", "px1", "pl", "ph")
    arrive(to_up[1, 0], piece(1, 0, down))
    pass_on(over["dr"], side, 1, 0, down, right)
    arrive(to_down[1, 0], piece(1, 0, up))
    pass_on(over["ur"], side, 1, 0, up, right)
    arrive(to_up[1, 1], piece(1, 1, down))
    pass_on(two["d1l"], up, 1, 1, down, left)
    pass_on(over["d"], side, 1, 1, down)
    arrive(to_down[1, 1], piece(1, 1, up))
    pass_on(two["d1r"], down, 1, 1, up, right)
    pass_on(over["u"], side, 1, 1, up)
    pass_on(two["d0l"], up, 1, 0, down, left)
    pass_on(two["d0r"], down, 1, 0, up, right)
    relay_side(2)
    pass_on(two["x0"], up, 0, 0, down)
    pass_on(two["x1"], down, 0, 1, up)
    hidden(down)
    arrive(to_side[1, 1], piece(1, 1, side))
    hidden(side)
    hidden(up)
    arrive(via_up[1, 0], piece(1, 0, pdown, left))
    pass_on(two["pl"], up, 1, 0, pdown, low)
    arrive(via_down[1, 0], piece(1, 0, pup, left))
    pass_on(two["ph"], down, 1, 0, pup, high)
    arrive(via_up[0, 0], piece(0, 0, pdown))
    pass_on(two["px0"], up, 0, 0, pdown)
    arrive(via_down[0, 1], piece(0, 1, pup))
    pass_on(two["px1"], down, 0, 1, pup)
    arrive(two["d0r"], piece(1, 0, far, right))
    pass_on(over["f0"], side, 1, 0, far, right)
    arrive(two["d1l"], piece(1, 1, far, left))
    pass_on(over["fl"], side, 1, 1, far, left)
    arrive(two["d1r"], piece(1, 1, far, right))
    pass_on(over["fr"], side, 1, 1, far, right)
    arrive(via_up[0, 1], piece(0, 1, pdown))
    arrive(over["dr"], piece(1, 0, pdown, right))
    arrive(over["d"], piece(1, 1, pdown))
    hidden(pdown)
    arrive(via_down[0, 0], piece(0, 0, pup))
    arrive(over["ur"], piece(1, 0, pup, right))
    arrive(over["u"], piece(1, 1, pup))
    hidden(pup)
    def part_of(s, h):
        return pl.ds(pl.multiple_of(s * SHARD + h * PIECE, PIECE), PIECE)

    def partial(dz):
        first, second = rows_of(at(0, dz)), rows_of(at(1, dz))
        g2 = jnp.concatenate([dg_ref[first, :], dg_ref[second, :]], axis=0)
        u2 = jnp.concatenate([du_ref[first, :], du_ref[second, :]], axis=0)

        def body(k, _):
            cols = pl.ds(pl.multiple_of(k * WIDE, WIDE), WIDE)
            v = lax.dot_general(g2, wg[cols, :], NT, preferred_element_type=F32)
            v = (v + lax.dot_general(u2, wu[cols, :], NT, preferred_element_type=F32)).astype(BF)
            dall[first, cols] = v[:SHARD]
            dall[second, cols] = v[SHARD:]
            return 0

        lax.fori_loop(0, D // WIDE, body, 0)

    def add(s, h, cols, *others):
        def body(i, _):
            here = pl.ds(pl.multiple_of(s * SHARD + h * PIECE + i * 16, 16), 16)
            total = dall[here, cols].astype(F32)
            for other in others:
                total = total + other(pl.ds(pl.multiple_of(h * PIECE + i * 16, 16), 16)).astype(F32)
            dall[here, cols] = total.astype(BF)
            return 0

        lax.fori_loop(0, PIECE // 16, body, 0)

    rows48 = [slice(h * PIECE, (h + 1) * PIECE) for h in range(2)]
    s_ya = {(h, dz): slot() for h in range(2) for dz in range(NZ)}
    s_relay_b = {(h, y, d): slot() for h in range(2) for y in range(2) for d in range(2)}
    s_fin_l = {(h, y, d): slot() for h in range(2) for y in range(2) for d in range(2)}
    s_fin_r = {(h, y, d): slot() for h in range(2) for y in range(2) for d in range(2)}
    s_relay_a = {(h, d): slot() for h in range(2) for d in range(2)}
    s_fin_a = {(h, d): slot() for h in range(2) for d in range(2)}
    s_yb = [slot(), slot()]
    s_back = [[slot() for _ in range(EXP)] for _ in range(2)]
    rel_l, rel_r = slice(0, CB // 2), slice(CB // 2, CB)

    def over_y(dz, h):
        send(s_ya[h, dz], dall.at[part_of(at(1, dz), h), ALL_A], got_a.at[dz, rows48[h], :], (ex, side))

    def line(j, dz):
        return at(1 - j, dz)

    def far_b(h, y):
        src = part_of(line(y, 2), h)
        send(s_relay_b[h, y, 0], dall.at[src, LB], relay_b.at[0, y, rows48[h], :], (ex, up))
        send(s_relay_b[h, y, 1], dall.at[src, RB], relay_b.at[1, y, rows48[h], :], (ex, down))

    def direct_up(h, y):
        send(s_fin_r[h, y, 0], dall.at[part_of(line(y, 1), h), RB], fin_b.at[0, y, rows48[h], rel_r], (ex, up))

    def direct_down(h, y):
        send(s_fin_l[h, y, 1], dall.at[part_of(line(y, NZ - 1), h), LB], fin_b.at[1, y, rows48[h], rel_l], (ex, down))

    def combined_b(h, y):
        arrive(s_relay_b[h, y, 0], relay_b.at[0, y, rows48[h], :])
        add(line(y, 1), h, LB, lambda r, y=y: relay_b[0, y, r, :])
        send(s_fin_l[h, y, 0], dall.at[part_of(line(y, 1), h), LB], fin_b.at[0, y, rows48[h], rel_l], (ex, up))
        arrive(s_relay_b[h, y, 1], relay_b.at[1, y, rows48[h], :])
        add(line(y, NZ - 1), h, RB, lambda r, y=y: relay_b[1, y, r, :])
        send(s_fin_r[h, y, 1], dall.at[part_of(line(y, NZ - 1), h), RB], fin_b.at[1, y, rows48[h], rel_r], (ex, down))

    def far_a(h):
        arrive(s_ya[h, 2], got_a.at[2, rows48[h], :])
        add(at(0, 2), h, ALL_A, lambda r: got_a[2, r, :])
        src = part_of(at(0, 2), h)
        send(s_relay_a[h, 0], dall.at[src, LA], relay_a.at[0, rows48[h], :], (ex, up))
        send(s_relay_a[h, 1], dall.at[src, RA], relay_a.at[1, rows48[h], :], (ex, down))

    def near_a(h):
        for d, dz, peer, mixed in ((0, 1, up, LA), (1, NZ - 1, down, RA)):
            plain = RA if d == 0 else LA
            arrive(s_ya[h, dz], got_a.at[dz, rows48[h], :])
            add(at(0, dz), h, plain, lambda r, dz=dz: got_a[dz, r, plain])
            arrive(s_relay_a[h, d], relay_a.at[d, rows48[h], :])
            add(at(0, dz), h, mixed, lambda r, dz=dz: got_a[dz, r, mixed], lambda r, d=d: relay_a[d, r, :])
            send(s_fin_a[h, d], dall.at[part_of(at(0, dz), h), ALL_A], fin_a.at[d, rows48[h], :], (ex, peer))

    def wait_b(h, j):
        for d in range(2):
            arrive(s_fin_l[h, j, d], fin_b.at[d, j, rows48[h], rel_l])
            arrive(s_fin_r[h, j, d], fin_b.at[d, j, rows48[h], rel_r])

    def fold_b(h):
        wait_b(h, 0)
        add(side, h, ALL_B, lambda r: fin_b[0, 0, r, :], lambda r: fin_b[1, 0, r, :])
        send(s_yb[h], dall.at[part_of(side, h), ALL_B], got_b.at[rows48[h], :], (ex, side))

    backs = (back, back_out)

    def finish(h):
        arrive(s_ya[h, 0], got_a.at[0, rows48[h], :])
        for d in range(2):
            arrive(s_fin_a[h, d], fin_a.at[d, rows48[h], :])
        add(dp, h, ALL_A, lambda r: got_a[0, r, :], lambda r: fin_a[0, r, :], lambda r: fin_a[1, r, :])
        wait_b(h, 1)
        arrive(s_yb[h], got_b.at[rows48[h], :])
        add(
            dp, h, ALL_B,
            lambda r: fin_b[0, 1, r, :], lambda r: fin_b[1, 1, r, :], lambda r: got_b[r, :],
        )
        where = pl.ds(pl.multiple_of(ex * PIECE, PIECE), PIECE)

        def cols(e):
            return pl.ds(pl.multiple_of(e // 2 * WIDE + e % 2 * 384, 128), PART)

        for r in range(1, EXP):
            to = (ex + r) % EXP
            send(s_back[h][r], dall.at[part_of(dp, h), cols(to)], backs[h].at[where, :], (to, dp))
        return copy_in(dall.at[part_of(dp, h), cols(ex)], backs[h].at[where, :])

    def returned(h, own):
        own.wait()
        for r in range(1, EXP):
            src = (ex + EXP - r) % EXP
            arrive(s_back[h][r], backs[h].at[pl.ds(pl.multiple_of(src * PIECE, PIECE), PIECE), :])

    def place_tables():
        table = tab_r[...].astype(F32)
        ids = lax.broadcasted_iota(jnp.int32, (EXP, LOCAL), 0).astype(F32)
        hit = jnp.zeros((EXP, LOCAL), F32)
        for k in range(TOP):
            hit = hit + jnp.where(table[k : k + 1] == ids, 1.0, 0.0)
        stacked = jnp.concatenate([hit[:, b * TOK : (b + 1) * TOK] for b in range(EXP)], axis=0)
        tri = (
            lax.broadcasted_iota(jnp.int32, (TOK, TOK), 0) < lax.broadcasted_iota(jnp.int32, (TOK, TOK), 1)
        ).astype(F32).astype(BF)
        before = jnp.dot(stacked.astype(BF), tri, preferred_element_type=F32)
        for b in range(EXP):
            part = slice(b * EXP, (b + 1) * EXP)
            spots[:, b * TOK : (b + 1) * TOK] = jnp.where(
                stacked[part] > 0.0, before[part] + float(CAP * (b % CHIPS)), -1.0
            )
        slot_row = lax.broadcasted_iota(jnp.int32, (PIECE, LOCAL // 2), 0).astype(F32)
        for h in range(2):
            for e in range(EXP):
                equal = spots[e : e + 1, h * (LOCAL // 2) : (h + 1) * (LOCAL // 2)] == slot_row
                places[h, e * PIECE : (e + 1) * PIECE] = jnp.where(equal, 1.0, 0.0).astype(BF)

    def grad_copy(j, i):
        cols = pl.ds(pl.multiple_of(i * TILE, TILE), TILE)
        out = gg_out if j == 0 else gu_out
        return pltpu.make_async_copy(gbuf.at[j, i % 2], out.at[cols, :], gsem.at[j, i % 2])

    def weight_grads(start, stop):
        def body(i, _):
            cols = pl.ds(pl.multiple_of(i * TILE, TILE), TILE)
            block = xall[:, cols]
            dims = (((0,), (0,)), ((), ()))
            for j, grad in enumerate((dg_ref, du_ref)):
                @pl.when(i >= 2)
                def _():
                    grad_copy(j, i - 2).wait()

                gbuf[j, i % 2] = lax.dot_general(
                    block, grad[...], dims, preferred_element_type=F32
                ).astype(BF)
                grad_copy(j, i).start()
            return 0

        lax.fori_loop(start, stop, body, 0)

    place_tables()
    place_copy = copy_in(places.at[1], place_out)
    flush(*(k[q] for k in (to_up, to_down, to_side) for q in pieces[2:]))
    flush(via_up[1, 0], via_down[1, 0])
    partial(0)
    flush(two["d1r"], two["d0r"], over["u"], over["ur"], two["ph"])
    partial(1)
    for h in range(2):
        direct_up(h, 0)
    flush(two["d1l"], two["d0l"], over["d"], over["dr"], two["pl"])
    partial(NZ - 1)
    for h in range(2):
        direct_down(h, 0)
    for h in range(2):
        direct_up(h, 1)
        direct_down(h, 1)
    for dz in (0, 1, NZ - 1):
        for h in range(2):
            over_y(dz, h)
    arrive(two["d0l"], piece(1, 0, far, left))
    arrive(two["x0"], piece(0, 0, far))
    arrive(two["x1"], piece(0, 1, far))
    hidden(far)
    arrive(two["px0"], piece(0, 0, pfar))
    arrive(two["px1"], piece(0, 1, pfar))
    contract(pfar, True, False)
    arrive(two["pl"], piece(1, 0, pfar, low))
    arrive(two["ph"], piece(1, 0, pfar, high))
    arrive(over["f0"], piece(1, 0, pfar, right))
    arrive(over["fl"], piece(1, 1, pfar, left))
    arrive(over["fr"], piece(1, 1, pfar, right))
    contract(pfar, False, True)
    activate(pfar)
    flush(over["f0"], over["fl"], over["fr"])
    partial(2)
    for y in range(2):
        for h in range(2):
            far_b(h, y)
    for h in range(2):
        over_y(2, h)
    weight_grads(0, 6)
    combined_b(0, 0)
    far_a(0)
    far_a(1)
    combined_b(1, 0)
    fold_b(0)
    near_a(0)
    near_a(1)
    combined_b(0, 1)
    combined_b(1, 1)
    fold_b(1)
    weight_grads(6, D // TILE)
    own0 = finish(0)
    own1 = finish(1)
    returned(0, own0)
    combine(back, places.at[0], outbuf)
    keep = pl.ds(pl.multiple_of(core * 64, 64), WIDE // 2)
    out0 = copy_in(outbuf.at[keep, :], first_out)
    returned(1, own1)
    flush(*list(sent))
    out0.wait()
    place_copy.wait()
    for j in range(2):
        for i in (D // TILE - 2, D // TILE - 1):
            grad_copy(j, i).wait()


def layer(xt, dt, rt, gt, wg, wu, wd):
    hbm = pl.BlockSpec(memory_space=pl.ANY)
    rows = DP * SHARD
    return pl.pallas_call(
        layer_kernel,
        out_shape=(
            jax.ShapeDtypeStruct((WIDE // 2, LOCAL // 2), BF),
            jax.ShapeDtypeStruct((EXP * PIECE, PART), BF),
            jax.ShapeDtypeStruct((EXP * PIECE, LOCAL // 2), BF),
            jax.ShapeDtypeStruct((D, HID), BF),
            jax.ShapeDtypeStruct((D, HID), BF),
        ),
        in_specs=[hbm] * 7,
        out_specs=(hbm,) * 5,
        scratch_shapes=[
            pltpu.VMEM((2, WIDE, LOCAL), BF),
            pltpu.VMEM((TOP, LOCAL), jnp.int32),
            pltpu.VMEM((TOP, LOCAL), BF),
            pltpu.VMEM((CHIPS, LOCAL), F32),
            pltpu.VMEM((CHIPS, LOCAL), F32),
            pltpu.VMEM((CHIPS * PIECE, LOCAL // 2), BF),
            pltpu.VMEM((2, 2, CHIPS, PIECE, WIDE), BF),
            pltpu.VMEM((rows, D), BF),
            pltpu.VMEM((rows, D), BF),
            pltpu.VMEM((D, HID), BF),
            pltpu.VMEM((D, HID), BF),
            pltpu.VMEM((HID, D), BF),
            pltpu.VMEM((3, SHARD, HID), F32),
            pltpu.VMEM((rows, HID), BF),
            pltpu.VMEM((rows, HID), BF),
            pltpu.VMEM((EXP, LOCAL), F32),
            pltpu.VMEM((2, EXP * PIECE, LOCAL // 2), BF),
            pltpu.VMEM((NZ, SHARD, CA), BF),
            pltpu.VMEM((2, SHARD, CA // 2), BF),
            pltpu.VMEM((2, SHARD, CA), BF),
            pltpu.VMEM((2, 2, SHARD, CB // 2), BF),
            pltpu.VMEM((2, 2, SHARD, CB), BF),
            pltpu.VMEM((SHARD, CB), BF),
            pltpu.VMEM((EXP * PIECE, PART), BF),
            pltpu.VMEM((PART, LOCAL // 2), BF),
            pltpu.VMEM((2, 2, TILE, HID), BF),
            pltpu.SemaphoreType.DMA((208,)),
            pltpu.SemaphoreType.DMA((208,)),
            pltpu.SemaphoreType.DMA((24,)),
            pltpu.SemaphoreType.DMA((2, 2)),
        ],
        compiler_params=pltpu.CompilerParams(
            collective_id=0, has_side_effects=True, vmem_limit_bytes=67_000_000
        ),
        name="layer",
    )(xt, dt, rt, gt, wg, wu, wd)


PARTS = 4


def last_kernel(
    first_ref, back_ref, place_ref, gg_ref, gu_ref,
    out_t, gg_out, gu_out,
    first, back, places, out, grads, lsem, gsem, osem,
):
    core = lax.axis_index("expert") % 2
    span = D // PARTS
    loads = [
        pltpu.make_async_copy(src, dst, lsem.at[i])
        for i, (src, dst) in enumerate(((back_ref, back), (place_ref, places), (first_ref, first)))
    ]
    pairs = ((gg_ref, gg_out), (gu_ref, gu_out))
    rows = [slice(n * span, (n + 1) * span) for n in range(PARTS)]
    takes = [[pltpu.make_async_copy(src.at[r, :], grads.at[j, r, :], gsem.at[0, j, n]) for n, r in enumerate(rows)]
             for j, (src, _) in enumerate(pairs)]
    gives = [[pltpu.make_async_copy(grads.at[j, r, :], dst.at[r, :], gsem.at[1, j, n]) for n, r in enumerate(rows)]
             for j, (_, dst) in enumerate(pairs)]
    for c in loads:
        c.start()
    for n in range(PARTS):
        for j in range(2):
            takes[j][n].start()
    half = LOCAL // 2
    keep = pl.ds(pl.multiple_of(core * 64, 64), WIDE // 2)
    for c in loads:
        c.wait()
    early = pltpu.make_async_copy(first, out_t.at[:, :half], osem.at[0])
    late = pltpu.make_async_copy(out.at[keep, :], out_t.at[:, half:], osem.at[1])
    early.start()
    width = half // PARTS
    for n in range(PARTS):
        cols = slice(n * width, (n + 1) * width)
        got = lax.dot_general(
            back[...], places[:, cols], (((0,), (0,)), ((), ())), preferred_element_type=F32
        )
        out[:, cols] = got.astype(BF)
        for j in range(2):
            takes[j][n].wait()
            gives[j][n].start()
    late.start()
    for n in range(PARTS):
        for j in range(2):
            gives[j][n].wait()
    early.wait()
    late.wait()


def last(first, back, places, gg, gu):
    hbm = pl.BlockSpec(memory_space=pl.ANY)
    return pl.pallas_call(
        last_kernel,
        out_shape=(
            jax.ShapeDtypeStruct((WIDE // 2, LOCAL), BF),
            jax.ShapeDtypeStruct((D, HID), BF),
            jax.ShapeDtypeStruct((D, HID), BF),
        ),
        in_specs=[hbm] * 5,
        out_specs=(hbm,) * 3,
        scratch_shapes=[
            pltpu.VMEM((WIDE // 2, LOCAL // 2), BF),
            pltpu.VMEM((EXP * PIECE, PART), BF),
            pltpu.VMEM((EXP * PIECE, LOCAL // 2), BF),
            pltpu.VMEM((PART, LOCAL // 2), BF),
            pltpu.VMEM((2, D, HID), BF),
            pltpu.SemaphoreType.DMA((3,)),
            pltpu.SemaphoreType.DMA((2, 2, PARTS)),
            pltpu.SemaphoreType.DMA((2,)),
        ],
        compiler_params=pltpu.CompilerParams(vmem_limit_bytes=60 * 1024 * 1024),
        name="last",
    )(first, back, places, gg, gu)


def per_device(attn_rows, out_grad, routes, gates, w_gate, w_up, w_down):
    results = layer(attn_rows.T, out_grad.T, routes.T, gates.T, w_gate[0], w_up[0], w_down[0])
    grad_t, g_gate, g_up = last(*results)
    return grad_t.T, g_gate[None], g_up[None]


def solution(mesh):
    return jax.shard_map(
        per_device,
        mesh=mesh,
        in_specs=(
            P("dp", "expert"),
            P("dp", "expert"),
            P(("dp", "expert"), None),
            P(("dp", "expert"), None),
            P("expert", None, "dp"),
            P("expert", None, "dp"),
            P("expert", "dp", None),
        ),
        out_specs=(P("dp", "expert"), P("expert", None, "dp"), P("expert", None, "dp")),
        check_vma=False,
    )
```

```python
import jax
import jax.numpy as jnp
from jax import lax
from jax.experimental import pallas as pl
from jax.experimental.pallas import tpu as pltpu
from jax.sharding import PartitionSpec as P

BF = jnp.bfloat16
F32 = jnp.float32
MESH = pl.DeviceIdType.MESH
NT = (((1,), (1,)), ((), ()))
EXP, DP, NZ, CHIPS = 16, 8, 4, 8
TOK, TOP, CAP = 128, 8, 6
LOCAL = EXP * TOK
WIDE, D, HID = 896, 7168, 256
PIECE = 48
SHARD = 96
STEP = 1024


NA = 2
CA = NA * WIDE
CB = D - CA
LA, RA = slice(0, CA // 2), slice(CA // 2, CA)
ALL_A, ALL_B = slice(0, CA), slice(CA, D)
LB, RB = slice(CA, CA + CB // 2), slice(CA + CB // 2, D)
PART = 512
TILE = 512


def combine(back, places, out, width=256):
    for n in range(0, LOCAL // 2, width):
        got = lax.dot_general(
            back[...], places[:, n : n + width], (((0,), (0,)), ((), ())), preferred_element_type=F32
        )
        out[:, n : n + width] = got.astype(BF)


def layer_kernel(
    xt_ref, dt_ref, rt_ref, gt_ref, wg_ref, wu_ref, wd_ref,
    first_out, back_out, place_out, gg_out, gu_out,
    raw, tab_r, tab_g, code, coef, onehot, pay, xall, dall, wg, wu, wd, acc, dg_ref, du_ref,
    spots, places, got_a, relay_a, fin_a, relay_b, fin_b, got_b, back, outbuf, gbuf,
    ssem, rsem, lsem, gsem,
):
    ex = lax.axis_index("expert")
    dp = lax.axis_index("dp")
    core = ex % 2
    chip = ex // 2
    row, z = dp // NZ, dp % NZ

    def at(dy, dz):
        return (row + dy) % 2 * NZ + (z + dz) % NZ

    up, down, side = at(0, 1), at(0, NZ - 1), at(1, 0)
    bufs = (xall, dall)

    barrier = pltpu.get_barrier_semaphore()
    for r in range(1, EXP):
        pl.semaphore_signal(barrier, inc=1, device_id=((ex + r) % EXP, dp), device_id_type=MESH)
    for peer in (up, down, side):
        pl.semaphore_signal(barrier, inc=1, device_id=(ex, peer), device_id_type=MESH)

    local = []

    def copy_in(src, dst):
        c = pltpu.make_async_copy(src, dst, lsem.at[len(local)])
        c.start()
        local.append(c)
        return c

    mine = pl.ds(pl.multiple_of(core * (WIDE // 2), WIDE // 2), WIDE // 2)
    lanes = pl.ds(pl.multiple_of(ex * TOK, TOK), TOK)
    in_tab = [copy_in(rt_ref, tab_r.at[:, lanes]), copy_in(gt_ref, tab_g.at[:, lanes])]
    in_raw = [copy_in(ref, raw.at[t, mine, :]) for t, ref in enumerate((xt_ref, dt_ref))]

    pl.semaphore_wait(barrier, EXP - 1 + 3)

    sent = {}
    slots = [0]

    def slot():
        slots[0] += 1
        return slots[0] - 1

    def send(k, src, dst, device):
        c = pltpu.make_async_remote_copy(
            src_ref=src, dst_ref=dst, send_sem=ssem.at[k], recv_sem=rsem.at[k],
            device_id=device, device_id_type=MESH,
        )
        c.start()
        sent[k] = c

    def flush(*keys):
        for k in keys:
            sent.pop(k).wait_send()

    def arrive(k, dst):
        pltpu.make_async_remote_copy(
            src_ref=dst, dst_ref=dst, send_sem=ssem.at[k], recv_sem=rsem.at[k],
            device_id=(ex, side), device_id_type=MESH,
        ).wait_recv()

    other = pl.ds(pl.multiple_of((1 - core) * (WIDE // 2), WIDE // 2), WIDE // 2)
    tab_slot = [(slot(), slot()) for _ in range(EXP)]
    for r in range(1, EXP):
        send(tab_slot[r][0], rt_ref, tab_r.at[:, lanes], ((ex + r) % EXP, dp))
        send(tab_slot[r][1], gt_ref, tab_g.at[:, lanes], ((ex + r) % EXP, dp))
    raw_slot = [slot(), slot()]
    sibling = (chip * 2 + 1 - core, dp)
    for t, ref in enumerate((xt_ref, dt_ref)):
        send(raw_slot[t], ref, raw.at[t, mine, :], sibling)

    for c in in_tab:
        c.wait()
    for r in range(1, EXP):
        theirs = pl.ds(pl.multiple_of((ex + EXP - r) % EXP * TOK, TOK), TOK)
        arrive(tab_slot[r][0], tab_r.at[:, theirs])
        arrive(tab_slot[r][1], tab_g.at[:, theirs])

    route, gate = tab_r[...].astype(F32), tab_g[...].astype(F32)
    ids = (lax.broadcasted_iota(jnp.int32, (CHIPS, LOCAL), 0) * 2 + core).astype(F32)
    hit = jnp.zeros((CHIPS, LOCAL), F32)
    weight = jnp.zeros((CHIPS, LOCAL), F32)
    for k in range(TOP):
        same = route[k : k + 1] == ids
        hit = hit + jnp.where(same, 1.0, 0.0)
        weight = weight + jnp.where(same, gate[k : k + 1], 0.0)
    coef[...] = weight
    stacked = jnp.concatenate([hit[:, b * TOK : (b + 1) * TOK] for b in range(EXP)], axis=0)
    tri = (
        lax.broadcasted_iota(jnp.int32, (TOK, TOK), 0) < lax.broadcasted_iota(jnp.int32, (TOK, TOK), 1)
    ).astype(F32).astype(BF)
    before = jnp.dot(stacked.astype(BF), tri, preferred_element_type=F32)
    for b in range(EXP):
        part = slice(b * CHIPS, (b + 1) * CHIPS)
        code[:, b * TOK : (b + 1) * TOK] = jnp.where(
            stacked[part] > 0.0, before[part] + float(CAP * (b % CHIPS)), -1.0
        )

    slot_row = lax.broadcasted_iota(jnp.int32, (PIECE, LOCAL // 2), 0).astype(F32)
    own_rows = [pl.ds(pl.multiple_of(dp * SHARD + h * PIECE, PIECE), PIECE) for h in range(2)]
    chip_cols = pl.ds(pl.multiple_of(chip * WIDE, WIDE), WIDE)
    a2a_slot = [[[slot() for _ in range(CHIPS)] for _ in range(2)] for _ in range(2)]
    a2a_self = [[None, None], [None, None]]

    def dispatch(t, h):
        half = slice(h * (LOCAL // 2), (h + 1) * (LOCAL // 2))
        for i in range(CHIPS):
            equal = code[i : i + 1, half] == slot_row
            value = 1.0 if t == 0 else coef[i : i + 1, half]
            onehot[i * PIECE : (i + 1) * PIECE] = jnp.where(equal, value, 0.0).astype(BF)
        for n in range(0, WIDE, 128):
            got = lax.dot_general(onehot[...], raw[t, n : n + 128, half], NT, preferred_element_type=F32)
            pay[t, h, :, :, n : n + 128] = got.astype(BF).reshape(CHIPS, PIECE, 128)
        where = bufs[t].at[own_rows[h], chip_cols]
        for r in range(1, CHIPS):
            to = (chip + r) % CHIPS
            send(a2a_slot[t][h][r], pay.at[t, h, to], where, (to * 2 + core, dp))
        a2a_self[t][h] = copy_in(pay.at[t, h, chip], where)

    def complete(t, h):
        a2a_self[t][h].wait()
        for r in range(1, CHIPS):
            src = (chip + CHIPS - r) % CHIPS
            arrive(a2a_slot[t][h][r], bufs[t].at[own_rows[h], pl.ds(pl.multiple_of(src * WIDE, WIDE), WIDE)])

    def rows_of(s):
        return pl.ds(pl.multiple_of(s * SHARD, SHARD), SHARD)

    def contract(s, with_x, with_d):
        rows = rows_of(s)
        if with_x:
            acc[0:2] = jnp.zeros((2, SHARD, HID), F32)
        if with_d:
            acc[2] = jnp.zeros((SHARD, HID), F32)

        def body(k, _):
            cols = pl.ds(pl.multiple_of(k * STEP, STEP), STEP)
            if with_x:
                xs = xall[rows, cols]
                acc[0] += jnp.dot(xs, wg[cols, :], preferred_element_type=F32)
                acc[1] += jnp.dot(xs, wu[cols, :], preferred_element_type=F32)
            if with_d:
                acc[2] += lax.dot_general(dall[rows, cols], wd[:, cols], NT, preferred_element_type=F32)
            return 0

        lax.fori_loop(0, D // STEP, body, 0)

    def activate(s):
        rows = rows_of(s)
        g, u, q = acc[0], acc[1], acc[2]
        sig = jax.nn.sigmoid(g)
        dg_ref[rows, :] = (q * u * sig * (1.0 + g * (1.0 - sig))).astype(BF)
        du_ref[rows, :] = (q * (g * sig)).astype(BF)

    def hidden(s):
        contract(s, True, True)
        activate(s)

    half = D // 2
    left, right, whole = slice(0, half), slice(half, D), slice(0, D)
    low, high = slice(0, half // 2), slice(half // 2, half)

    def piece(t, h, s, cols=whole):
        return bufs[t].at[pl.ds(pl.multiple_of(s * SHARD + h * PIECE, PIECE), PIECE), cols]

    def pass_on(k, to, t, h, s, cols=whole):
        send(k, piece(t, h, s, cols), piece(t, h, s, cols), (ex, to))

    def slots_for(*names):
        return {name: slot() for name in names}

    pieces = ((0, 0), (0, 1), (1, 0), (1, 1))
    to_up, to_down, to_side = slots_for(*pieces), slots_for(*pieces), slots_for(*pieces)

    def spread_z(t, h):
        pass_on(to_up[t, h], up, t, h, dp)
        pass_on(to_down[t, h], down, t, h, dp)

    first_up, first_down = [slot() for _ in range(CHIPS)], [slot() for _ in range(CHIPS)]
    order = (0, 2, 6, 1, 7, 3, 5, 4)

    def chunk(r, s):
        src = (chip + CHIPS - r) % CHIPS
        rows = pl.ds(pl.multiple_of(s * SHARD, SHARD), PIECE)
        return xall.at[rows, pl.ds(pl.multiple_of(src * WIDE, WIDE), WIDE)]

    def spread_first(some):
        for r in some:
            if r == 0:
                a2a_self[0][0].wait()
            else:
                arrive(a2a_slot[0][0][r], chunk(r, dp))
            send(first_up[r], chunk(r, dp), chunk(r, dp), (ex, up))
            send(first_down[r], chunk(r, dp), chunk(r, dp), (ex, down))

    def spread_y(t, h):
        pass_on(to_side[t, h], side, t, h, dp)

    in_raw[0].wait()
    arrive(raw_slot[0], raw.at[0, other, :])
    dispatch(0, 0)
    spread_first(order[:1])
    dispatch(0, 1)
    spread_first(order[1:])
    in_w = [copy_in(wg_ref, wg), copy_in(wu_ref, wu), copy_in(wd_ref, wd)]
    in_raw[1].wait()
    arrive(raw_slot[1], raw.at[1, other, :])
    dispatch(1, 0)
    complete(0, 1)
    spread_z(0, 1)
    dispatch(1, 1)
    spread_y(0, 0)
    spread_y(0, 1)
    complete(1, 0)
    spread_z(1, 0)
    spread_y(1, 0)
    complete(1, 1)
    spread_z(1, 1)
    spread_y(1, 1)
    for c in in_w:
        c.wait()

    far, pdown, pup, pfar = at(0, 2), at(1, NZ - 1), at(1, 1), at(1, 2)
    early = ((0, 0, whole), (0, 1, whole), (1, 0, left))
    via_up, via_down = slots_for(*pieces[:3]), slots_for(*pieces[:3])

    def relay_side(i):
        t, h, cols = early[i]
        arrive(to_side[t, h], piece(t, h, side))
        pass_on(via_up[t, h], up, t, h, side, cols)
        pass_on(via_down[t, h], down, t, h, side, cols)

    relay_side(0)
    hidden(dp)
    relay_side(1)
    for r in order:
        arrive(first_up[r], chunk(r, down))
        arrive(first_down[r], chunk(r, up))
    arrive(to_up[0, 1], piece(0, 1, down))
    arrive(to_down[0, 1], piece(0, 1, up))
    over = slots_for("d", "dr", "u", "ur", "fl", "fr", "f0")
    two = slots_for("d1l", "d1r", "d0l", "d0r", "x0", "x1", "px0", "px1", "pl", "ph")
    arrive(to_up[1, 0], piece(1, 0, down))
    pass_on(over["dr"], side, 1, 0, down, right)
    arrive(to_down[1, 0], piece(1, 0, up))
    pass_on(over["ur"], side, 1, 0, up, right)
    arrive(to_up[1, 1], piece(1, 1, down))
    pass_on(two["d1l"], up, 1, 1, down, left)
    pass_on(over["d"], side, 1, 1, down)
    arrive(to_down[1, 1], piece(1, 1, up))
    pass_on(two["d1r"], down, 1, 1, up, right)
    pass_on(over["u"], side, 1, 1, up)
    pass_on(two["d0l"], up, 1, 0, down, left)
    pass_on(two["d0r"], down, 1, 0, up, right)
    relay_side(2)
    pass_on(two["x0"], up, 0, 0, down)
    pass_on(two["x1"], down, 0, 1, up)
    hidden(down)
    arrive(to_side[1, 1], piece(1, 1, side))
    hidden(side)
    hidden(up)
    arrive(via_up[1, 0], piece(1, 0, pdown, left))
    pass_on(two["pl"], up, 1, 0, pdown, low)
    arrive(via_down[1, 0], piece(1, 0, pup, left))
    pass_on(two["ph"], down, 1, 0, pup, high)
    arrive(via_up[0, 0], piece(0, 0, pdown))
    pass_on(two["px0"], up, 0, 0, pdown)
    arrive(via_down[0, 1], piece(0, 1, pup))
    pass_on(two["px1"], down, 0, 1, pup)
    arrive(two["d0r"], piece(1, 0, far, right))
    pass_on(over["f0"], side, 1, 0, far, right)
    arrive(two["d1l"], piece(1, 1, far, left))
    pass_on(over["fl"], side, 1, 1, far, left)
    arrive(two["d1r"], piece(1, 1, far, right))
    pass_on(over["fr"], side, 1, 1, far, right)
    arrive(via_up[0, 1], piece(0, 1, pdown))
    arrive(over["dr"], piece(1, 0, pdown, right))
    arrive(over["d"], piece(1, 1, pdown))
    hidden(pdown)
    arrive(via_down[0, 0], piece(0, 0, pup))
    arrive(over["ur"], piece(1, 0, pup, right))
    arrive(over["u"], piece(1, 1, pup))
    hidden(pup)
    def part_of(s, h):
        return pl.ds(pl.multiple_of(s * SHARD + h * PIECE, PIECE), PIECE)

    def partial(dz):
        first, second = rows_of(at(0, dz)), rows_of(at(1, dz))
        g2 = jnp.concatenate([dg_ref[first, :], dg_ref[second, :]], axis=0)
        u2 = jnp.concatenate([du_ref[first, :], du_ref[second, :]], axis=0)

        def body(k, _):
            cols = pl.ds(pl.multiple_of(k * WIDE, WIDE), WIDE)
            v = lax.dot_general(g2, wg[cols, :], NT, preferred_element_type=F32)
            v = (v + lax.dot_general(u2, wu[cols, :], NT, preferred_element_type=F32)).astype(BF)
            dall[first, cols] = v[:SHARD]
            dall[second, cols] = v[SHARD:]
            return 0

        lax.fori_loop(0, D // WIDE, body, 0)

    def add(s, h, cols, *others):
        def body(i, _):
            here = pl.ds(pl.multiple_of(s * SHARD + h * PIECE + i * 16, 16), 16)
            total = dall[here, cols].astype(F32)
            for other in others:
                total = total + other(pl.ds(pl.multiple_of(h * PIECE + i * 16, 16), 16)).astype(F32)
            dall[here, cols] = total.astype(BF)
            return 0

        lax.fori_loop(0, PIECE // 16, body, 0)

    rows48 = [slice(h * PIECE, (h + 1) * PIECE) for h in range(2)]
    s_ya = {(h, dz): slot() for h in range(2) for dz in range(NZ)}
    s_relay_b = {(h, y, d): slot() for h in range(2) for y in range(2) for d in range(2)}
    s_fin_l = {(h, y, d): slot() for h in range(2) for y in range(2) for d in range(2)}
    s_fin_r = {(h, y, d): slot() for h in range(2) for y in range(2) for d in range(2)}
    s_relay_a = {(h, d): slot() for h in range(2) for d in range(2)}
    s_fin_a = {(h, d): slot() for h in range(2) for d in range(2)}
    s_yb = [slot(), slot()]
    s_back = [[slot() for _ in range(EXP)] for _ in range(2)]
    rel_l, rel_r = slice(0, CB // 2), slice(CB // 2, CB)

    def over_y(dz, h):
        send(s_ya[h, dz], dall.at[part_of(at(1, dz), h), ALL_A], got_a.at[dz, rows48[h], :], (ex, side))

    def line(j, dz):
        return at(1 - j, dz)

    def far_b(h, y):
        src = part_of(line(y, 2), h)
        send(s_relay_b[h, y, 0], dall.at[src, LB], relay_b.at[0, y, rows48[h], :], (ex, up))
        send(s_relay_b[h, y, 1], dall.at[src, RB], relay_b.at[1, y, rows48[h], :], (ex, down))

    def direct_up(h, y):
        send(s_fin_r[h, y, 0], dall.at[part_of(line(y, 1), h), RB], fin_b.at[0, y, rows48[h], rel_r], (ex, up))

    def direct_down(h, y):
        send(s_fin_l[h, y, 1], dall.at[part_of(line(y, NZ - 1), h), LB], fin_b.at[1, y, rows48[h], rel_l], (ex, down))

    def combined_b(h, y):
        arrive(s_relay_b[h, y, 0], relay_b.at[0, y, rows48[h], :])
        add(line(y, 1), h, LB, lambda r, y=y: relay_b[0, y, r, :])
        send(s_fin_l[h, y, 0], dall.at[part_of(line(y, 1), h), LB], fin_b.at[0, y, rows48[h], rel_l], (ex, up))
        arrive(s_relay_b[h, y, 1], relay_b.at[1, y, rows48[h], :])
        add(line(y, NZ - 1), h, RB, lambda r, y=y: relay_b[1, y, r, :])
        send(s_fin_r[h, y, 1], dall.at[part_of(line(y, NZ - 1), h), RB], fin_b.at[1, y, rows48[h], rel_r], (ex, down))

    def far_a(h):
        arrive(s_ya[h, 2], got_a.at[2, rows48[h], :])
        add(at(0, 2), h, ALL_A, lambda r: got_a[2, r, :])
        src = part_of(at(0, 2), h)
        send(s_relay_a[h, 0], dall.at[src, LA], relay_a.at[0, rows48[h], :], (ex, up))
        send(s_relay_a[h, 1], dall.at[src, RA], relay_a.at[1, rows48[h], :], (ex, down))

    def near_a(h):
        for d, dz, peer, mixed in ((0, 1, up, LA), (1, NZ - 1, down, RA)):
            plain = RA if d == 0 else LA
            arrive(s_ya[h, dz], got_a.at[dz, rows48[h], :])
            add(at(0, dz), h, plain, lambda r, dz=dz: got_a[dz, r, plain])
            arrive(s_relay_a[h, d], relay_a.at[d, rows48[h], :])
            add(at(0, dz), h, mixed, lambda r, dz=dz: got_a[dz, r, mixed], lambda r, d=d: relay_a[d, r, :])
            send(s_fin_a[h, d], dall.at[part_of(at(0, dz), h), ALL_A], fin_a.at[d, rows48[h], :], (ex, peer))

    def wait_b(h, j):
        for d in range(2):
            arrive(s_fin_l[h, j, d], fin_b.at[d, j, rows48[h], rel_l])
            arrive(s_fin_r[h, j, d], fin_b.at[d, j, rows48[h], rel_r])

    def fold_b(h):
        wait_b(h, 0)
        add(side, h, ALL_B, lambda r: fin_b[0, 0, r, :], lambda r: fin_b[1, 0, r, :])
        send(s_yb[h], dall.at[part_of(side, h), ALL_B], got_b.at[rows48[h], :], (ex, side))

    backs = (back, back_out)

    def finish(h):
        arrive(s_ya[h, 0], got_a.at[0, rows48[h], :])
        for d in range(2):
            arrive(s_fin_a[h, d], fin_a.at[d, rows48[h], :])
        add(dp, h, ALL_A, lambda r: got_a[0, r, :], lambda r: fin_a[0, r, :], lambda r: fin_a[1, r, :])
        wait_b(h, 1)
        arrive(s_yb[h], got_b.at[rows48[h], :])
        add(
            dp, h, ALL_B,
            lambda r: fin_b[0, 1, r, :], lambda r: fin_b[1, 1, r, :], lambda r: got_b[r, :],
        )
        where = pl.ds(pl.multiple_of(ex * PIECE, PIECE), PIECE)

        def cols(e):
            return pl.ds(pl.multiple_of(e // 2 * WIDE + e % 2 * 384, 128), PART)

        for r in range(1, EXP):
            to = (ex + r) % EXP
            send(s_back[h][r], dall.at[part_of(dp, h), cols(to)], backs[h].at[where, :], (to, dp))
        return copy_in(dall.at[part_of(dp, h), cols(ex)], backs[h].at[where, :])

    def returned(h, own):
        own.wait()
        for r in range(1, EXP):
            src = (ex + EXP - r) % EXP
            arrive(s_back[h][r], backs[h].at[pl.ds(pl.multiple_of(src * PIECE, PIECE), PIECE), :])

    def place_tables():
        table = tab_r[...].astype(F32)
        ids = lax.broadcasted_iota(jnp.int32, (EXP, LOCAL), 0).astype(F32)
        hit = jnp.zeros((EXP, LOCAL), F32)
        for k in range(TOP):
            hit = hit + jnp.where(table[k : k + 1] == ids, 1.0, 0.0)
        stacked = jnp.concatenate([hit[:, b * TOK : (b + 1) * TOK] for b in range(EXP)], axis=0)
        tri = (
            lax.broadcasted_iota(jnp.int32, (TOK, TOK), 0) < lax.broadcasted_iota(jnp.int32, (TOK, TOK), 1)
        ).astype(F32).astype(BF)
        before = jnp.dot(stacked.astype(BF), tri, preferred_element_type=F32)
        for b in range(EXP):
            part = slice(b * EXP, (b + 1) * EXP)
            spots[:, b * TOK : (b + 1) * TOK] = jnp.where(
                stacked[part] > 0.0, before[part] + float(CAP * (b % CHIPS)), -1.0
            )
        slot_row = lax.broadcasted_iota(jnp.int32, (PIECE, LOCAL // 2), 0).astype(F32)
        for h in range(2):
            for e in range(EXP):
                equal = spots[e : e + 1, h * (LOCAL // 2) : (h + 1) * (LOCAL // 2)] == slot_row
                places[h, e * PIECE : (e + 1) * PIECE] = jnp.where(equal, 1.0, 0.0).astype(BF)

    def grad_copy(j, i):
        cols = pl.ds(pl.multiple_of(i * TILE, TILE), TILE)
        out = gg_out if j == 0 else gu_out
        return pltpu.make_async_copy(gbuf.at[j, i % 2], out.at[cols, :], gsem.at[j, i % 2])

    def weight_grads(start, stop):
        def body(i, _):
            cols = pl.ds(pl.multiple_of(i * TILE, TILE), TILE)
            block = xall[:, cols]
            dims = (((0,), (0,)), ((), ()))
            for j, grad in enumerate((dg_ref, du_ref)):
                @pl.when(i >= 2)
                def _():
                    grad_copy(j, i - 2).wait()

                gbuf[j, i % 2] = lax.dot_general(
                    block, grad[...], dims, preferred_element_type=F32
                ).astype(BF)
                grad_copy(j, i).start()
            return 0

        lax.fori_loop(start, stop, body, 0)

    place_tables()
    place_copy = copy_in(places.at[1], place_out)
    flush(*(k[q] for k in (to_up, to_down, to_side) for q in pieces[2:]))
    flush(via_up[1, 0], via_down[1, 0])
    partial(0)
    flush(two["d1r"], two["d0r"], over["u"], over["ur"], two["ph"])
    partial(1)
    for h in range(2):
        direct_up(h, 0)
    flush(two["d1l"], two["d0l"], over["d"], over["dr"], two["pl"])
    partial(NZ - 1)
    for h in range(2):
        direct_down(h, 0)
    for h in range(2):
        direct_up(h, 1)
        direct_down(h, 1)
    for dz in (0, 1, NZ - 1):
        for h in range(2):
            over_y(dz, h)
    arrive(two["d0l"], piece(1, 0, far, left))
    arrive(two["x0"], piece(0, 0, far))
    arrive(two["x1"], piece(0, 1, far))
    hidden(far)
    arrive(two["px0"], piece(0, 0, pfar))
    arrive(two["px1"], piece(0, 1, pfar))
    contract(pfar, True, False)
    arrive(two["pl"], piece(1, 0, pfar, low))
    arrive(two["ph"], piece(1, 0, pfar, high))
    arrive(over["f0"], piece(1, 0, pfar, right))
    arrive(over["fl"], piece(1, 1, pfar, left))
    arrive(over["fr"], piece(1, 1, pfar, right))
    contract(pfar, False, True)
    activate(pfar)
    flush(over["f0"], over["fl"], over["fr"])
    partial(2)
    for y in range(2):
        for h in range(2):
            far_b(h, y)
    for h in range(2):
        over_y(2, h)
    weight_grads(0, 6)
    combined_b(0, 0)
    far_a(0)
    far_a(1)
    combined_b(1, 0)
    fold_b(0)
    near_a(0)
    near_a(1)
    combined_b(0, 1)
    combined_b(1, 1)
    fold_b(1)
    weight_grads(6, D // TILE)
    own0 = finish(0)
    own1 = finish(1)
    returned(0, own0)
    combine(back, places.at[0], outbuf)
    keep = pl.ds(pl.multiple_of(core * 64, 64), WIDE // 2)
    out0 = copy_in(outbuf.at[keep, :], first_out)
    returned(1, own1)
    flush(*list(sent))
    out0.wait()
    place_copy.wait()
    for j in range(2):
        for i in (D // TILE - 2, D // TILE - 1):
            grad_copy(j, i).wait()


def layer(xt, dt, rt, gt, wg, wu, wd):
    hbm = pl.BlockSpec(memory_space=pl.ANY)
    rows = DP * SHARD
    return pl.pallas_call(
        layer_kernel,
        out_shape=(
            jax.ShapeDtypeStruct((WIDE // 2, LOCAL // 2), BF),
            jax.ShapeDtypeStruct((EXP * PIECE, PART), BF),
            jax.ShapeDtypeStruct((EXP * PIECE, LOCAL // 2), BF),
            jax.ShapeDtypeStruct((D, HID), BF),
            jax.ShapeDtypeStruct((D, HID), BF),
        ),
        in_specs=[hbm] * 7,
        out_specs=(hbm,) * 5,
        scratch_shapes=[
            pltpu.VMEM((2, WIDE, LOCAL), BF),
            pltpu.VMEM((TOP, LOCAL), jnp.int32),
            pltpu.VMEM((TOP, LOCAL), BF),
            pltpu.VMEM((CHIPS, LOCAL), F32),
            pltpu.VMEM((CHIPS, LOCAL), F32),
            pltpu.VMEM((CHIPS * PIECE, LOCAL // 2), BF),
            pltpu.VMEM((2, 2, CHIPS, PIECE, WIDE), BF),
            pltpu.VMEM((rows, D), BF),
            pltpu.VMEM((rows, D), BF),
            pltpu.VMEM((D, HID), BF),
            pltpu.VMEM((D, HID), BF),
            pltpu.VMEM((HID, D), BF),
            pltpu.VMEM((3, SHARD, HID), F32),
            pltpu.VMEM((rows, HID), BF),
            pltpu.VMEM((rows, HID), BF),
            pltpu.VMEM((EXP, LOCAL), F32),
            pltpu.VMEM((2, EXP * PIECE, LOCAL // 2), BF),
            pltpu.VMEM((NZ, SHARD, CA), BF),
            pltpu.VMEM((2, SHARD, CA // 2), BF),
            pltpu.VMEM((2, SHARD, CA), BF),
            pltpu.VMEM((2, 2, SHARD, CB // 2), BF),
            pltpu.VMEM((2, 2, SHARD, CB), BF),
            pltpu.VMEM((SHARD, CB), BF),
            pltpu.VMEM((EXP * PIECE, PART), BF),
            pltpu.VMEM((PART, LOCAL // 2), BF),
            pltpu.VMEM((2, 2, TILE, HID), BF),
            pltpu.SemaphoreType.DMA((208,)),
            pltpu.SemaphoreType.DMA((208,)),
            pltpu.SemaphoreType.DMA((24,)),
            pltpu.SemaphoreType.DMA((2, 2)),
        ],
        compiler_params=pltpu.CompilerParams(
            collective_id=0, has_side_effects=True, vmem_limit_bytes=67_000_000
        ),
        name="layer",
    )(xt, dt, rt, gt, wg, wu, wd)


PARTS = 4


def last_kernel(
    first_ref, back_ref, place_ref, gg_ref, gu_ref,
    out_t, gg_out, gu_out,
    first, back, places, out, grads, lsem, gsem, osem,
):
    core = lax.axis_index("expert") % 2
    span = D // PARTS
    loads = [
        pltpu.make_async_copy(src, dst, lsem.at[i])
        for i, (src, dst) in enumerate(((back_ref, back), (place_ref, places), (first_ref, first)))
    ]
    pairs = ((gg_ref, gg_out), (gu_ref, gu_out))
    rows = [slice(n * span, (n + 1) * span) for n in range(PARTS)]
    takes = [[pltpu.make_async_copy(src.at[r, :], grads.at[j, r, :], gsem.at[0, j, n]) for n, r in enumerate(rows)]
             for j, (src, _) in enumerate(pairs)]
    gives = [[pltpu.make_async_copy(grads.at[j, r, :], dst.at[r, :], gsem.at[1, j, n]) for n, r in enumerate(rows)]
             for j, (_, dst) in enumerate(pairs)]
    for c in loads[:2]:
        c.start()
    for n in range(PARTS):
        for j in range(2):
            takes[j][n].start()
    loads[2].start()
    half = LOCAL // 2
    keep = pl.ds(pl.multiple_of(core * 64, 64), WIDE // 2)
    for c in loads[:2]:
        c.wait()
    early = pltpu.make_async_copy(first, out_t.at[:, :half], osem.at[0])
    late = pltpu.make_async_copy(out.at[keep, :], out_t.at[:, half:], osem.at[1])
    width = half // PARTS
    for n in range(PARTS):
        cols = slice(n * width, (n + 1) * width)
        got = lax.dot_general(
            back[...], places[:, cols], (((0,), (0,)), ((), ())), preferred_element_type=F32
        )
        out[:, cols] = got.astype(BF)
        for j in range(2):
            takes[j][n].wait()
            gives[j][n].start()
    late.start()
    loads[2].wait()
    early.start()
    for n in range(PARTS):
        for j in range(2):
            gives[j][n].wait()
    early.wait()
    late.wait()


def last(first, back, places, gg, gu):
    hbm = pl.BlockSpec(memory_space=pl.ANY)
    return pl.pallas_call(
        last_kernel,
        out_shape=(
            jax.ShapeDtypeStruct((WIDE // 2, LOCAL), BF),
            jax.ShapeDtypeStruct((D, HID), BF),
            jax.ShapeDtypeStruct((D, HID), BF),
        ),
        in_specs=[hbm] * 5,
        out_specs=(hbm,) * 3,
        scratch_shapes=[
            pltpu.VMEM((WIDE // 2, LOCAL // 2), BF),
            pltpu.VMEM((EXP * PIECE, PART), BF),
            pltpu.VMEM((EXP * PIECE, LOCAL // 2), BF),
            pltpu.VMEM((PART, LOCAL // 2), BF),
            pltpu.VMEM((2, D, HID), BF),
            pltpu.SemaphoreType.DMA((3,)),
            pltpu.SemaphoreType.DMA((2, 2, PARTS)),
            pltpu.SemaphoreType.DMA((2,)),
        ],
        compiler_params=pltpu.CompilerParams(vmem_limit_bytes=60 * 1024 * 1024),
        name="last",
    )(first, back, places, gg, gu)


def per_device(attn_rows, out_grad, routes, gates, w_gate, w_up, w_down):
    results = layer(attn_rows.T, out_grad.T, routes.T, gates.T, w_gate[0], w_up[0], w_down[0])
    grad_t, g_gate, g_up = last(*results)
    return grad_t.T, g_gate[None], g_up[None]


def solution(mesh):
    return jax.shard_map(
        per_device,
        mesh=mesh,
        in_specs=(
            P("dp", "expert"),
            P("dp", "expert"),
            P(("dp", "expert"), None),
            P(("dp", "expert"), None),
            P("expert", None, "dp"),
            P("expert", None, "dp"),
            P("expert", "dp", None),
        ),
        out_specs=(P("dp", "expert"), P("expert", None, "dp"), P("expert", None, "dp")),
        check_vma=False,
    )
```
